32 devices in a mesh: dp: 8 (over y, x, core), seq: 4 (over z).
Axes of the slice: x: 2, y: 2, z: 4, core: 2. Of those that a mesh axis runs over, the one named last changes fastest.
Arguments:
- encoder_input: bfloat16 [8, 1024, 512], P('dp', 'seq'), may hold values from -75 to 75, as said below
- decoder_input: bfloat16 [8, 1024, 512], P('dp', 'seq'), may hold values from -75 to 75, as said below
- output_grad: bfloat16 [8, 1024, 512], P('dp', 'seq'), may hold values from -6 to 6
- segment_lengths: int32 [8, 4], P('dp'), may hold values from 1 to 772, as said below
- bucket_table: int32 [2047], replicated, may hold values from 0 to 31, as said below
- enc_gain1: float32 [512], replicated, may hold values from 0.25 to 1.75
- enc_qkv: bfloat16 [512, 1536], replicated, may hold values from -0.125 to 0.125
- enc_proj: bfloat16 [512, 512], replicated, may hold values from -1.5 to 1.5
- enc_rel: float32 [32, 8], replicated, may hold values from -4 to 4
- enc_gain2: float32 [512], replicated, may hold values from 0.25 to 1.75
- enc_wi: bfloat16 [512, 2048], replicated, may hold values from -0.25 to 0.25
- enc_wo: bfloat16 [2048, 512], replicated, may hold values from -0.1875 to 0.1875
- enc_gainf: float32 [512], replicated, may hold values from 0.25 to 1.75
- dec_gain1: float32 [512], replicated, may hold values from 0.25 to 1.75
- dec_qkv: bfloat16 [512, 1536], replicated, may hold values from -0.125 to 0.125
- dec_proj: bfloat16 [512, 512], replicated, may hold values from -1.5 to 1.5
- dec_rel: float32 [32, 8], replicated, may hold values from -4 to 4
- dec_gain2: float32 [512], replicated, may hold values from 0.25 to 1.75
- cross_q: bfloat16 [512, 512], replicated, may hold values from -0.125 to 0.125
- cross_kv: bfloat16 [512, 1024], replicated, may hold values from -0.125 to 0.125
- cross_proj: bfloat16 [512, 512], replicated, may hold values from -1.5 to 1.5
- dec_gain3: float32 [512], replicated, may hold values from 0.25 to 1.75
- dec_wi: bfloat16 [512, 2048], replicated, may hold values from -0.25 to 0.25
- dec_wo: bfloat16 [2048, 512], replicated, may hold values from -0.1875 to 0.1875
Outputs:
- dec_output: bfloat16 [8, 1024, 512], P('dp', 'seq')
- encoder_grad: bfloat16 [8, 1024, 512], P('dp', 'seq')
- decoder_grad: bfloat16 [8, 1024, 512], P('dp', 'seq')
- sublayer_rms: float32 [8], replicated
- enc_gain1_grad: float32 [512], replicated
- enc_qkv_grad: float32 [512, 1536], P('dp', 'seq')
- enc_proj_grad: float32 [512, 512], P('dp', 'seq')
- enc_rel_grad: float32 [32, 8], replicated
- enc_gain2_grad: float32 [512], replicated
- enc_wi_grad: float32 [512, 2048], P('dp', 'seq')
- enc_wo_grad: float32 [2048, 512], P('dp', 'seq')
- enc_gainf_grad: float32 [512], replicated
- dec_gain1_grad: float32 [512], replicated
- dec_qkv_grad: float32 [512, 1536], P('dp', 'seq')
- dec_proj_grad: float32 [512, 512], P('dp', 'seq')
- dec_rel_grad: float32 [32, 8], replicated
- dec_gain2_grad: float32 [512], replicated
- cross_q_grad: float32 [512, 512], P('dp', 'seq')
- cross_kv_grad: float32 [512, 1024], P('dp', 'seq')
- cross_proj_grad: float32 [512, 512], P('dp', 'seq')
- dec_gain3_grad: float32 [512], replicated
- dec_wi_grad: float32 [512, 2048], P('dp', 'seq')
- dec_wo_grad: float32 [2048, 512], P('dp', 'seq')
The draws below stay inside these ranges and needn't reach their ends.
Inputs may be any that keep to these rules, and one draw needn't show every extreme that they name: `segment_lengths`: each row's 4 lengths add up to 1024; one of them, at a place drawn for the row, is the largest; the others are 1 or more, and in every row one of them is 1. `bucket_table`: offset 0 is bucket 0; negative offsets use the first 16 buckets and positive ones the rest; within each direction the bucket never falls as the distance grows. `encoder_input`: Real-valued activations. `decoder_input`: Real-valued activations.
All inputs are finite; a program needn't handle non-finite values.
Results may differ from the reference program's by a relative error of at most 0.025.
Values may be sent and summed in bfloat16 or wider, within the bound.
No kernel may reach another device: no remote copies, remote signals or barrier semaphores. Data moves between devices by JAX's collectives and lax.ppermute only.
A program may use at most 192 MiB of HBM per device.

```python
import math
from functools import partial
import jax
import jax.numpy as jnp
from jax import lax

D = 512
HEADS = 8
HEAD_DIM = 64
FF = 2048
BUCKETS = 32
LEN = 1024
SEGS = 4
STATS = 8
INNER = 512
ROWS = 8
TABLE = 2047
SHORT_MAX = 84


def scaled_rows(key):
    key_noise, key_cols = jax.random.split(key, 2)
    array_shape = (ROWS, LEN, D)
    steps_up = jnp.arange(ROWS, dtype=jnp.float32) / max(ROWS - 1, 1)
    samples = jnp.clip(jax.random.normal(key_noise, array_shape, jnp.float32), -6.0, 6.0)
    growth = 3.0 ** steps_up
    columns = jnp.exp(jax.random.uniform(key_cols, (D,), jnp.float32, math.log(0.3), math.log(3.0)))
    return (samples * growth[:, None, None] * columns[None, None, :]).astype(jnp.bfloat16)


def draw_encoder_input(key, part):
    return scaled_rows(jax.random.fold_in(key, 11))


def draw_decoder_input(key, part):
    return scaled_rows(jax.random.fold_in(key, 23))


def draw_segment_lengths(key, part):
    key_cuts, key_place = jax.random.split(jax.random.fold_in(key, 37))
    short_total = (SEGS - 1) * SHORT_MAX
    row_keys = jax.random.split(key_cuts, ROWS)
    shuffled = jax.vmap(lambda row_key: jax.random.permutation(row_key, short_total - 2))(row_keys) + 2
    drawn_cuts = shuffled[:, :SEGS - 3].astype(jnp.int32)
    cut_points = jnp.sort(jnp.concatenate([jnp.ones((ROWS, 1), jnp.int32), drawn_cuts], axis=1), axis=1)
    bounds = jnp.concatenate([jnp.zeros((ROWS, 1), jnp.int32), cut_points, jnp.full((ROWS, 1), short_total, jnp.int32)], axis=1)
    shorts = bounds[:, 1:] - bounds[:, :-1]
    padded_shorts = jnp.concatenate([shorts, jnp.zeros((ROWS, 1), jnp.int32)], axis=1)
    shifted = jnp.concatenate([jnp.zeros((ROWS, 1), jnp.int32), shorts], axis=1)
    long_slot = jax.random.randint(key_place, (ROWS, 1), 0, SEGS)
    slot_ids = jnp.arange(SEGS, dtype=jnp.int32)[None, :]
    long_len = LEN - short_total
    lengths_all = jnp.where(slot_ids < long_slot, padded_shorts, jnp.where(slot_ids == long_slot, long_len, shifted))
    return lengths_all.astype(jnp.int32)


def draw_bucket_table(key, part):
    half_count = BUCKETS // 2
    exact_count = half_count // 2
    cut_count = half_count - exact_count - 1
    shuffled = jax.random.permutation(jax.random.fold_in(key, 53), LEN - exact_count - 1)
    cut_points = (shuffled[:cut_count] + exact_count + 1).astype(jnp.int32)
    offsets = jnp.arange(TABLE, dtype=jnp.int32) - (LEN - 1)
    distance = jnp.abs(offsets)
    passed = jnp.sum((distance[:, None] >= cut_points[None, :]).astype(jnp.int32), axis=1)
    buckets = jnp.where(distance < exact_count, distance, exact_count + passed)
    return (buckets + jnp.where(offsets > 0, half_count, 0)).astype(jnp.int32)


def shard_levels(own_key, extent, pieces, low, high):
    def one(dim, parts):
        steps = jax.random.uniform(jax.random.fold_in(jax.random.fold_in(own_key, 6), dim), (parts,), jnp.float32, low / len(pieces), high / len(pieces))
        return jnp.repeat(jnp.exp(steps), extent[dim] // parts).reshape((-1,) + (1,) * (len(extent) - dim - 1))

    level = one(*pieces[0])
    for cut in pieces[1:]:
        level = level * one(*cut)
    return level


def gaussian(stream_key, extent, width, reach, shards=(), held_as=jnp.bfloat16):
    level = shard_levels(stream_key, extent, shards, -0.22, 0.18) if shards else 1.0
    result = jax.random.normal(stream_key, extent, jnp.float32) * width * level
    return jnp.minimum(jnp.maximum(result, -reach), reach).astype(held_as)


def setup_inputs(seed: int = 0) -> dict:
    seeds = jax.random.split(jax.random.key(seed), 25)
    encoder_input = draw_encoder_input(jax.random.fold_in(seeds[24], 71), 0)
    decoder_input = draw_decoder_input(jax.random.fold_in(seeds[24], 71), 0)
    output_grad = gaussian(seeds[2], (ROWS, LEN, D), 1.0, 6.0, ((0, 8), (1, 4)))
    segment_lengths = draw_segment_lengths(jax.random.fold_in(seeds[24], 71), 0)
    bucket_table = draw_bucket_table(jax.random.fold_in(seeds[24], 71), 0)
    enc_gain1 = jnp.clip(1.0 + 0.15 * jax.random.normal(seeds[5], (D,), jnp.float32), 0.25, 1.75)
    enc_qkv = gaussian(seeds[6], (D, 3 * INNER), (4 * D) ** -0.5, 0.125)
    enc_proj = gaussian(seeds[7], (INNER, D), (INNER // 32) ** -0.5, 1.5)
    enc_rel = gaussian(seeds[8], (BUCKETS, HEADS), 0.7, 4.0, (), jnp.float32)
    enc_gain2 = jnp.clip(1.0 + 0.15 * jax.random.normal(seeds[9], (D,), jnp.float32), 0.25, 1.75)
    enc_wi = gaussian(seeds[10], (D, FF), D ** -0.5, 0.25)
    enc_wo = gaussian(seeds[11], (FF, D), (FF // 2) ** -0.5, 0.1875)
    enc_gainf = jnp.clip(1.0 + 0.15 * jax.random.normal(seeds[12], (D,), jnp.float32), 0.25, 1.75)
    dec_gain1 = jnp.clip(1.0 + 0.15 * jax.random.normal(seeds[13], (D,), jnp.float32), 0.25, 1.75)
    dec_qkv = gaussian(seeds[14], (D, 3 * INNER), (4 * D) ** -0.5, 0.125)
    dec_proj = gaussian(seeds[15], (INNER, D), (INNER // 32) ** -0.5, 1.5)
    dec_rel = gaussian(seeds[16], (BUCKETS, HEADS), 0.7, 4.0, (), jnp.float32)
    dec_gain2 = jnp.clip(1.0 + 0.15 * jax.random.normal(seeds[17], (D,), jnp.float32), 0.25, 1.75)
    cross_q = gaussian(seeds[18], (D, INNER), (4 * D) ** -0.5, 0.125)
    cross_kv = gaussian(seeds[19], (D, 2 * INNER), (4 * D) ** -0.5, 0.125)
    cross_proj = gaussian(seeds[20], (INNER, D), (INNER // 32) ** -0.5, 1.5)
    dec_gain3 = jnp.clip(1.0 + 0.15 * jax.random.normal(seeds[21], (D,), jnp.float32), 0.25, 1.75)
    dec_wi = gaussian(seeds[22], (D, FF), D ** -0.5, 0.25)
    dec_wo = gaussian(seeds[23], (FF, D), (FF // 2) ** -0.5, 0.1875)
    return {"encoder_input": encoder_input, "decoder_input": decoder_input, "output_grad": output_grad, "segment_lengths": segment_lengths, "bucket_table": bucket_table, "enc_gain1": enc_gain1, "enc_qkv": enc_qkv, "enc_proj": enc_proj, "enc_rel": enc_rel, "enc_gain2": enc_gain2, "enc_wi": enc_wi, "enc_wo": enc_wo, "enc_gainf": enc_gainf, "dec_gain1": dec_gain1, "dec_qkv": dec_qkv, "dec_proj": dec_proj, "dec_rel": dec_rel, "dec_gain2": dec_gain2, "cross_q": cross_q, "cross_kv": cross_kv, "cross_proj": cross_proj, "dec_gain3": dec_gain3, "dec_wi": dec_wi, "dec_wo": dec_wo}


eps_norm = 1e-06
negative = -1000000000.0

@jax.custom_vjp
def low(v):
    return lax.optimization_barrier(v.astype(jnp.bfloat16)).astype(jnp.float32)

@jax.custom_vjp
def low_back(v):
    return v

def low_keep(v):
    return (low(v), None)

def low_pass(kept, grad):
    return (grad,)

def back_keep(v):
    return (v, None)

def back_low(kept, grad):
    return (low(grad),)
low.defvjp(low_keep, low_pass)
low_back.defvjp(back_keep, back_low)

def product(left, right):
    return jnp.dot(left, right, precision=lax.Precision.HIGHEST, preferred_element_type=jnp.float32)

def rms_norm(values, gain_vec):
    return values * lax.rsqrt(lax.optimization_barrier(jnp.mean(values * values, axis=-1, keepdims=True)) + eps_norm) * gain_vec

def attend(queries, key_rows, values, pos_bias, allowed):
    length = queries.shape[0]
    scores = jnp.einsum('qhd,khd->hqk', queries.reshape(length, HEADS, HEAD_DIM), key_rows.reshape(length, HEADS, HEAD_DIM), precision=lax.Precision.HIGHEST)
    if pos_bias is not None:
        scores = scores + pos_bias
    scores = low_back(scores)
    scores = jnp.where(allowed[None], scores, negative)
    probs_low = low(jax.nn.softmax(scores, axis=-1))
    mixed = jnp.einsum('hqk,khd->qhd', probs_low, values.reshape(length, HEADS, HEAD_DIM), precision=lax.Precision.HIGHEST)
    return mixed.reshape(length, HEADS * HEAD_DIM)

def feed(values, gain_vec, w_in, w_out):
    normed = low(rms_norm(values, gain_vec))
    hidden = low_back(product(normed, w_in))
    active = low(jax.nn.gelu(hidden, approximate=True))
    return low_back(product(active, w_out))

def self_block(values, gain_vec, w_qkv, w_proj, pos_bias, allowed):
    normed = low(rms_norm(values, gain_vec))
    triple = low_back(low(product(normed, w_qkv)))
    inner_w = w_proj.shape[0]
    mixed = low_back(low(attend(triple[:, :inner_w], triple[:, inner_w:2 * inner_w], triple[:, 2 * inner_w:], pos_bias, allowed)))
    return low_back(product(mixed, w_proj))

def row_pass(weights, enc_bias, dec_bias, enc_row, dec_row, lengths_row):
    enc_gain1, enc_qkv, enc_proj, enc_gain2, enc_wi, enc_wo, enc_gainf, dec_gain1, dec_qkv, dec_proj, dec_gain2, cross_q, cross_kv, cross_proj, dec_gain3, dec_wi, dec_wo = weights
    length = enc_row.shape[0]
    places = jnp.arange(length, dtype=jnp.int32)
    seg_ends = jnp.cumsum(lengths_row).astype(jnp.int32)
    seg_ids = lax.optimization_barrier(jnp.sum((places[:, None] >= seg_ends[None, :]).astype(jnp.int32), axis=1))
    same_seg = seg_ids[:, None] == seg_ids[None, :]
    causal = same_seg & (places[None, :] <= places[:, None])
    enc_att = self_block(enc_row, enc_gain1, enc_qkv, enc_proj, enc_bias, same_seg)
    enc_h1 = enc_row + enc_att
    enc_ffn = feed(enc_h1, enc_gain2, enc_wi, enc_wo)
    enc_h2 = enc_h1 + enc_ffn
    encoded = low(rms_norm(enc_h2, enc_gainf))
    dec_att = self_block(dec_row, dec_gain1, dec_qkv, dec_proj, dec_bias, causal)
    dec_h1 = dec_row + dec_att
    cross_in = low(rms_norm(dec_h1, dec_gain2))
    cross_query = low_back(low(product(cross_in, cross_q)))
    cross_pair = low_back(low(product(encoded, cross_kv)))
    inner_w = cross_q.shape[1]
    cross_mix = low_back(low(attend(cross_query, cross_pair[:, :inner_w], cross_pair[:, inner_w:], None, same_seg)))
    cross_att = low_back(product(cross_mix, cross_proj))
    dec_h2 = dec_h1 + cross_att
    dec_ffn = feed(dec_h2, dec_gain3, dec_wi, dec_wo)
    dec_h3 = dec_h2 + dec_ffn
    members = (enc_att, enc_h1, enc_ffn, enc_h2, dec_att, cross_att, dec_ffn, dec_h3)
    sums = jnp.stack([jnp.sum(member * member) for member in members])
    return (dec_h3, sums)

def forward(params, enc_in, dec_in, segment_lengths, bucket_table):
    length = enc_in.shape[1]
    places = jnp.arange(length, dtype=jnp.int32)
    offsets = (places[None, :] - places[:, None] + (length - 1)).astype(jnp.int32)
    buckets = bucket_table[offsets]
    enc_bias = jnp.transpose(params[3][buckets], (2, 0, 1))
    dec_bias = jnp.transpose(params[11][buckets], (2, 0, 1))
    weights = params[:3] + params[4:11] + params[12:]
    row_fn = jax.checkpoint(row_pass)

    def step(totals, row_data):
        out_row, sums = row_fn(weights, enc_bias, dec_bias, row_data[0], row_data[1], row_data[2])
        return (totals + sums, out_row)
    totals, outputs = lax.scan(step, jnp.zeros((STATS,), jnp.float32), (enc_in, dec_in, segment_lengths))
    return (outputs, totals)

def reference(encoder_input, decoder_input, output_grad, segment_lengths, bucket_table, enc_gain1, enc_qkv, enc_proj, enc_rel, enc_gain2, enc_wi, enc_wo, enc_gainf, dec_gain1, dec_qkv, dec_proj, dec_rel, dec_gain2, cross_q, cross_kv, cross_proj, dec_gain3, dec_wi, dec_wo):
    params = tuple((member.astype(jnp.float32) for member in (enc_gain1, enc_qkv, enc_proj, enc_rel, enc_gain2, enc_wi, enc_wo, enc_gainf, dec_gain1, dec_qkv, dec_proj, dec_rel, dec_gain2, cross_q, cross_kv, cross_proj, dec_gain3, dec_wi, dec_wo)))
    outputs, pull, totals = jax.vjp(partial(forward, segment_lengths=segment_lengths, bucket_table=bucket_table), params, encoder_input.astype(jnp.float32), decoder_input.astype(jnp.float32), has_aux=True)
    grads, enc_grad, dec_grad = pull(output_grad.astype(jnp.float32))
    rms_values = jnp.sqrt(totals / float(outputs.size))
    return (outputs.astype(jnp.bfloat16), enc_grad.astype(jnp.bfloat16), dec_grad.astype(jnp.bfloat16), rms_values, grads[0], grads[1], grads[2], grads[3], grads[4], grads[5], grads[6], grads[7], grads[8], grads[9], grads[10], grads[11], grads[12], grads[13], grads[14], grads[15], grads[16], grads[17], grads[18])
```

```python
from functools import partial

import jax
import jax.numpy as jnp
from jax import lax
from jax.sharding import PartitionSpec as P

HEAD_DIM = 64
BF = jnp.bfloat16
F32 = jnp.float32

eps_norm = 1e-06
negative = -1000000000.0


def rms_norm(values, gain_vec):
    return (
        values * lax.rsqrt(jnp.mean(values * values, axis=-1, keepdims=True) + eps_norm) * gain_vec
    )


def norm_back(values, gain_vec, incoming):
    _, pull = jax.vjp(rms_norm, values, gain_vec)
    return pull(incoming)


def gelu_back(hidden, incoming):
    _, pull = jax.vjp(partial(jax.nn.gelu, approximate=True), hidden)
    return pull(incoming)[0]


def dense(acts, weight):
    return jnp.dot(acts, weight, preferred_element_type=F32)


def dense_back(incoming, weight):
    return lax.dot_general(
        incoming, weight, (((1,), (1,)), ((), ())), preferred_element_type=F32
    )


def weight_grad(acts, incoming):
    return lax.dot_general(acts, incoming, (((0,), (0,)), ((), ())), preferred_element_type=F32)


def split_heads(tensor):
    return tensor.reshape(tensor.shape[0], -1, HEAD_DIM)


def segment_ids(lengths_row, length):
    places = jnp.arange(length, dtype=jnp.int32)
    total = jnp.zeros((length,), jnp.int32)
    end = jnp.int32(0)
    for slot in range(lengths_row.shape[0]):
        end = end + lengths_row[slot]
        total = total + (places >= end).astype(jnp.int32)
    return total


def bucket_onehot(lookup, first_pos, row_count, length, bucket_count):
    width_all = length + row_count - 1
    window = lax.dynamic_slice_in_dim(lookup, length - first_pos - row_count, width_all)
    return (window[:, None] == jnp.arange(bucket_count, dtype=jnp.int32)[None, :]).astype(F32)


def position_bias(rel_table, lookup, first_pos, row_count, length):
    onehot = bucket_onehot(lookup, first_pos, row_count, length, rel_table.shape[0])
    width_all = length + row_count - 1
    per_offset = jnp.dot(onehot, rel_table, precision=lax.Precision.HIGHEST).T
    padded = jnp.pad(per_offset, ((0, 0), (0, 1)))
    repeated = jnp.tile(padded, (1, row_count))
    trimmed = repeated[:, row_count - 1 : row_count - 1 + row_count * width_all]
    return trimmed.reshape(-1, row_count, width_all)[:, :, :length]


def bias_grad(grad_sum, lookup, first_pos, bucket_count):
    head_count, row_count, length = grad_sum.shape
    width_all = length + row_count - 1
    padded = jnp.pad(grad_sum, ((0, 0), (0, 0), (0, row_count)))
    flat_grad = jnp.pad(padded.reshape(head_count, -1), ((0, 0), (row_count - 1, 1)))
    skewed = flat_grad.reshape(head_count, row_count, length + row_count + 1)[:, :, :width_all]
    per_offset = jnp.sum(skewed, axis=1)
    onehot = bucket_onehot(lookup, first_pos, row_count, length, bucket_count)
    return jnp.dot(onehot.T, per_offset.T, precision=lax.Precision.HIGHEST)


def raw_scores(queries, key_rows, pos_bias, allowed):
    scores = jnp.einsum(
        "qhd,khd->hqk", split_heads(queries), split_heads(key_rows), preferred_element_type=F32
    )
    if pos_bias is not None:
        scores = scores + pos_bias
    return jnp.where(allowed[None], scores, negative)


def attend_fwd(queries, key_rows, values, pos_bias, allowed):
    scores = raw_scores(queries, key_rows, pos_bias, allowed)
    row_max = jnp.max(scores, axis=-1, keepdims=True)
    exponent = jnp.exp(scores - row_max)
    row_sum = jnp.sum(exponent, axis=-1, keepdims=True)
    probs_low = (exponent / row_sum).astype(BF)
    mixed = jnp.einsum("hqk,khd->qhd", probs_low, split_heads(values), preferred_element_type=F32)
    return (mixed.reshape(queries.shape), row_max + jnp.log(row_sum))


def attend_back(queries, key_rows, values, pos_bias, allowed, log_total, incoming):
    scores = raw_scores(queries, key_rows, pos_bias, allowed)
    probs_f = jnp.exp(scores - log_total)
    grad_heads = split_heads(incoming)
    grad_values = jnp.einsum(
        "hqk,qhd->khd", probs_f.astype(BF), grad_heads, preferred_element_type=F32
    )
    grad_probs = jnp.einsum(
        "qhd,khd->hqk", grad_heads, split_heads(values), preferred_element_type=F32
    )
    grad_scores = (
        probs_f * (grad_probs - jnp.sum(probs_f * grad_probs, axis=-1, keepdims=True))
    ).astype(BF)
    grad_queries = jnp.einsum(
        "hqk,khd->qhd", grad_scores, split_heads(key_rows), preferred_element_type=F32
    )
    grad_keys = jnp.einsum(
        "hqk,qhd->khd", grad_scores, split_heads(queries), preferred_element_type=F32
    )
    return (
        grad_queries.reshape(queries.shape),
        grad_keys.reshape(key_rows.shape),
        grad_values.reshape(key_rows.shape),
        grad_scores.astype(F32),
    )


def flip(value, axis, bit):
    count = lax.axis_size(axis)
    return lax.ppermute(value, axis, [(i, i ^ bit) for i in range(count)])


def swap_rows(value):
    dp, seq = lax.axis_size("dp"), lax.axis_size("seq")
    half = seq // 2
    pairs = []
    for d in range(dp):
        for s in range(seq):
            if (d & 1) != (s >= half):
                pairs.append((d * seq + s, (d ^ 1) * seq + (s ^ half)))
    return lax.ppermute(value, ("dp", "seq"), pairs)


def gather_row(own):
    other = flip(own, "seq", 1)
    core_own = flip(own, "dp", 1)
    core_other = flip(other, "dp", 1)
    return [own, other, core_own, core_other]


def scatter_row(parts):
    low = [part.astype(BF) for part in parts]
    got = flip(jnp.stack([low[2], low[3]]), "dp", 1).astype(F32)
    mine = parts[0] + got[0]
    theirs = (parts[1] + got[1]).astype(BF)
    return mine + flip(theirs, "seq", 1).astype(F32)


def natural(parts, quarter):
    rel = jnp.stack(parts)
    return jnp.concatenate(
        [lax.dynamic_index_in_dim(rel, quarter ^ b, 0, keepdims=False) for b in range(4)]
    )


def relative(whole, quarter):
    nat = whole.reshape(4, -1, whole.shape[-1])
    return [lax.dynamic_index_in_dim(nat, quarter ^ b, 0, keepdims=False) for b in range(4)]


def reduce_weight(grad, late_first):
    dp, seq = lax.axis_size("dp"), lax.axis_size("seq")
    bits = dp.bit_length() - 1
    rows, cols = grad.shape
    order = [0] + (list(range(bits - 1, 0, -1)) if late_first else list(range(1, bits)))
    me = lax.axis_index("dp")
    now = grad.astype(BF).reshape([2] * bits + [rows // dp, cols])
    left = list(range(bits - 1, -1, -1))
    for bit in order:
        axis = left.index(bit)
        mine = (me >> bit) & 1
        keep = lax.dynamic_index_in_dim(now, mine, axis, keepdims=False)
        send = lax.dynamic_index_in_dim(now, 1 - mine, axis, keepdims=False)
        left.pop(axis)
        total = keep.astype(F32) + flip(send, "dp", 1 << bit).astype(F32)
        now = total.astype(BF)
    me = lax.axis_index("seq")
    width = cols
    total = now.astype(F32)
    for step in (seq // 2, 1):
        width = width // 2
        mine = jnp.where((me & step) != 0, 1, 0)
        keep = lax.dynamic_slice_in_dim(total, mine * width, width, 1)
        send = lax.dynamic_slice_in_dim(total, (1 - mine) * width, width, 1).astype(BF)
        total = keep + flip(send, "seq", step).astype(F32)
    return total


def all_sum(flat):
    for bit in range(lax.axis_size("dp").bit_length() - 1):
        flat = flat + flip(flat, "dp", 1 << bit)
    for bit in range(lax.axis_size("seq").bit_length() - 1):
        flat = flat + flip(flat, "seq", 1 << bit)
    return flat


def flatten_all(members):
    return jnp.concatenate([member.reshape(-1) for member in members])


def unflatten(flat_grad, members):
    result = []
    offset = 0
    for member in members:
        result.append(flat_grad[offset : offset + member.size].reshape(member.shape))
        offset += member.size
    return result


def on_device(
    encoder_input,
    decoder_input,
    output_grad,
    segment_lengths,
    bucket_table,
    enc_gain1,
    enc_qkv,
    enc_proj,
    enc_rel,
    enc_gain2,
    enc_wi,
    enc_wo,
    enc_gainf,
    dec_gain1,
    dec_qkv,
    dec_proj,
    dec_rel,
    dec_gain2,
    cross_q,
    cross_kv,
    cross_proj,
    dec_gain3,
    dec_wi,
    dec_wo,
):
    seq_count = lax.axis_size("seq")
    device_count = lax.axis_size(("dp", "seq"))
    _, query_len, model_width = encoder_input.shape
    full_len = query_len * seq_count
    core = lax.axis_index("dp") & 1
    place = lax.axis_index("seq")
    moved = core != (place // 2)
    quarter = (place & 1) + 2 * core
    first_pos = quarter * query_len
    inner = enc_proj.shape[0]
    bucket_count = enc_rel.shape[0]

    def bring(value):
        return jnp.where(moved, swap_rows(value), value)

    lengths = bring(segment_lengths)[0]
    enc_own = bring(encoder_input[0])
    enc_all = natural(gather_row(enc_own), quarter)
    dec_own = bring(decoder_input[0])
    dec_all = natural(gather_row(dec_own), quarter)
    top_low = bring(output_grad[0])

    ids_full = segment_ids(lengths, full_len)
    ids_own = lax.dynamic_slice_in_dim(ids_full, first_pos, query_len)
    same_seg = ids_own[:, None] == ids_full[None, :]
    key_pos = jnp.arange(full_len, dtype=jnp.int32)
    query_pos = first_pos + jnp.arange(query_len, dtype=jnp.int32)
    causal = same_seg & (key_pos[None, :] <= query_pos[:, None])
    enc_bias = position_bias(enc_rel, bucket_table, first_pos, query_len, full_len)
    dec_bias = position_bias(dec_rel, bucket_table, first_pos, query_len, full_len)

    enc_in = enc_own.astype(F32)
    enc_a_all = rms_norm(enc_all.astype(F32), enc_gain1).astype(BF)
    enc_a = rms_norm(enc_in, enc_gain1).astype(BF)
    enc_query = dense(enc_a, enc_qkv[:, :inner]).astype(BF)
    enc_pair = dense(enc_a_all, enc_qkv[:, inner:]).astype(BF)
    enc_keys, enc_vals = enc_pair[:, :inner], enc_pair[:, inner:]
    enc_mix, enc_lse = attend_fwd(enc_query, enc_keys, enc_vals, enc_bias, same_seg)
    enc_mix_low = enc_mix.astype(BF)
    enc_att = dense(enc_mix_low, enc_proj)
    enc_h1 = enc_in + enc_att
    enc_b = rms_norm(enc_h1, enc_gain2).astype(BF)
    enc_u = dense(enc_b, enc_wi)
    enc_g = jax.nn.gelu(enc_u, approximate=True).astype(BF)
    enc_ffn = dense(enc_g, enc_wo)
    enc_h2 = enc_h1 + enc_ffn
    encoded = rms_norm(enc_h2, enc_gainf).astype(BF)
    encoded_all = natural(gather_row(encoded), quarter)

    dec_in = dec_own.astype(F32)
    dec_a_all = rms_norm(dec_all.astype(F32), dec_gain1).astype(BF)
    dec_a = rms_norm(dec_in, dec_gain1).astype(BF)
    dec_query = dense(dec_a, dec_qkv[:, :inner]).astype(BF)
    dec_pair = dense(dec_a_all, dec_qkv[:, inner:]).astype(BF)
    dec_keys, dec_vals = dec_pair[:, :inner], dec_pair[:, inner:]
    dec_mix, dec_lse = attend_fwd(dec_query, dec_keys, dec_vals, dec_bias, causal)
    dec_mix_low = dec_mix.astype(BF)
    dec_att = dense(dec_mix_low, dec_proj)
    dec_h1 = dec_in + dec_att
    dec_c = rms_norm(dec_h1, dec_gain2).astype(BF)
    cross_query = dense(dec_c, cross_q).astype(BF)

    cross_pair = dense(encoded_all, cross_kv).astype(BF)
    cross_keys, cross_vals = cross_pair[:, :inner], cross_pair[:, inner:]
    cross_mix, cross_lse = attend_fwd(cross_query, cross_keys, cross_vals, None, same_seg)
    cross_mix_low = cross_mix.astype(BF)
    cross_att = dense(cross_mix_low, cross_proj)
    dec_h2 = dec_h1 + cross_att
    dec_b = rms_norm(dec_h2, dec_gain3).astype(BF)
    dec_u = dense(dec_b, dec_wi)
    dec_g = jax.nn.gelu(dec_u, approximate=True).astype(BF)
    dec_ffn = dense(dec_g, dec_wo)
    dec_h3 = dec_h2 + dec_ffn
    dec_output = bring(dec_h3.astype(BF))
    stat_terms = jnp.stack(
        [
            jnp.sum(member * member)
            for member in (enc_att, enc_h1, enc_ffn, enc_h2, dec_att, cross_att, dec_ffn, dec_h3)
        ]
    )

    top_grad = top_low.astype(F32)
    dec_wo_grad = weight_grad(dec_g, top_low)
    dec_u_grad = gelu_back(dec_u, dense_back(top_low, dec_wo)).astype(BF)
    dec_wi_grad = weight_grad(dec_b, dec_u_grad)
    dec_h2_part, dec_gain3_grad = norm_back(dec_h2, dec_gain3, dense_back(dec_u_grad, dec_wi))
    dec_h2_grad = top_grad + dec_h2_part
    cross_att_grad = dec_h2_grad.astype(BF)
    cross_proj_grad = weight_grad(cross_mix_low, cross_att_grad)
    cross_mix_grad = dense_back(cross_att_grad, cross_proj).astype(BF)
    cross_q_part, cross_k_part, cross_v_part, _ = attend_back(
        cross_query, cross_keys, cross_vals, None, same_seg, cross_lse, cross_mix_grad
    )
    cross_pair_grad = jnp.concatenate([cross_k_part, cross_v_part], axis=-1).astype(BF)
    encoded_grad = scatter_row(relative(dense_back(cross_pair_grad, cross_kv), quarter))
    cross_query_grad = cross_q_part.astype(BF)
    cross_q_grad = weight_grad(dec_c, cross_query_grad)
    cross_kv_grad = weight_grad(encoded_all, cross_pair_grad)
    dec_h1_part, dec_gain2_grad = norm_back(
        dec_h1, dec_gain2, dense_back(cross_query_grad, cross_q)
    )
    dec_h1_grad = dec_h2_grad + dec_h1_part
    dec_att_grad = dec_h1_grad.astype(BF)
    dec_proj_grad = weight_grad(dec_mix_low, dec_att_grad)
    dec_mix_grad = dense_back(dec_att_grad, dec_proj).astype(BF)
    dec_q_part, dec_k_part, dec_v_part, dec_bias_sum = attend_back(
        dec_query, dec_keys, dec_vals, dec_bias, causal, dec_lse, dec_mix_grad
    )
    dec_query_grad = dec_q_part.astype(BF)
    dec_pair_grad = jnp.concatenate([dec_k_part, dec_v_part], axis=-1).astype(BF)
    dec_qkv_grad = jnp.concatenate(
        [weight_grad(dec_a, dec_query_grad), weight_grad(dec_a_all, dec_pair_grad)], axis=1
    )
    dec_a_parts = relative(dense_back(dec_pair_grad, dec_qkv[:, inner:]), quarter)
    dec_a_parts[0] = dec_a_parts[0] + dense_back(dec_query_grad, dec_qkv[:, :inner])
    dec_in_part, dec_gain1_grad = norm_back(dec_in, dec_gain1, scatter_row(dec_a_parts))
    decoder_grad = bring((dec_h1_grad + dec_in_part).astype(BF))
    dec_rel_grad = bias_grad(dec_bias_sum, bucket_table, first_pos, bucket_count)

    enc_h2_grad, enc_gainf_grad = norm_back(enc_h2, enc_gainf, encoded_grad)
    enc_ffn_grad = enc_h2_grad.astype(BF)
    enc_wo_grad = weight_grad(enc_g, enc_ffn_grad)
    enc_u_grad = gelu_back(enc_u, dense_back(enc_ffn_grad, enc_wo)).astype(BF)
    enc_wi_grad = weight_grad(enc_b, enc_u_grad)
    enc_h1_part, enc_gain2_grad = norm_back(enc_h1, enc_gain2, dense_back(enc_u_grad, enc_wi))
    enc_h1_grad = enc_h2_grad + enc_h1_part
    enc_att_grad = enc_h1_grad.astype(BF)
    enc_proj_grad = weight_grad(enc_mix_low, enc_att_grad)
    enc_mix_grad = dense_back(enc_att_grad, enc_proj).astype(BF)
    enc_q_part, enc_k_part, enc_v_part, enc_bias_sum = attend_back(
        enc_query, enc_keys, enc_vals, enc_bias, same_seg, enc_lse, enc_mix_grad
    )
    enc_query_grad = enc_q_part.astype(BF)
    enc_pair_grad = jnp.concatenate([enc_k_part, enc_v_part], axis=-1).astype(BF)
    enc_qkv_grad = jnp.concatenate(
        [weight_grad(enc_a, enc_query_grad), weight_grad(enc_a_all, enc_pair_grad)], axis=1
    )
    enc_a_parts = relative(dense_back(enc_pair_grad, enc_qkv[:, inner:]), quarter)
    enc_a_parts[0] = enc_a_parts[0] + dense_back(enc_query_grad, enc_qkv[:, :inner])
    enc_in_part, enc_gain1_grad = norm_back(enc_in, enc_gain1, scatter_row(enc_a_parts))
    encoder_grad = bring((enc_h1_grad + enc_in_part).astype(BF))
    enc_rel_grad = bias_grad(enc_bias_sum, bucket_table, first_pos, bucket_count)

    small_members = [
        stat_terms,
        enc_gain1_grad,
        enc_rel_grad,
        enc_gain2_grad,
        enc_gainf_grad,
        dec_gain1_grad,
        dec_rel_grad,
        dec_gain2_grad,
        dec_gain3_grad,
    ]
    flat = flatten_all(small_members)
    flat = jnp.pad(flat, (0, -flat.size % 1024)).reshape(-1, 128)
    (
        stat_total,
        enc_gain1_sum,
        enc_rel_sum,
        enc_gain2_sum,
        enc_gainf_sum,
        dec_gain1_sum,
        dec_rel_sum,
        dec_gain2_sum,
        dec_gain3_sum,
    ) = unflatten(all_sum(flat).reshape(-1), small_members)
    blocks = [
        reduce_weight(grad, late)
        for grad, late in (
            (dec_wo_grad, False),
            (dec_wi_grad, True),
            (cross_proj_grad, False),
            (cross_q_grad, False),
            (cross_kv_grad, True),
            (dec_proj_grad, False),
            (dec_qkv_grad, True),
            (enc_wo_grad, False),
            (enc_wi_grad, True),
            (enc_proj_grad, False),
            (enc_qkv_grad, True),
        )
    ]
    token_total = float(query_len * model_width * device_count)
    sublayer_rms = jnp.sqrt(stat_total / token_total)
    return (
        dec_output[None],
        encoder_grad[None],
        decoder_grad[None],
        sublayer_rms,
        enc_gain1_sum,
        blocks[10],
        blocks[9],
        enc_rel_sum,
        enc_gain2_sum,
        blocks[8],
        blocks[7],
        enc_gainf_sum,
        dec_gain1_sum,
        blocks[6],
        blocks[5],
        dec_rel_sum,
        dec_gain2_sum,
        blocks[3],
        blocks[4],
        blocks[2],
        dec_gain3_sum,
        blocks[1],
        blocks[0],
    )


def solution(mesh):
    rows = P("dp", "seq", None)
    both = P("dp", "seq")
    return jax.shard_map(
        on_device,
        mesh=mesh,
        in_specs=(rows, rows, rows, P("dp", None)) + (P(),) * 20,
        out_specs=(
            (rows,) * 3
            + (P(),) * 2
            + (both,) * 2
            + (P(),) * 2
            + (both,) * 2
            + (P(),) * 2
            + (both,) * 2
            + (P(),) * 2
            + (both,) * 3
            + (P(),)
            + (both,) * 2
        ),
        check_vma=False,
    )
```

```python
import functools

import jax
import jax.numpy as jnp
from jax import lax
from jax.experimental import pallas as pl
from jax.experimental.pallas import tpu as pltpu
from jax.sharding import PartitionSpec as P

HEAD_DIM = 64
LANES = 128
BF = jnp.bfloat16
F32 = jnp.float32

eps_norm = 1e-06
negative = -1000000000.0
gelu_in = 0.7978845608028654
gelu_cube = 0.044715

ANY = pl.BlockSpec(memory_space=pl.ANY)
SMALL = pl.BlockSpec(memory_space=pltpu.VMEM)
SCALARS = pl.BlockSpec(memory_space=pltpu.SMEM)
VMEM_BYTES = 60 << 20


def mm(left, right):
    return jnp.dot(left, right, preferred_element_type=F32)


def mm_nt(left, right):
    return lax.dot_general(left, right, (((1,), (1,)), ((), ())), preferred_element_type=F32)


def start(source, target, sem):
    copy = pltpu.make_async_copy(source, target, sem)
    copy.start()
    return copy


def rows_of(step, size):
    return pl.ds(pl.multiple_of(step * size, size), size)


def chunks(count, body):
    def step(i, carry):
        body(i)
        return carry

    lax.fori_loop(0, count, step, 0)


def inv_rms(values):
    return lax.rsqrt(jnp.mean(values * values, axis=-1, keepdims=True) + eps_norm)


def norm_into(source, gain, target, rows, chunk=64):
    def body(i):
        at = rows_of(i, chunk)
        v = source[at, :].astype(F32)
        target[at, :] = (v * inv_rms(v) * gain).astype(target.dtype)

    chunks(rows // chunk, body)


def norm_back_into(values, gain, incoming, residual, target, grad_sum, rows, chunk=32):
    grad_sum[...] = jnp.zeros_like(grad_sum)

    def body(i):
        at = rows_of(i, chunk)
        v = values[at, :]
        dy = incoming[at, :]
        r = inv_rms(v)
        hat = v * r
        part = dy * hat
        grad_sum[...] += jnp.sum(part.reshape(chunk // 8, 8, part.shape[-1]), axis=0)
        scaled = dy * gain
        mean = jnp.mean(scaled * hat, axis=-1, keepdims=True)
        out = r * (scaled - hat * mean)
        target[at, :] = out if residual is None else residual[at, :].astype(F32) + out

    chunks(rows // chunk, body)


def square_sum(values):
    rows, width = values.shape
    return jnp.sum((values * values).reshape(rows // 8, 8, width), axis=0)


def gelu_pair(u):
    sq = u * u
    t = jnp.tanh(gelu_in * u * (1.0 + gelu_cube * sq))
    half = 0.5 * (1.0 + t)
    slope = half + 0.5 * u * (1.0 - t * t) * (gelu_in * (1.0 + 3.0 * gelu_cube * sq))
    return u * half, slope


def place_ids(info, shape, axis, base):
    place = lax.broadcasted_iota(jnp.int32, shape, axis) + base
    ids = jnp.zeros(shape, jnp.int32)
    for slot in range(1, 5):
        ids = ids + (place >= info[slot]).astype(jnp.int32)
    return place, ids


def fill_mask(info, mask, causal):
    rows, keys = mask.shape
    first = info[0] * rows
    key_place, key_ids = place_ids(info, (1, keys), 1, 0)

    def body(i):
        place, ids = place_ids(info, (32, 1), 0, first + i * 32)
        allowed = ids == key_ids
        if causal:
            allowed = jnp.logical_and(allowed, key_place <= place)
        mask[rows_of(i, 32), :] = jnp.where(allowed, 0.0, negative)

    chunks(rows // 32, body)


def lane_split(pair):
    low = lax.broadcasted_iota(jnp.int32, pair.shape, 1) < HEAD_DIM
    zero = jnp.zeros_like(pair)
    return jnp.concatenate([jnp.where(low, pair, zero), jnp.where(low, zero, pair)], axis=0)


def lane_join(first, second):
    low = lax.broadcasted_iota(jnp.int32, first.shape, 1) < HEAD_DIM
    return jnp.where(low, first, second)


def attend_fwd(q, kv, table, mask, probs, probs_out, sem, scores, toeplitz, mix):
    rows, inner = q.shape
    keys = kv.shape[0]
    half = LANES
    for pair in range(inner // LANES):
        lanes = slice(pair * LANES, (pair + 1) * LANES)
        scores[...] = mm_nt(lane_split(q[:, lanes]), kv[:, lanes])
        for side in range(2):
            head = 2 * pair + side
            if table is not None:
                width = table.shape[1]
                row = jnp.broadcast_to(table[head : head + 1, :], (half, width))
                toeplitz[...] = pltpu.roll(row, width - half + 1, 1, stride=1, stride_axis=0)
            for block in range(rows // half):
                shift = half * (rows // half - 1 - block)

                def body(i, side=side, block=block, head=head, shift=shift):
                    at = rows_of(i, 32)
                    whole = pl.ds(pl.multiple_of(side * rows + block * half + i * 32, 32), 32)
                    mine = pl.ds(pl.multiple_of(block * half + i * 32, 32), 32)
                    s = scores[whole, :] + mask[mine, :]
                    if table is not None:
                        s = s + toeplitz[at, shift : shift + keys]
                    e = jnp.exp(s - jnp.max(s, axis=-1, keepdims=True))
                    total = jnp.sum(e, axis=-1, keepdims=True)
                    probs[head, mine, :] = (e * (1.0 / total)).astype(BF)

                chunks(half // 32, body)
        v_pair = kv[:, inner + pair * LANES : inner + (pair + 1) * LANES]
        mix[:, lanes] = lane_join(
            mm(probs[2 * pair], v_pair), mm(probs[2 * pair + 1], v_pair)
        ).astype(BF)
        at = pl.ds(2 * pair, 2)
        start(probs.at[at], probs_out.at[at], sem)


def attend_back(q, kv, probs, out_grad, mix, dq, dkv_t, scores, dscores, delta, skew, spread):
    rows, inner = q.shape
    keys = kv.shape[0]
    half = LANES
    for pair in range(inner // LANES):
        lanes = slice(pair * LANES, (pair + 1) * LANES)
        later = slice(inner + pair * LANES, inner + (pair + 1) * LANES)
        do_pair = out_grad[:, lanes]
        do_two = lane_split(do_pair)
        scores[...] = mm_nt(do_two, kv[:, later])
        both = do_two.astype(F32) * jnp.concatenate([mix[:, lanes], mix[:, lanes]], axis=0).astype(F32)
        delta[...] = jnp.broadcast_to(jnp.sum(both, axis=-1, keepdims=True), delta.shape)
        for side in range(2):
            head = 2 * pair + side
            for block in range(rows // half):
                shift = half * (rows // half - 1 - block)

                def body(i, side=side, block=block, head=head, shift=shift):
                    at = rows_of(i, 32)
                    whole = pl.ds(pl.multiple_of(side * rows + block * half + i * 32, 32), 32)
                    mine = pl.ds(pl.multiple_of(block * half + i * 32, 32), 32)
                    ds = probs[head, mine, :].astype(F32) * (scores[whole, :] - delta[whole, 0:1])
                    dscores[whole, :] = ds.astype(BF)
                    if skew is not None:
                        if block == 0:
                            skew[at, shift : shift + keys] = ds
                        else:
                            skew[at, shift : shift + keys] += ds

                if skew is not None and block == 0:
                    skew[:, 0:shift] = jnp.zeros((half, shift), F32)
                chunks(half // 32, body)
            if skew is not None:
                width = spread.shape[1]
                wide = skew.shape[1]
                total = jnp.zeros((8, width), F32)
                for group in range(half // 8):
                    part = jnp.concatenate(
                        [skew[8 * group : 8 * group + 8, :], jnp.zeros((8, width - wide), F32)], axis=1
                    )
                    by = half - 8 - 8 * group
                    total = total + (pltpu.roll(part, by, 1) if by else part)
                left = 7 - lax.broadcasted_iota(jnp.int32, (8, width), 0)
                for bit in (1, 2, 4):
                    total = jnp.where((left & bit) != 0, pltpu.roll(total, bit, 1), total)
                spread[head : head + 1, :] = jnp.sum(total, axis=0, keepdims=True)
        k_pair = kv[:, lanes]
        dq[:, lanes] = lane_join(mm(dscores[0:rows, :], k_pair), mm(dscores[rows:, :], k_pair)).astype(BF)
        q_two = lane_split(q[:, lanes])
        dkv_t[lanes, :] = mm(q_two.T, dscores[...]).astype(BF)
        dv = mm(do_two[0:rows].T, probs[2 * pair]) + mm(do_two[rows:].T, probs[2 * pair + 1])
        dkv_t[later, :] = dv.astype(BF)


class Blocks:
    def __init__(self, info, keep, send, dp, seq):
        self.info, self.keep, self.send, self.dp, self.seq = info, keep, send, dp, seq

    def put(self, grad, base, sem):
        rows, cols = grad.shape
        tall, wide = rows // self.dp, cols // self.seq
        me, place = self.info[5], self.info[6]

        def body(j):
            for s in range(self.seq):
                for ch in range(wide // LANES):
                    col = pl.ds(pl.multiple_of((place ^ s) * wide + ch * LANES, LANES), LANES)
                    to = pl.ds(base + ch * tall, tall)
                    for target, flip_core in ((self.keep, 0), (self.send, 1)):
                        row = pl.ds(pl.multiple_of((me ^ (2 * j) ^ flip_core) * tall, tall), tall)
                        start(grad.at[row, col], target.at[j, s, to, :], sem)

        chunks(self.dp // 2, body)

    def wait(self, sem):
        for target in (self.keep, self.send):
            pltpu.make_async_copy(target, target, sem).wait()


def block_rows(shape, dp, seq):
    return shape[0] * shape[1] // (dp * seq * LANES)


def self_fwd_kernel(causal, last, info, x0, x1, x2, x3, gain, w_qkv, w_proj, table, *rest):
    if last == "ffn":
        (gain2, w_in, w_out, gainf), rest = rest[:4], rest[4:]
        outs, rest = rest[:12], rest[12:]
        a_out, kv_out, q_out, p_out, o_out, h1_out, b_out, g_out, s_out, h2_out, fin_out, small = outs
        (x, wq, wp, a, kv, q, probs, scores, toeplitz, mask, mix, h1, normed, wi, wo, hidden, act, slope, h2, sems) = rest
    else:
        (gain2, w_in), rest = rest[:2], rest[2:]
        outs, rest = rest[:8], rest[8:]
        a_out, kv_out, q_out, p_out, o_out, h1_out, b_out, fin_out, small = outs + rest[:1]
        rest = rest[1:]
        (x, wq, wp, a, kv, q, probs, scores, toeplitz, mask, mix, h1, normed, wi, fin, sems) = rest
    rows = h1.shape[0]
    inner = w_proj.shape[0]
    quarter = info[0]
    at_own = rows_of(quarter, rows)
    loads = [
        start(src, x.at[rows_of(quarter ^ j, rows)], sems.at[j]) for j, src in enumerate((x0, x1, x2, x3))
    ]
    load_q = start(w_qkv, wq, sems.at[4])
    load_p = start(w_proj, wp, sems.at[5])
    load_i = start(w_in, wi, sems.at[6])
    if last == "ffn":
        load_o = start(w_out, wo, sems.at[7])
    fill_mask(info, mask, causal)
    for load in loads:
        load.wait()
    norm_into(x, gain[...], a, x.shape[0])
    saves = [start(a, a_out, sems.at[8])]
    load_q.wait()
    q[...] = mm(a[at_own, :], wq[:, 0:inner]).astype(BF)

    def project(i):
        at = rows_of(i, rows)
        kv[at, :] = mm(a[at, :], wq[:, inner:]).astype(BF)

    chunks(4, project)
    saves += [start(kv, kv_out, sems.at[9]), start(q, q_out, sems.at[10])]
    attend_fwd(q, kv, table, mask, probs, p_out, sems.at[11], scores, toeplitz, mix)
    saves.append(pltpu.make_async_copy(probs, p_out, sems.at[11]))
    saves.append(start(mix, o_out, sems.at[12]))
    load_p.wait()
    att = mm(mix[...], wp[...])
    small[0:8, :] = square_sum(att)
    first = x[at_own, :].astype(F32) + att
    h1[...] = first
    small[8:16, :] = square_sum(first)
    saves.append(start(h1, h1_out, sems.at[13]))
    norm_into(h1, gain2[...], normed, rows)
    saves.append(start(normed, b_out, sems.at[14]))
    load_i.wait()
    if last == "ffn":
        hidden[...] = mm(normed[...], wi[...])

        def activate(i):
            at = rows_of(i, 16)
            value, rate = gelu_pair(hidden[at, :])
            act[at, :] = value.astype(BF)
            slope[at, :] = rate.astype(BF)

        chunks(rows // 16, activate)
        saves += [start(act, g_out, sems.at[15]), start(slope, s_out, sems.at[16])]
        load_o.wait()
        ffn = mm(act[...], wo[...])
        small[16:24, :] = square_sum(ffn)
        second = h1[...] + ffn
        h2[...] = second
        small[24:32, :] = square_sum(second)
        saves.append(start(h2, h2_out, sems.at[17]))
        norm_into(h2, gainf[...], fin_out, rows)
    else:
        fin_out[...] = mm(normed[...], wi[...]).astype(BF)
    for save in saves:
        save.wait()


def cross_kernel(
    info, e0, e1, e2, e3, q_in, d1_in, top_in, w_kv, w_proj, gain, w_in, w_out,
    enc_out, kv_out, p_out, o_out, out_out, g2_out, keep, send, small,
    enc, kv, q, probs, scores, mask, mix, h, top, normed, wkv, wp, wi, wo, hidden, act, slope, du, back, gsum, grad_a, grad_b, sems,
    dp, seq,
):
    rows = h.shape[0]
    quarter = info[0]
    loads = [
        start(src, enc.at[rows_of(quarter ^ j, rows)], sems.at[j]) for j, src in enumerate((e0, e1, e2, e3))
    ]
    load_kv = start(w_kv, wkv, sems.at[4])
    load_q = start(q_in, q, sems.at[5])
    load_p = start(w_proj, wp, sems.at[6])
    load_d = start(d1_in, h, sems.at[7])
    load_i = start(w_in, wi, sems.at[8])
    load_o = start(w_out, wo, sems.at[9])
    load_t = start(top_in, top, sems.at[10])
    fill_mask(info, mask, False)
    for load in loads:
        load.wait()
    saves = [start(enc, enc_out, sems.at[11])]
    load_kv.wait()

    def project(i):
        at = rows_of(i, rows)
        kv[at, :] = mm(enc[at, :], wkv[...]).astype(BF)

    chunks(4, project)
    saves.append(start(kv, kv_out, sems.at[12]))
    load_q.wait()
    attend_fwd(q, kv, None, mask, probs, p_out, sems.at[13], scores, None, mix)
    saves.append(pltpu.make_async_copy(probs, p_out, sems.at[13]))
    saves.append(start(mix, o_out, sems.at[14]))
    load_p.wait()
    load_d.wait()
    att = mm(mix[...], wp[...])
    small[0:8, :] = square_sum(att)
    h[...] = h[...] + att
    norm_into(h, gain[...], normed, rows)
    load_i.wait()
    hidden[...] = mm(normed[...], wi[...])

    def activate(i):
        at = rows_of(i, 16)
        value, rate = gelu_pair(hidden[at, :])
        act[at, :] = value.astype(BF)
        slope[at, :] = rate.astype(BF)

    chunks(rows // 16, activate)
    load_o.wait()
    ffn = mm(act[...], wo[...])
    small[8:16, :] = square_sum(ffn)
    third = h[...] + ffn
    small[16:24, :] = square_sum(third)
    out_out[...] = third.astype(BF)
    load_t.wait()
    ffn_back(top, act, slope, normed, wi, wo, hidden, du, back, grad_a, grad_b, keep, send, info, sems.at[15], dp, seq)
    norm_back_into(h, gain[...], back, top, g2_out, gsum, rows)
    small[24:32, :] = gsum[...]
    for save in saves:
        save.wait()
    Blocks(info, keep, send, dp, seq).wait(sems.at[15])


def ffn_back(top, act, slope, normed, wi, wo, hidden, du, back, grad_wo, grad_wi, keep, send, info, sem, dp, seq):
    rows = top.shape[0]
    blocks = Blocks(info, keep, send, dp, seq)
    hidden[...] = mm_nt(top[...], wo[...])

    def slide(i):
        at = rows_of(i, 16)
        du[at, :] = (hidden[at, :] * slope[at, :].astype(F32)).astype(BF)

    chunks(rows // 16, slide)
    back[...] = mm_nt(du[...], wi[...])
    grad_wo[...] = mm(act[...].T, top[...]).astype(BF)
    blocks.put(grad_wo, 0, sem)
    grad_wi[...] = mm(normed[...].T, du[...]).astype(BF)
    blocks.put(grad_wi, block_rows(grad_wo.shape, dp, seq), sem)


def enc_ffn_back_kernel(
    info, fin_grad, h2_in, gainf, h1_in, gain2, act_in, slope_in, normed_in, w_in, w_out,
    g1_out, keep, send, small,
    up, h2, h1, act, slope, normed, wi, wo, g2, top, hidden, du, back, gsum, grad_a, grad_b, sems,
    dp, seq,
):
    rows = h1.shape[0]
    names = ((fin_grad, up), (h2_in, h2), (h1_in, h1), (act_in, act), (slope_in, slope), (normed_in, normed), (w_in, wi), (w_out, wo))
    loads = [start(src, dst, sems.at[j]) for j, (src, dst) in enumerate(names)]
    for load in loads[:2]:
        load.wait()
    norm_back_into(h2, gainf[...], up, None, g2, gsum, rows)
    small[0:8, :] = gsum[...]
    top[...] = g2[...].astype(BF)
    for load in loads[2:]:
        load.wait()
    ffn_back(top, act, slope, normed, wi, wo, hidden, du, back, grad_a, grad_b, keep, send, info, sems.at[8], dp, seq)
    norm_back_into(h1, gain2[...], back, g2, g1_out, gsum, rows)
    small[8:16, :] = gsum[...]
    Blocks(info, keep, send, dp, seq).wait(sems.at[8])


def attn_back_kernel(info, g_in, o_in, w_proj, p_in, kv_in, q_in, a_in, w_q, *rest, kind, dp, seq):
    if kind == "self":
        (p0, p1, p2, p3, spread, keep, send), rest = rest[:7], rest[7:]
        (g, mix, wp, probs, kv, q, a, wq, gb, do, dq, dkv_t, dkv, scores, dscores, delta, skew, part, wide, grad_p, grad_q, grad_kv, sems) = rest
    else:
        (w_kv, c_in, d1_in, gain), rest = rest[:4], rest[4:]
        (p0, p1, p2, p3, g1_out, keep, send, small), rest = rest[:8], rest[8:]
        (g, mix, wp, probs, kv, q, a, wq, wkv, c, d1, gb, do, dq, dkv_t, dkv, scores, dscores, delta, part, wide, gsum, grad_p, grad_q, grad_kv, sems) = rest
        skew = spread = None
    rows = g.shape[0]
    inner = w_proj.shape[0]
    quarter = info[0]
    names = [(g_in, g), (w_proj, wp), (o_in, mix), (kv_in, kv), (p_in, probs), (q_in, q), (a_in, a), (w_q, wq)]
    if kind == "cross":
        names += [(w_kv, wkv), (c_in, c), (d1_in, d1)]
    loads = [start(src, dst, sems.at[j]) for j, (src, dst) in enumerate(names)]
    for load in loads[:2]:
        load.wait()
    gb[...] = g[...].astype(BF)
    do[...] = mm_nt(gb[...], wp[...]).astype(BF)
    for load in loads[2:]:
        load.wait()
    attend_back(q, kv, probs, do, mix, dq, dkv_t, scores, dscores, delta, skew, spread)
    dkv[...] = dkv_t[...].T
    blocks = Blocks(info, keep, send, dp, seq)
    weight_kv = wkv[...] if kind == "cross" else wq[:, inner:]

    def project(i):
        at = rows_of(i, rows)
        wide[at, :] = mm_nt(dkv[at, :], weight_kv)

    chunks(4, project)
    p1[...] = wide[rows_of(quarter ^ 1, rows), :].astype(BF)
    p2[...] = wide[rows_of(quarter ^ 2, rows), :].astype(BF)
    p3[...] = wide[rows_of(quarter ^ 3, rows), :].astype(BF)
    own = wide[rows_of(quarter, rows), :]
    if kind == "self":
        p0[...] = own + mm_nt(dq[...], wq[:, 0:inner])
        source = a[rows_of(quarter, rows), :]
    else:
        p0[...] = own
        part[...] = mm_nt(dq[...], wq[...])
        norm_back_into(d1, gain[...], part, g, g1_out, gsum, rows)
        small[...] = gsum[...]
        source = c[...]
    grad_p[...] = mm(mix[...].T, gb[...]).astype(BF)
    blocks.put(grad_p, 0, sems.at[11])
    base = block_rows(grad_p.shape, dp, seq)
    grad_q[...] = mm(source.T, dq[...]).astype(BF)
    grad_kv[...] = mm(a[...].T, dkv[...]).astype(BF)
    if kind == "self":
        put_columns(blocks, (grad_q, grad_kv), base, sems.at[11])
    else:
        blocks.put(grad_q, base, sems.at[11])
        blocks.put(grad_kv, base + block_rows(grad_q.shape, dp, seq), sems.at[11])
    blocks.wait(sems.at[11])


def put_columns(blocks, grads, base, sem):
    rows = grads[0].shape[0]
    cols = grads[0].shape[1] + grads[1].shape[1]
    tall, wide = rows // blocks.dp, cols // blocks.seq
    per = wide // LANES
    me, place = blocks.info[5], blocks.info[6]

    def body(j):
        for chunk in range(cols // LANES):
            s = (chunk // per) ^ place
            to = pl.ds(base + (chunk % per) * tall, tall)
            first = chunk * LANES
            grad, col = (grads[0], first) if first < grads[0].shape[1] else (grads[1], first - grads[0].shape[1])
            for target, flip_core in ((blocks.keep, 0), (blocks.send, 1)):
                row = pl.ds(pl.multiple_of((me ^ (2 * j) ^ flip_core) * tall, tall), tall)
                start(grad.at[row, pl.ds(col, LANES)], target.at[j, s, to, :], sem)

    chunks(blocks.dp // 2, body)


def call(kernel, name, args, outs, scratch, specs, out_specs, flops, bytes_accessed):
    return pl.pallas_call(
        kernel,
        out_shape=outs,
        in_specs=specs,
        out_specs=out_specs,
        scratch_shapes=scratch,
        name=name,
        compiler_params=pltpu.CompilerParams(vmem_limit_bytes=VMEM_BYTES),
        cost_estimate=pl.CostEstimate(flops=flops, bytes_accessed=bytes_accessed, transcendentals=0),
    )(*args)


def sds(shape, dtype=BF):
    return jax.ShapeDtypeStruct(shape, dtype)


def vm(shape, dtype=BF):
    return pltpu.VMEM(shape, dtype)


def flip(value, axis, bit):
    count = lax.axis_size(axis)
    return lax.ppermute(value, axis, [(i, i ^ bit) for i in range(count)])


def swap_rows(value):
    dp, seq = lax.axis_size("dp"), lax.axis_size("seq")
    half = seq // 2
    pairs = []
    for d in range(dp):
        for s in range(seq):
            if (d & 1) != (s >= half):
                pairs.append((d * seq + s, (d ^ 1) * seq + (s ^ half)))
    return lax.ppermute(value, ("dp", "seq"), pairs)


def gather_row(own):
    other = flip(own, "seq", 1)
    core_own = flip(own, "dp", 1)
    core_other = flip(other, "dp", 1)
    return [own, other, core_own, core_other]


def scatter_row(parts):
    got_two = flip(parts[2], "dp", 1)
    got_three = flip(parts[3], "dp", 1)
    theirs = (parts[1].astype(F32) + got_three.astype(F32)).astype(BF)
    return parts[0] + got_two.astype(F32) + flip(theirs, "seq", 1).astype(F32)


def reduce_blocks(keep, send, late_first):
    dp, seq = lax.axis_size("dp"), lax.axis_size("seq")
    rows = keep.shape[2]
    now = (keep.astype(F32) + flip(send, "dp", 1).astype(F32)).astype(BF)
    bits = dp.bit_length() - 2
    now = now.reshape([2] * bits + [seq, rows, LANES])
    left = list(range(bits, 0, -1))
    for bit in range(bits, 0, -1) if late_first else range(1, bits + 1):
        axis = left.index(bit)
        left.pop(axis)
        mine = lax.index_in_dim(now, 0, axis, keepdims=False)
        theirs = lax.index_in_dim(now, 1, axis, keepdims=False)
        now = (mine.astype(F32) + flip(theirs, "dp", 1 << bit).astype(F32)).astype(BF)
    step = 1
    total = now
    while step < seq:
        view = total.reshape(-1, 2, rows, LANES)
        total = view[:, 0].astype(F32) + flip(view[:, 1].astype(BF), "seq", step).astype(F32)
        step *= 2
    return total.reshape(rows, LANES)


def all_sum(flat):
    for bit in range(lax.axis_size("dp").bit_length() - 1):
        flat = flat + flip(flat, "dp", 1 << bit)
    for bit in range(lax.axis_size("seq").bit_length() - 1):
        flat = flat + flip(flat, "seq", 1 << bit)
    return flat


def flatten_all(members):
    return jnp.concatenate([member.reshape(-1) for member in members])


def unflatten(flat_grad, members):
    result = []
    offset = 0
    for member in members:
        result.append(flat_grad[offset : offset + member.size].reshape(member.shape))
        offset += member.size
    return result


def unblock(flat, shape, dp, seq):
    tall, wide = shape[0] // dp, shape[1] // seq
    return flat.reshape(wide // LANES, tall, LANES).transpose(1, 0, 2).reshape(tall, wide)


def offset_onehot(lookup, first_pos, row_count, length, bucket_count):
    width = length + row_count
    window = lax.dynamic_slice_in_dim(jnp.pad(lookup, (0, 1)), length - first_pos - row_count, width)
    return (window[:, None] == jnp.arange(bucket_count, dtype=jnp.int32)[None, :]).astype(F32)


def top_norm_back(values, gain, incoming):
    r = lax.rsqrt(jnp.mean(values * values, axis=-1, keepdims=True) + eps_norm)
    hat = values * r
    scaled = incoming * gain
    return (
        r * (scaled - hat * jnp.mean(scaled * hat, axis=-1, keepdims=True)),
        jnp.sum(incoming * hat, axis=0),
    )


def on_device(
    encoder_input,
    decoder_input,
    output_grad,
    segment_lengths,
    bucket_table,
    enc_gain1,
    enc_qkv,
    enc_proj,
    enc_rel,
    enc_gain2,
    enc_wi,
    enc_wo,
    enc_gainf,
    dec_gain1,
    dec_qkv,
    dec_proj,
    dec_rel,
    dec_gain2,
    cross_q,
    cross_kv,
    cross_proj,
    dec_gain3,
    dec_wi,
    dec_wo,
):
    dp, seq = lax.axis_size("dp"), lax.axis_size("seq")
    _, rows, width = encoder_input.shape
    full = rows * seq
    inner = enc_proj.shape[0]
    heads = enc_rel.shape[1]
    hid = enc_wi.shape[1]
    bucket_count = enc_rel.shape[0]
    me, place = lax.axis_index("dp"), lax.axis_index("seq")
    core = me & 1
    moved = core != (place // 2)
    quarter = (place & 1) + 2 * core
    first_pos = quarter * rows

    def bring(value):
        return jnp.where(moved, swap_rows(value), value)

    def row(vec):
        return vec.reshape(1, -1)

    lengths = bring(segment_lengths)[0]
    enc_own = bring(encoder_input[0])
    enc_blocks = gather_row(enc_own)
    dec_own = bring(decoder_input[0])
    dec_blocks = gather_row(dec_own)
    top_low = bring(output_grad[0])

    end1 = lengths[0]
    end2 = end1 + lengths[1]
    end3 = end2 + lengths[2]
    end4 = end3 + lengths[3]
    info = jnp.stack([quarter, end1, end2, end3, end4, me, place, me]).astype(jnp.int32)
    onehot = offset_onehot(bucket_table, first_pos, rows, full, bucket_count)
    span = onehot.shape[0]
    enc_table = jnp.dot(enc_rel.T, onehot.T, precision=lax.Precision.HIGHEST)
    dec_table = jnp.dot(dec_rel.T, onehot.T, precision=lax.Precision.HIGHEST)

    probs_shape = (heads, rows, full)
    sems = pltpu.SemaphoreType.DMA

    attn_scratch = [
        vm((full, width)),
        vm((width, 3 * inner)),
        vm((inner, width)),
        vm((full, width)),
        vm((full, 2 * inner)),
        vm((rows, inner)),
        vm(probs_shape),
        vm((2 * rows, full), F32),
        vm((LANES, full + rows), F32),
        vm((rows, full), F32),
        vm((rows, inner)),
        vm((rows, width), F32),
        vm((rows, width)),
    ]
    attn_outs = [
        sds((full, width)),
        sds((full, 2 * inner)),
        sds((rows, inner)),
        sds(probs_shape),
        sds((rows, inner)),
        sds((rows, width), F32),
        sds((rows, width)),
    ]
    enc_a, enc_pair, enc_query, enc_probs, enc_mix, enc_h1, enc_b, enc_g, enc_s, enc_h2, encoded, enc_small = call(
        functools.partial(self_fwd_kernel, False, "ffn"),
        "enc_fwd",
        (info, *enc_blocks, row(enc_gain1), enc_qkv, enc_proj, enc_table, row(enc_gain2), enc_wi, enc_wo, row(enc_gainf)),
        attn_outs
        + [sds((rows, hid)), sds((rows, hid)), sds((rows, width), F32), sds((rows, width)), sds((32, width), F32)],
        attn_scratch
        + [
            vm((width, hid)),
            vm((hid, width)),
            vm((rows, hid), F32),
            vm((rows, hid)),
            vm((rows, hid)),
            vm((rows, width), F32),
            sems((18,)),
        ],
        [SCALARS] + [ANY] * 4 + [SMALL, ANY, ANY, SMALL, SMALL, ANY, ANY, SMALL],
        [ANY] * 10 + [SMALL] * 2,
        6_000_000_000,
        20_000_000,
    )
    encoded_blocks = gather_row(encoded)

    dec_a, dec_pair, dec_query, dec_probs, dec_mix, dec_h1, dec_c, cross_query, dec_small = call(
        functools.partial(self_fwd_kernel, True, "query"),
        "dec_fwd",
        (info, *dec_blocks, row(dec_gain1), dec_qkv, dec_proj, dec_table, row(dec_gain2), cross_q),
        attn_outs + [sds((rows, inner)), sds((16, width), F32)],
        attn_scratch + [vm((width, inner)), vm((8, LANES)), sems((18,))],
        [SCALARS] + [ANY] * 4 + [SMALL, ANY, ANY, SMALL, SMALL, ANY],
        [ANY] * 7 + [SMALL] * 2,
        4_000_000_000,
        16_000_000,
    )

    def wide_blocks(*shapes):
        total = sum(block_rows(shape, dp, seq) for shape in shapes)
        return [sds((dp // 2, seq, total, LANES))] * 2

    enc_all, cross_pair, cross_probs, cross_mix, dec_out, g_d2, ffn_keep, ffn_send, cross_small = call(
        functools.partial(cross_kernel, dp=dp, seq=seq),
        "cross_fwd",
        (info, *encoded_blocks, cross_query, dec_h1, top_low, cross_kv, cross_proj, row(dec_gain3), dec_wi, dec_wo),
        [
            sds((full, width)),
            sds((full, 2 * inner)),
            sds(probs_shape),
            sds((rows, inner)),
            sds((rows, width)),
            sds((rows, width), F32),
            *wide_blocks((hid, width), (width, hid)),
            sds((32, width), F32),
        ],
        [
            vm((full, width)),
            vm((full, 2 * inner)),
            vm((rows, inner)),
            vm(probs_shape),
            vm((2 * rows, full), F32),
            vm((rows, full), F32),
            vm((rows, inner)),
            vm((rows, width), F32),
            vm((rows, width)),
            vm((rows, width)),
            vm((width, 2 * inner)),
            vm((inner, width)),
            vm((width, hid)),
            vm((hid, width)),
            vm((rows, hid), F32),
            vm((rows, hid)),
            vm((rows, hid)),
            vm((rows, hid)),
            vm((rows, width), F32),
            vm((8, width), F32),
            vm((hid, width)),
            vm((width, hid)),
            sems((16,)),
        ],
        [SCALARS] + [ANY] * 9 + [SMALL, ANY, ANY],
        [ANY] * 4 + [SMALL] * 2 + [ANY] * 2 + [SMALL],
        7_000_000_000,
        30_000_000,
    )
    dec_output = bring(dec_out)

    def back_scratch(kind):
        out = [
            vm((rows, width), F32),
            vm((rows, inner)),
            vm((inner, width)),
            vm(probs_shape),
            vm((full, 2 * inner)),
            vm((rows, inner)),
            vm((full, width)),
            vm((width, 3 * inner)) if kind == "self" else vm((width, inner)),
        ]
        if kind == "cross":
            out += [vm((width, 2 * inner)), vm((rows, width)), vm((rows, width), F32)]
        out += [
            vm((rows, width)),
            vm((rows, inner)),
            vm((rows, inner)),
            vm((2 * inner, full)),
            vm((full, 2 * inner)),
            vm((2 * rows, full), F32),
            vm((2 * rows, full)),
            vm((2 * rows, LANES), F32),
        ]
        if kind == "self":
            out += [vm((LANES, full + LANES), F32)]
        out += [vm((rows, width), F32), vm((full, width), F32)]
        if kind == "cross":
            out += [vm((8, width), F32)]
        out += [vm((inner, width)), vm((width, inner)), vm((width, 2 * inner)), sems((12,))]
        return out

    part_outs = [sds((rows, width), F32)] + [sds((rows, width))] * 3
    ep0, ep1, ep2, ep3, g_d1, cross_keep, cross_send, gain2_small = call(
        functools.partial(attn_back_kernel, kind="cross", dp=dp, seq=seq),
        "cross_back",
        (info, g_d2, cross_mix, cross_proj, cross_probs, cross_pair, cross_query, enc_all, cross_q, cross_kv, dec_c, dec_h1, row(dec_gain2)),
        part_outs
        + [
            sds((rows, width), F32),
            *wide_blocks((inner, width), (width, inner), (width, 2 * inner)),
            sds((8, width), F32),
        ],
        back_scratch("cross"),
        [SCALARS] + [ANY] * 11 + [SMALL],
        [SMALL] * 5 + [ANY] * 2 + [SMALL],
        7_000_000_000,
        20_000_000,
    )
    g_enc = scatter_row([ep0, ep1, ep2, ep3])

    def self_back(name, grad, mix, proj, probs, pair, query, source, qkv):
        return call(
            functools.partial(attn_back_kernel, kind="self", dp=dp, seq=seq),
            name,
            (info, grad, mix, proj, probs, pair, query, source, qkv),
            part_outs
            + [
                sds((heads, span), F32),
                *wide_blocks((inner, width), (width, 3 * inner)),
            ],
            back_scratch("self"),
            [SCALARS] + [ANY] * 8,
            [SMALL] * 5 + [ANY] * 2,
            7_000_000_000,
            20_000_000,
        )

    dp0, dp1, dp2, dp3, dec_spread, dec_keep, dec_send = self_back(
        "dec_back", g_d1, dec_mix, dec_proj, dec_probs, dec_pair, dec_query, dec_a, dec_qkv
    )
    dec_in = dec_own.astype(F32)
    dec_in_part, dec_gain1_grad = top_norm_back(dec_in, dec_gain1, scatter_row([dp0, dp1, dp2, dp3]))
    decoder_grad = bring((g_d1 + dec_in_part).astype(BF))
    dec_rel_grad = jnp.dot(onehot.T, dec_spread.T, precision=lax.Precision.HIGHEST)

    g_e1, encffn_keep, encffn_send, enc_gain_small = call(
        functools.partial(enc_ffn_back_kernel, dp=dp, seq=seq),
        "enc_ffn_back",
        (info, g_enc, enc_h2, row(enc_gainf), enc_h1, row(enc_gain2), enc_g, enc_s, enc_b, enc_wi, enc_wo),
        [sds((rows, width), F32), *wide_blocks((hid, width), (width, hid)), sds((16, width), F32)],
        [
            vm((rows, width), F32),
            vm((rows, width), F32),
            vm((rows, width), F32),
            vm((rows, hid)),
            vm((rows, hid)),
            vm((rows, width)),
            vm((width, hid)),
            vm((hid, width)),
            vm((rows, width), F32),
            vm((rows, width)),
            vm((rows, hid), F32),
            vm((rows, hid)),
            vm((rows, width), F32),
            vm((8, width), F32),
            vm((hid, width)),
            vm((width, hid)),
            sems((9,)),
        ],
        [SCALARS, ANY, ANY, SMALL, ANY, SMALL] + [ANY] * 5,
        [SMALL, ANY, ANY, SMALL],
        3_000_000_000,
        14_000_000,
    )
    xp0, xp1, xp2, xp3, enc_spread, enc_keep, enc_send = self_back(
        "enc_back", g_e1, enc_mix, enc_proj, enc_probs, enc_pair, enc_query, enc_a, enc_qkv
    )
    enc_in = enc_own.astype(F32)
    enc_in_part, enc_gain1_grad = top_norm_back(enc_in, enc_gain1, scatter_row([xp0, xp1, xp2, xp3]))
    encoder_grad = bring((g_e1 + enc_in_part).astype(BF))
    enc_rel_grad = jnp.dot(onehot.T, enc_spread.T, precision=lax.Precision.HIGHEST)

    def part_sum(small, index):
        return jnp.sum(small[8 * index : 8 * index + 8], axis=0)

    stat_terms = jnp.stack(
        [
            jnp.sum(enc_small[0:8]),
            jnp.sum(enc_small[8:16]),
            jnp.sum(enc_small[16:24]),
            jnp.sum(enc_small[24:32]),
            jnp.sum(dec_small[0:8]),
            jnp.sum(cross_small[0:8]),
            jnp.sum(cross_small[8:16]),
            jnp.sum(cross_small[16:24]),
        ]
    )
    small_members = [
        stat_terms,
        enc_gain1_grad,
        enc_rel_grad,
        part_sum(enc_gain_small, 1),
        part_sum(enc_gain_small, 0),
        dec_gain1_grad,
        dec_rel_grad,
        part_sum(gain2_small, 0),
        part_sum(cross_small, 3),
    ]
    flat = flatten_all(small_members)
    flat = jnp.pad(flat, (0, -flat.size % 1024)).reshape(-1, LANES)
    (
        stat_total,
        enc_gain1_sum,
        enc_rel_sum,
        enc_gain2_sum,
        enc_gainf_sum,
        dec_gain1_sum,
        dec_rel_sum,
        dec_gain2_sum,
        dec_gain3_sum,
    ) = unflatten(all_sum(flat).reshape(-1), small_members)

    def weights(keep, send, late, *shapes):
        total = reduce_blocks(keep, send, late)
        result, base = [], 0
        for shape in shapes:
            count = block_rows(shape, dp, seq)
            result.append(unblock(total[base : base + count], shape, dp, seq))
            base += count
        return result

    dec_wo_g, dec_wi_g = weights(ffn_keep, ffn_send, False, dec_wo.shape, dec_wi.shape)
    cross_proj_g, cross_q_g, cross_kv_g = weights(
        cross_keep, cross_send, True, cross_proj.shape, cross_q.shape, cross_kv.shape
    )
    dec_proj_g, dec_qkv_g = weights(dec_keep, dec_send, True, dec_proj.shape, dec_qkv.shape)
    enc_wo_g, enc_wi_g = weights(encffn_keep, encffn_send, False, enc_wo.shape, enc_wi.shape)
    enc_proj_g, enc_qkv_g = weights(enc_keep, enc_send, True, enc_proj.shape, enc_qkv.shape)

    token_total = float(rows * width * dp * seq)
    sublayer_rms = jnp.sqrt(stat_total / token_total)
    return (
        dec_output[None],
        encoder_grad[None],
        decoder_grad[None],
        sublayer_rms,
        enc_gain1_sum,
        enc_qkv_g,
        enc_proj_g,
        enc_rel_sum,
        enc_gain2_sum,
        enc_wi_g,
        enc_wo_g,
        enc_gainf_sum,
        dec_gain1_sum,
        dec_qkv_g,
        dec_proj_g,
        dec_rel_sum,
        dec_gain2_sum,
        cross_q_g,
        cross_kv_g,
        cross_proj_g,
        dec_gain3_sum,
        dec_wi_g,
        dec_wo_g,
    )


def solution(mesh):
    rows = P("dp", "seq", None)
    both = P("dp", "seq")
    return jax.shard_map(
        on_device,
        mesh=mesh,
        in_specs=(rows, rows, rows, P("dp", None)) + (P(),) * 20,
        out_specs=(
            (rows,) * 3
            + (P(),) * 2
            + (both,) * 2
            + (P(),) * 2
            + (both,) * 2
            + (P(),) * 2
            + (both,) * 2
            + (P(),) * 2
            + (both,) * 3
            + (P(),)
            + (both,) * 2
        ),
        check_vma=False,
    )
```

```python
import functools

import jax
import jax.numpy as jnp
from jax import lax
from jax.experimental import pallas as pl
from jax.experimental.pallas import tpu as pltpu
from jax.sharding import PartitionSpec as P

HEAD_DIM = 64
LANES = 128
BF = jnp.bfloat16
F32 = jnp.float32

eps_norm = 1e-06
negative = -1000000000.0
gelu_in = 0.7978845608028654
gelu_cube = 0.044715

ANY = pl.BlockSpec(memory_space=pltpu.HBM)
SMALL = pl.BlockSpec(memory_space=pltpu.VMEM)
SCALARS = pl.BlockSpec(memory_space=pltpu.SMEM)


def mm(left, right):
    return jnp.dot(left, right, preferred_element_type=F32)


def mm_nt(left, right):
    return lax.dot_general(left, right, (((1,), (1,)), ((), ())), preferred_element_type=F32)


def start(source, target, sem):
    copy = pltpu.make_async_copy(source, target, sem)
    copy.start()
    return copy


def rows_of(step, size):
    return pl.ds(pl.multiple_of(step * size, size), size)


def chunks(count, body, unroll=1):
    def step(i, carry):
        body(i)
        return carry

    lax.fori_loop(0, count, step, 0, unroll=unroll)


def inv_rms(values):
    return lax.rsqrt(jnp.mean(values * values, axis=-1, keepdims=True) + eps_norm)


def norm_into(source, gain, target, rows, chunk=64):
    def body(i):
        at = rows_of(i, chunk)
        v = source[at, :].astype(F32)
        target[at, :] = (v * inv_rms(v) * gain).astype(target.dtype)

    chunks(rows // chunk, body)


def norm_back_into(values, gain, incoming, residual, target, grad_sum, rows, chunk=32):
    grad_sum[...] = jnp.zeros_like(grad_sum)

    def body(i):
        at = rows_of(i, chunk)
        v = values[at, :]
        dy = incoming[at, :]
        r = inv_rms(v)
        hat = v * r
        part = dy * hat
        grad_sum[...] += jnp.sum(part.reshape(chunk // 8, 8, part.shape[-1]), axis=0)
        scaled = dy * gain
        mean = jnp.mean(scaled * hat, axis=-1, keepdims=True)
        out = r * (scaled - hat * mean)
        target[at, :] = out if residual is None else residual[at, :].astype(F32) + out

    chunks(rows // chunk, body)


def square_sum(values):
    rows, width = values.shape
    return jnp.sum((values * values).reshape(rows // 8, 8, width), axis=0)


def gelu_pair(u):
    sq = u * u
    t = jnp.tanh(gelu_in * u * (1.0 + gelu_cube * sq))
    half = 0.5 * (1.0 + t)
    slope = half + 0.5 * u * (1.0 - t * t) * (gelu_in * (1.0 + 3.0 * gelu_cube * sq))
    return u * half, slope


def place_ids(info, shape, axis, base):
    place = lax.broadcasted_iota(jnp.int32, shape, axis) + base
    ids = jnp.zeros(shape, jnp.int32)
    for slot in range(1, 5):
        ids = ids + (place >= info[slot]).astype(jnp.int32)
    return place, ids


def fill_mask(info, mask, causal):
    rows, keys = mask.shape
    first = info[0] * rows
    key_place, key_ids = place_ids(info, (1, keys), 1, 0)

    def body(i):
        place, ids = place_ids(info, (32, 1), 0, first + i * 32)
        allowed = ids == key_ids
        if causal:
            allowed = jnp.logical_and(allowed, key_place <= place)
        mask[rows_of(i, 32), :] = jnp.where(allowed, 0.0, negative)

    chunks(rows // 32, body)


def lane_split(pair):
    low = lax.broadcasted_iota(jnp.int32, pair.shape, 1) < HEAD_DIM
    zero = jnp.zeros_like(pair)
    return jnp.concatenate([jnp.where(low, pair, zero), jnp.where(low, zero, pair)], axis=0)


def lane_join(first, second):
    low = lax.broadcasted_iota(jnp.int32, first.shape, 1) < HEAD_DIM
    return jnp.where(low, first, second)


def attend_fwd(q, kv, table, mask, exps, exps_out, sem, scores, toeplitz, mix, inverse):
    rows, inner = q.shape
    keys = kv.shape[0]
    half = LANES
    low = lax.broadcasted_iota(jnp.int32, (1, LANES), 1) < HEAD_DIM
    for pair in range(inner // LANES):
        lanes = slice(pair * LANES, (pair + 1) * LANES)
        scores[...] = mm_nt(lane_split(q[:, lanes]), kv[:, lanes])
        for side in range(2):
            head = 2 * pair + side
            if table is not None:
                width = table.shape[1]
                row = jnp.broadcast_to(table[head : head + 1, :], (half, width))
                toeplitz[...] = pltpu.roll(row, width - half + 1, 1, stride=1, stride_axis=0)
            for block in range(rows // half):
                shift = half * (rows // half - 1 - block)

                def body(i, side=side, block=block, head=head, shift=shift):
                    at = rows_of(i, 32)
                    whole = pl.ds(pl.multiple_of(side * rows + block * half + i * 32, 32), 32)
                    mine = pl.ds(pl.multiple_of(block * half + i * 32, 32), 32)
                    s = scores[whole, :] + mask[mine, :]
                    if table is not None:
                        s = s + toeplitz[at, shift : shift + keys]
                    exps[head, mine, :] = jnp.exp(s - jnp.max(s, axis=-1, keepdims=True)).astype(BF)

                chunks(half // 32, body, half // 32)
        v_pair = kv[:, inner + pair * LANES : inner + (pair + 1) * LANES]
        one = jnp.ones_like(v_pair)
        first = mm(exps[2 * pair], jnp.where(low, v_pair, one))
        second = mm(exps[2 * pair + 1], jnp.where(low, one, v_pair))
        first_inv = 1.0 / first[:, HEAD_DIM : HEAD_DIM + 1]
        second_inv = 1.0 / second[:, 0:1]
        inv = jnp.where(low, first_inv, second_inv)
        inverse[:, lanes] = inv
        mix[:, lanes] = (lane_join(first, second) * inv).astype(BF)
        at = pl.ds(2 * pair, 2)
        start(exps.at[at], exps_out.at[at], sem)


def attend_back(q, kv, exps, scaled, mix, dq, dkv_t, scores, dscores, delta, skew, spread):
    rows, inner = q.shape
    keys = kv.shape[0]
    half = LANES
    count = keys // LANES
    for pair in range(inner // LANES):
        lanes = slice(pair * LANES, (pair + 1) * LANES)
        later = slice(inner + pair * LANES, inner + (pair + 1) * LANES)
        do_two = lane_split(scaled[:, lanes])
        scores[...] = mm_nt(do_two, kv[:, later])
        both = do_two.astype(F32) * jnp.concatenate([mix[:, lanes], mix[:, lanes]], axis=0).astype(F32)
        delta[...] = jnp.broadcast_to(jnp.sum(both, axis=-1, keepdims=True), delta.shape)
        for side in range(2):
            head = 2 * pair + side

            def body(i, side=side, head=head):
                at = rows_of(i, 32)
                spots = [
                    (
                        pl.ds(pl.multiple_of(side * rows + block * half + i * 32, 32), 32),
                        pl.ds(pl.multiple_of(block * half + i * 32, 32), 32),
                    )
                    for block in range(2)
                ]
                shifts = [delta[whole, :] for whole, _ in spots]
                before = None
                for k in range(count + 1):
                    cols = slice(k * LANES, (k + 1) * LANES)
                    made = []
                    if k < count:
                        for (whole, mine), shift in zip(spots, shifts):
                            ds = exps[head, mine, cols].astype(F32) * (scores[whole, cols] - shift)
                            dscores[whole, cols] = ds.astype(BF)
                            made.append(ds)
                    if skew is not None:
                        terms = made[1:] + ([] if before is None else [before])
                        skew[at, cols] = terms[0] if len(terms) == 1 else terms[0] + terms[1]
                        before = made[0] if made else None

            chunks(half // 32, body, half // 32)
            if skew is not None:
                width = spread.shape[1]
                wide = skew.shape[1]
                total = jnp.zeros((8, width), F32)
                for group in range(half // 8):
                    part = jnp.concatenate(
                        [skew[8 * group : 8 * group + 8, :], jnp.zeros((8, width - wide), F32)], axis=1
                    )
                    by = half - 8 - 8 * group
                    total = total + (pltpu.roll(part, by, 1) if by else part)
                left = 7 - lax.broadcasted_iota(jnp.int32, (8, width), 0)
                for bit in (1, 2, 4):
                    total = jnp.where((left & bit) != 0, pltpu.roll(total, bit, 1), total)
                spread[head : head + 1, :] = jnp.sum(total, axis=0, keepdims=True)
        k_pair = kv[:, lanes]
        dq[:, lanes] = lane_join(mm(dscores[0:rows, :], k_pair), mm(dscores[rows:, :], k_pair)).astype(BF)
        q_two = lane_split(q[:, lanes])
        dkv_t[lanes, :] = mm(q_two.T, dscores[...]).astype(BF)
        dv = mm(do_two[0:rows].T, exps[2 * pair]) + mm(do_two[rows:].T, exps[2 * pair + 1])
        dkv_t[later, :] = dv.astype(BF)


class Blocks:
    def __init__(self, info, keep, send, dp, seq):
        self.info, self.keep, self.send, self.dp, self.seq = info, keep, send, dp, seq

    def put(self, grad, base, sem):
        rows, cols = grad.shape
        tall, wide = rows // self.dp, cols // self.seq
        me, place = self.info[5], self.info[6]

        def body(j):
            for s in range(self.seq):
                for ch in range(wide // LANES):
                    col = pl.ds(pl.multiple_of((place ^ s) * wide + ch * LANES, LANES), LANES)
                    to = pl.ds(base + ch * tall, tall)
                    for target, flip_core in ((self.keep, 0), (self.send, 1)):
                        row = pl.ds(pl.multiple_of((me ^ (2 * j) ^ flip_core) * tall, tall), tall)
                        start(grad.at[row, col], target.at[j, s, to, :], sem)

        chunks(self.dp // 2, body)

    def wait(self, sem):
        for target in (self.keep, self.send):
            pltpu.make_async_copy(target, target, sem).wait()


def block_rows(shape, dp, seq):
    return shape[0] * shape[1] // (dp * seq * LANES)


def put_columns(blocks, grads, base, sem):
    rows = grads[0].shape[0]
    cols = grads[0].shape[1] + grads[1].shape[1]
    tall, wide = rows // blocks.dp, cols // blocks.seq
    per = wide // LANES
    me, place = blocks.info[5], blocks.info[6]

    def body(j):
        for chunk in range(cols // LANES):
            s = (chunk // per) ^ place
            to = pl.ds(base + (chunk % per) * tall, tall)
            first = chunk * LANES
            grad, col = (grads[0], first) if first < grads[0].shape[1] else (grads[1], first - grads[0].shape[1])
            for target, flip_core in ((blocks.keep, 0), (blocks.send, 1)):
                row = pl.ds(pl.multiple_of((me ^ (2 * j) ^ flip_core) * tall, tall), tall)
                start(grad.at[row, pl.ds(col, LANES)], target.at[j, s, to, :], sem)

    chunks(blocks.dp // 2, body)


def load_all(names, sems, base=0):
    return [start(src, dst, sems.at[base + j]) for j, (src, dst) in enumerate(names)]


def wait_all(copies):
    for copy in copies:
        copy.wait()


def self_fwd_kernel(causal, last, info, x0, x1, x2, x3, gain, w_qkv, w_proj, table, *rest):
    if last == "ffn":
        (gain2, w_in, w_out, gainf), rest = rest[:4], rest[4:]
        (a_out, kv_out, q_out, e_out, inv_out, o_out, h1_out, b_out, g_out, s_out, h2_out, fin_out, small), rest = rest[:13], rest[13:]
        (wq, wp, a, kv, q, exps, inv, scores, toeplitz, mask, mix, h1, normed, wi, wo, hidden, act, slope, h2, sems) = rest
    else:
        (gain2, w_in), rest = rest[:2], rest[2:]
        (a_out, kv_out, q_out, e_out, inv_out, o_out, h1_out, b_out, fin_out, small), rest = rest[:10], rest[10:]
        (wq, wp, a, kv, q, exps, inv, scores, toeplitz, mask, mix, h1, normed, wi, sems) = rest
    rows = h1.shape[0]
    inner = w_proj.shape[0]
    quarter = info[0]
    load_q = start(w_qkv, wq, sems.at[4])
    load_p = start(w_proj, wp, sems.at[5])
    load_i = start(w_in, wi, sems.at[6])
    if last == "ffn":
        load_o = start(w_out, wo, sems.at[7])
    fill_mask(info, mask, causal)
    for j, block in enumerate((x0, x1, x2, x3)):
        norm_into(block, gain[...], a.at[rows_of(quarter ^ j, rows)], rows)
    saves = [start(a, a_out, sems.at[8])]
    load_q.wait()
    q[...] = mm(a[rows_of(quarter, rows), :], wq[:, 0:inner]).astype(BF)

    def project(i):
        at = rows_of(i, rows)
        kv[at, :] = mm(a[at, :], wq[:, inner:]).astype(BF)

    chunks(4, project)
    saves += [start(kv, kv_out, sems.at[9]), start(q, q_out, sems.at[10])]
    attend_fwd(q, kv, table, mask, exps, e_out, sems.at[11], scores, toeplitz, mix, inv)
    saves.append(pltpu.make_async_copy(exps, e_out, sems.at[11]))
    saves += [start(mix, o_out, sems.at[12]), start(inv, inv_out, sems.at[18])]
    load_p.wait()
    att = mm(mix[...], wp[...])
    small[0:8, :] = square_sum(att)
    first = x0[...].astype(F32) + att
    h1[...] = first
    small[8:16, :] = square_sum(first)
    saves.append(start(h1, h1_out, sems.at[13]))
    norm_into(h1, gain2[...], normed, rows)
    saves.append(start(normed, b_out, sems.at[14]))
    load_i.wait()
    if last == "ffn":
        hidden[...] = mm(normed[...], wi[...])
        activate(hidden, act, slope)
        saves += [start(act, g_out, sems.at[15]), start(slope, s_out, sems.at[16])]
        load_o.wait()
        ffn = mm(act[...], wo[...])
        small[16:24, :] = square_sum(ffn)
        second = h1[...] + ffn
        h2[...] = second
        small[24:32, :] = square_sum(second)
        saves.append(start(h2, h2_out, sems.at[17]))
        norm_into(h2, gainf[...], fin_out, rows)
    else:
        fin_out[...] = mm(normed[...], wi[...]).astype(BF)
    wait_all(saves)


def activate(hidden, act, slope):
    def body(i):
        at = rows_of(i, 16)
        value, rate = gelu_pair(hidden[at, :])
        act[at, :] = value.astype(BF)
        slope[at, :] = rate.astype(BF)

    chunks(hidden.shape[0] // 16, body)


def ffn_back(blocks, base, top, act, slope, normed, wi, wo, hidden, du, back, grad_wo, grad_wi, sem):
    rows = top.shape[0]
    hidden[...] = mm_nt(top[...], wo[...])

    def slide(i):
        at = rows_of(i, 16)
        du[at, :] = (hidden[at, :] * slope[at, :].astype(F32)).astype(BF)

    chunks(rows // 16, slide)
    back[...] = mm_nt(du[...], wi[...])
    grad_wo[...] = mm(act[...].T, top[...]).astype(BF)
    blocks.put(grad_wo, base, sem)
    grad_wi[...] = mm(normed[...].T, du[...]).astype(BF)
    blocks.put(grad_wi, base + block_rows(grad_wo.shape, blocks.dp, blocks.seq), sem)


def cross_kernel(
    info, e0, e1, e2, e3, q_in, d1_in, top_in, w_kv, w_proj, gain, w_in, w_out,
    enc_out, kv_out, e_out, inv_out, o_out, out_out, g2_out, keep, send, small,
    enc, kv, q, exps, inv, scores, mask, mix, h, top, normed, wkv, wp, wi, wo, hidden, act, slope, du, back, gsum, grad_a, grad_b, grad_p, sems,
    dp, seq,
):
    rows = h.shape[0]
    quarter = info[0]
    load_kv = start(w_kv, wkv, sems.at[4])
    load_q = start(q_in, q, sems.at[5])
    load_p = start(w_proj, wp, sems.at[6])
    load_d = start(d1_in, h, sems.at[7])
    load_i = start(w_in, wi, sems.at[8])
    load_o = start(w_out, wo, sems.at[9])
    load_t = start(top_in, top, sems.at[10])
    fill_mask(info, mask, False)
    load_kv.wait()
    for j, block in enumerate((e0, e1, e2, e3)):
        at = rows_of(quarter ^ j, rows)
        enc[at, :] = block[...]
        kv[at, :] = mm(block[...], wkv[...]).astype(BF)
    saves = [start(enc, enc_out, sems.at[11]), start(kv, kv_out, sems.at[12])]
    load_q.wait()
    attend_fwd(q, kv, None, mask, exps, e_out, sems.at[13], scores, None, mix, inv)
    saves.append(pltpu.make_async_copy(exps, e_out, sems.at[13]))
    saves += [start(mix, o_out, sems.at[14]), start(inv, inv_out, sems.at[0])]
    load_p.wait()
    load_d.wait()
    att = mm(mix[...], wp[...])
    small[0:8, :] = square_sum(att)
    h[...] = h[...] + att
    norm_into(h, gain[...], normed, rows)
    load_i.wait()
    hidden[...] = mm(normed[...], wi[...])
    activate(hidden, act, slope)
    load_o.wait()
    ffn = mm(act[...], wo[...])
    small[8:16, :] = square_sum(ffn)
    third = h[...] + ffn
    small[16:24, :] = square_sum(third)
    out_out[...] = third.astype(BF)
    load_t.wait()
    blocks = Blocks(info, keep, send, dp, seq)
    ffn_back(blocks, 0, top, act, slope, normed, wi, wo, hidden, du, back, grad_a, grad_b, sems.at[15])
    norm_back_into(h, gain[...], back, top, g2_out, gsum, rows)
    small[24:32, :] = gsum[...]
    grad_p[...] = mm(mix[...].T, g2_out[...].astype(BF)).astype(BF)
    blocks.put(grad_p, block_rows(grad_a.shape, dp, seq) + block_rows(grad_b.shape, dp, seq), sems.at[15])
    wait_all(saves)
    blocks.wait(sems.at[15])


def enc_ffn_back_kernel(
    info, own, got, last, h2_in, gainf, h1_in, gain2, act_in, slope_in, normed_in, w_in, w_out, mix_in,
    g1_out, keep, send, small,
    up, h2, h1, act, slope, normed, wi, wo, mix, g2, top, hidden, du, back, gsum, grad_a, grad_b, grad_p, sems,
    dp, seq,
):
    rows = h1.shape[0]
    loads = load_all(
        ((h2_in, h2), (w_out, wo), (slope_in, slope), (act_in, act), (w_in, wi), (normed_in, normed), (h1_in, h1), (mix_in, mix)),
        sems,
    )
    up[...] = own[...] + got[...].astype(F32) + last[...].astype(F32)
    loads[0].wait()
    norm_back_into(h2, gainf[...], up, None, g2, gsum, rows)
    small[0:8, :] = gsum[...]
    top[...] = g2[...].astype(BF)
    wait_all(loads[1:])
    blocks = Blocks(info, keep, send, dp, seq)
    ffn_back(blocks, 0, top, act, slope, normed, wi, wo, hidden, du, back, grad_a, grad_b, sems.at[8])
    norm_back_into(h1, gain2[...], back, g2, g1_out, gsum, rows)
    small[8:16, :] = gsum[...]
    grad_p[...] = mm(mix[...].T, g1_out[...].astype(BF)).astype(BF)
    blocks.put(grad_p, block_rows(grad_a.shape, dp, seq) + block_rows(grad_b.shape, dp, seq), sems.at[8])
    blocks.wait(sems.at[8])


def attn_back_kernel(info, g_in, inv_in, o_in, w_proj, e_in, kv_in, q_in, *rest, kind):
    spread = skew = None
    if kind == "self":
        (dq, dkv, spread), rest = rest[:3], rest[3:]
        (g, inv, mix, wp, exps, kv, q, scaled, dkv_t, scores, dscores, delta, skew, sems) = rest
    else:
        (w_kv, p0, p1, p2, p3, dq, dkv), rest = rest[:7], rest[7:]
        (g, inv, mix, wp, exps, kv, q, wkv, scaled, dkv_t, scores, dscores, delta, wide, sems) = rest
    rows = g.shape[0]
    quarter = info[0]
    names = [(g_in, g), (w_proj, wp), (inv_in, inv), (o_in, mix), (q_in, q), (kv_in, kv), (e_in, exps)]
    if kind == "cross":
        names.append((w_kv, wkv))
    loads = load_all(names, sems)
    wait_all(loads[:3])
    scaled[...] = (mm_nt(g[...].astype(BF), wp[...]) * inv[...]).astype(BF)
    wait_all(loads[3:])
    attend_back(q, kv, exps, scaled, mix, dq, dkv_t, scores, dscores, delta, skew, spread)
    dkv[...] = dkv_t[...].T
    if kind == "cross":

        def project(i):
            at = rows_of(i, rows)
            wide[at, :] = mm_nt(dkv[at, :], wkv[...])

        chunks(4, project)
        p1[...] = wide[rows_of(quarter ^ 1, rows), :].astype(BF)
        p2[...] = wide[rows_of(quarter ^ 2, rows), :].astype(BF)
        p3[...] = wide[rows_of(quarter ^ 3, rows), :].astype(BF)
        p0[...] = wide[rows_of(quarter, rows), :]


def cross_weights_kernel(
    info, dq, dkv, enc_in, c_in, w_q, d1_in, gain, g2_in, mix_in,
    g1_out, keep, send, small,
    enc, c, wq, d1, g2, mix, part, gsum, grad_p, grad_q, grad_kv, sems,
    dp, seq,
):
    rows = d1.shape[0]
    loads = load_all(((w_q, wq), (d1_in, d1), (g2_in, g2), (c_in, c), (mix_in, mix), (enc_in, enc)), sems)
    loads[0].wait()
    part[...] = mm_nt(dq[...], wq[...])
    wait_all(loads[1:])
    norm_back_into(d1, gain[...], part, g2, g1_out, gsum, rows)
    small[...] = gsum[...]
    blocks = Blocks(info, keep, send, dp, seq)
    grad_p[...] = mm(mix[...].T, g1_out[...].astype(BF)).astype(BF)
    blocks.put(grad_p, 0, sems.at[6])
    base = block_rows(grad_p.shape, dp, seq)
    grad_q[...] = mm(c[...].T, dq[...]).astype(BF)
    blocks.put(grad_q, base, sems.at[6])
    grad_kv[...] = mm(enc[...].T, dkv[...]).astype(BF)
    blocks.put(grad_kv, base + block_rows(grad_q.shape, dp, seq), sems.at[6])
    blocks.wait(sems.at[6])


def self_weights_kernel(
    info, dq, dkv, a_in, w_qkv, gain,
    p0, p1, p2, p3, keep, send, small,
    a, wq, wide, grad_q, grad_kv, sems,
    dp, seq,
):
    rows, inner = dq.shape
    quarter = info[0]
    load_w = start(w_qkv, wq, sems.at[0])
    load_a = start(a_in, a, sems.at[1])
    load_w.wait()

    def project(i):
        at = rows_of(i, rows)
        wide[at, :] = mm_nt(dkv[at, :], wq[:, inner:])

    chunks(4, project)
    own = rows_of(quarter, rows)
    wide[own, :] = wide[own, :] + mm_nt(dq[...], wq[:, 0:inner])
    p2[...] = wide[rows_of(quarter ^ 2, rows), :].astype(BF)
    p3[...] = wide[rows_of(quarter ^ 3, rows), :].astype(BF)
    p1[...] = wide[rows_of(quarter ^ 1, rows), :].astype(BF)
    p0[...] = wide[own, :]
    load_a.wait()
    blocks = Blocks(info, keep, send, dp, seq)
    grad_q[...] = mm(a[own, :].T, dq[...]).astype(BF)
    grad_kv[...] = mm(a[...].T, dkv[...]).astype(BF)
    put_columns(blocks, (grad_q, grad_kv), 0, sems.at[2])
    small[...] = jnp.zeros_like(small)

    def gain_part(i):
        at = rows_of(i, 64)
        part = wide[at, :] * a[at, :].astype(F32)
        small[...] += jnp.sum(part.reshape(8, 8, part.shape[-1]), axis=0)

    chunks(4 * rows // 64, gain_part)
    small[...] = small[...] / gain[...]
    blocks.wait(sems.at[2])


def finish_kernel(own, got, last, x, gain, g, out, value, up, res, gsum):
    rows = x.shape[0]
    value[...] = x[...].astype(F32)
    up[...] = own[...] + got[...].astype(F32) + last[...].astype(F32)
    norm_back_into(value, gain[...], up, g, res, gsum, rows)
    out[...] = res[...].astype(BF)


def pack_kernel(enc_s, dec_s, cross_s, gains, rels, onehot, out):
    for i, (small, index) in enumerate(gains):
        line = jnp.sum(small[8 * index : 8 * index + 8, :], axis=0, keepdims=True)
        for k in range(line.shape[1] // LANES):
            out[4 * i + k : 4 * i + k + 1, :] = line[:, k * LANES : (k + 1) * LANES]
    base = 4 * len(gains)
    count = onehot.shape[0]
    lane = lax.broadcasted_iota(jnp.int32, (count, LANES), 1)
    line = lax.broadcasted_iota(jnp.int32, (count, LANES), 0)
    rest = jnp.zeros((count, LANES), F32)
    for i, spread in enumerate(rels):
        heads = spread.shape[0]
        rel = lax.dot_general(
            onehot[...], spread[...], (((1,), (1,)), ((), ())), precision=lax.Precision.HIGHEST, preferred_element_type=F32
        )
        rel = jnp.concatenate([rel, jnp.zeros((count, LANES - heads), F32)], axis=1)
        rest = rest + (pltpu.roll(rel, i * heads, 1) if i else rel)
    terms = [(enc_s, j) for j in range(4)] + [(dec_s, 0)] + [(cross_s, j) for j in range(3)]
    for k, (small, j) in enumerate(terms):
        rest = jnp.where(jnp.logical_and(line == k, lane == 2 * LANES // 4), 0.0, rest)
        value = jnp.sum(small[8 * j : 8 * j + 8, :])
        rest = jnp.where(jnp.logical_and(line == k, lane == LANES // 2), value, rest)
    out[base : base + count, :] = rest


def size_of(item):
    total = jnp.dtype(item.dtype).itemsize
    for n in item.shape:
        total *= n
    return total


def call(kernel, name, args, outs, scratch, specs, out_specs, flops, bytes_accessed):
    grant = 3 << 20
    for item in scratch:
        if hasattr(item, "shape") and item.memory_space == pltpu.VMEM:
            grant += size_of(item)
    for item, spec in list(zip(args, specs)) + list(zip(outs, out_specs)):
        if spec is SMALL:
            grant += size_of(item) + (32 << 10)
    args = [pltpu.with_memory_space_constraint(a, pltpu.HBM) if s is ANY else a for a, s in zip(args, specs)]
    outs = [pltpu.HBM(o.shape, o.dtype) if s is ANY else o for o, s in zip(outs, out_specs)]
    return pl.pallas_call(
        kernel,
        out_shape=outs,
        in_specs=specs,
        out_specs=out_specs,
        scratch_shapes=scratch,
        name=name,
        compiler_params=pltpu.CompilerParams(vmem_limit_bytes=grant),
        cost_estimate=pl.CostEstimate(flops=5 * flops, bytes_accessed=bytes_accessed, transcendentals=0),
    )(*args)


def sds(shape, dtype=BF):
    return jax.ShapeDtypeStruct(shape, dtype)


def vm(shape, dtype=BF):
    return pltpu.VMEM(shape, dtype)


def flip(value, axis, bit):
    count = lax.axis_size(axis)
    return lax.ppermute(value, axis, [(i, i ^ bit) for i in range(count)])


def swap_rows(value):
    dp, seq = lax.axis_size("dp"), lax.axis_size("seq")
    half = seq // 2
    pairs = []
    for d in range(dp):
        for s in range(seq):
            move = (d & 1) != (s >= half)
            pairs.append((d * seq + s, (d ^ 1) * seq + (s ^ half) if move else d * seq + s))
    return lax.ppermute(value, ("dp", "seq"), pairs)


def gather_row(own):
    other = flip(own, "seq", 1)
    core_own = flip(own, "dp", 1)
    core_other = flip(other, "dp", 1)
    return [own, other, core_own, core_other]


class Tree:
    def __init__(self, keep, send, shapes):
        self.dp, self.seq = lax.axis_size("dp"), lax.axis_size("seq")
        self.bits = self.dp.bit_length() - 2
        rows = keep.shape[2]
        unit = 16 if rows % 16 == 0 else 8
        half = rows // unit // 2 * unit
        spans = [(0, half), (half, rows)] if half else [(0, rows)]
        order = list(range(1, self.bits + 1))
        self.parts = [(span, o) for span, o in zip(spans, (order, order[::-1]))]
        self.rows, self.shapes = rows, shapes
        self.stage = 0
        self.left = [list(range(self.bits, 0, -1)) for _ in self.parts]
        self.lead = keep.shape[0] * keep.shape[1]
        self.keep = [keep.reshape(self.lead, rows, LANES)]
        self.recv = [flip(send, "dp", 1).reshape(self.lead, rows, LANES)]
        self.done = None

    def task(self):
        seq, stage = self.seq, self.stage
        if stage == self.bits + 1:
            ins = [self.keep[0]] + self.recv
            outs = [sds((s[0] // self.dp, s[1] // seq), F32) for s in self.shapes]

            def last(ins, outs):
                base = 0
                for out in outs:
                    tall = out.shape[0]
                    for ch in range(out.shape[1] // LANES):
                        at = slice(base, base + tall)
                        total = ins[0][at, :].astype(F32)
                        for more in ins[1:]:
                            total = total + more[at, :].astype(F32)
                        out[:, ch * LANES : (ch + 1) * LANES] = total
                        base += tall

            return ins, outs, last
        ins = self.keep + self.recv
        count = len(self.keep)
        plans = []
        outs = []
        for p, (span, order) in enumerate(self.parts):
            tall = span[1] - span[0]
            left = self.left[p]
            src = 0 if stage == 0 else p
            first = span[0] if stage == 0 else 0
            if stage < self.bits:
                pos = left.index(order[stage])
                lead = (1 << (len(left) - 1)) * seq
                plans.append((src, first, tall, len(left), pos, len(outs)))
                outs += [sds((lead, tall, LANES))] * 2
            else:
                plans.append((src, first, tall, 0, None, span[0]))
        if stage == self.bits:
            outs = [sds((self.rows, LANES))] * seq

        def body(ins, outs):
            for src, first, tall, n, pos, slot in plans:
                keep, recv = ins[src], ins[count + src]
                for m in range((1 << n) * seq):
                    at = slice(first, first + tall)
                    total = (keep[m, at, :].astype(F32) + recv[m, at, :].astype(F32)).astype(BF)
                    index, s = divmod(m, seq)
                    if pos is None:
                        outs[s][slot : slot + tall, :] = total
                    else:
                        low = n - 1 - pos
                        bit = (index >> low) & 1
                        index = ((index >> (low + 1)) << low) | (index & ((1 << low) - 1))
                        outs[slot + bit][index * seq + s] = total

        return ins, outs, body

    def accept(self, outs):
        if self.stage == self.bits + 1:
            self.done = outs
            return []
        if self.stage == self.bits:
            self.keep = [outs[0]]
            return list(outs[1:])
        self.keep = list(outs[0::2])
        return list(outs[1::2])

    def launch(self, sends):
        if self.stage == self.bits:
            self.recv = [flip(send, "seq", s + 1) for s, send in enumerate(sends)]
        elif self.stage < self.bits:
            self.recv = []
            for p, send in enumerate(sends):
                bit = self.parts[p][1][self.stage]
                self.left[p].remove(bit)
                self.recv.append(flip(send, "dp", 1 << bit))
        self.stage += 1


class SmallSum:
    def __init__(self, value):
        self.value = value
        self.bits = lax.axis_size("dp").bit_length() - 1
        self.seq = lax.axis_size("seq")
        self.stage = 0
        self.recv = [flip(value, "dp", 1)]
        self.done = None

    def task(self):
        def body(ins, outs):
            total = ins[0][...]
            for more in ins[1:]:
                total = total + more[...]
            outs[0][...] = total

        return [self.value] + self.recv, [sds(self.value.shape, F32)], body

    def accept(self, outs):
        self.value = outs[0]
        if self.stage == self.bits:
            self.done = outs[0]
            return []
        return [outs[0]]

    def launch(self, sends):
        self.stage += 1
        if sends:
            if self.stage < self.bits:
                self.recv = [flip(sends[0], "dp", 1 << self.stage)]
            else:
                self.recv = [flip(sends[0], "seq", s) for s in range(1, self.seq)]


class PairSum:
    def __init__(self, one, two):
        self.ins = [one, two]
        self.done = None

    def task(self):
        def body(ins, outs):
            outs[0][...] = (ins[0][...].astype(F32) + ins[1][...].astype(F32)).astype(BF)

        return self.ins, [sds(self.ins[0].shape)], body

    def accept(self, outs):
        self.done = outs[0]
        return [outs[0]]

    def launch(self, sends):
        self.recv = flip(sends[0], "seq", 1)


def advance(name, items, hold):
    items = [item for item in items if item.done is None]
    tasks = [item.task() for item in items]
    flat_in = [a for ins, _, _ in tasks for a in ins]
    flat_out = [o for _, outs, _ in tasks for o in outs]

    def kernel(*refs):
        ins, outs = refs[: len(flat_in)], refs[len(flat_in) :]
        for task_in, task_out, body in tasks:
            body(ins[: len(task_in)], outs[: len(task_out)])
            ins, outs = ins[len(task_in) :], outs[len(task_out) :]

    total = sum(size_of(a) for a in flat_in + flat_out)
    results = call(
        kernel, name, flat_in, flat_out, [], [SMALL] * len(flat_in), [SMALL] * len(flat_out), total // 4, total
    )
    sends = []
    for item, (_, outs, _) in zip(items, tasks):
        sends.append(item.accept(results[: len(outs)]))
        results = results[len(outs) :]
    hold, sends = lax.optimization_barrier((hold, sends))
    for item, send in zip(items, sends):
        item.launch(send)
    return hold


def on_device(
    encoder_input,
    decoder_input,
    output_grad,
    segment_lengths,
    bucket_table,
    enc_gain1,
    enc_qkv,
    enc_proj,
    enc_rel,
    enc_gain2,
    enc_wi,
    enc_wo,
    enc_gainf,
    dec_gain1,
    dec_qkv,
    dec_proj,
    dec_rel,
    dec_gain2,
    cross_q,
    cross_kv,
    cross_proj,
    dec_gain3,
    dec_wi,
    dec_wo,
):
    dp, seq = lax.axis_size("dp"), lax.axis_size("seq")
    _, rows, width = encoder_input.shape
    full = rows * seq
    inner = enc_proj.shape[0]
    heads = enc_rel.shape[1]
    hid = enc_wi.shape[1]
    bucket_count = enc_rel.shape[0]
    me, place = lax.axis_index("dp"), lax.axis_index("seq")
    core = me & 1
    quarter = (place & 1) + 2 * core
    first_pos = quarter * rows
    barrier = lax.optimization_barrier

    def row(vec):
        return vec.reshape(1, -1)

    lengths = swap_rows(segment_lengths)[0]
    enc_own = swap_rows(encoder_input[0])
    enc_own, dec_from = barrier((enc_own, decoder_input[0]))
    enc_blocks = gather_row(enc_own)
    dec_own = swap_rows(dec_from)

    end1 = lengths[0]
    end2 = end1 + lengths[1]
    end3 = end2 + lengths[2]
    end4 = end3 + lengths[3]
    info = jnp.stack([quarter, end1, end2, end3, end4, me, place, me]).astype(jnp.int32)
    span = full + rows
    window = lax.dynamic_slice_in_dim(jnp.pad(bucket_table, (0, 1)), full - first_pos - rows, span)
    onehot = (jnp.arange(bucket_count, dtype=jnp.int32)[:, None] == window[None, :]).astype(F32)

    def offsets_of(rel):
        return lax.dot_general(rel, onehot, (((0,), (0,)), ((), ())), precision=lax.Precision.HIGHEST)

    enc_table, dec_table = offsets_of(enc_rel), offsets_of(dec_rel)
    dec_own, top_from = barrier((dec_own, output_grad[0]))
    dec_blocks = gather_row(dec_own)

    exps_shape = (heads, rows, full)
    sems = pltpu.SemaphoreType.DMA
    act2, act1 = (rows, width), (rows, inner)

    attn_scratch = [
        vm((width, 3 * inner)),
        vm((inner, width)),
        vm((full, width)),
        vm((full, 2 * inner)),
        vm(act1),
        vm(exps_shape),
        vm(act1, F32),
        vm((2 * rows, full), F32),
        vm((LANES, full + rows), F32),
        vm((rows, full), F32),
        vm(act1),
        vm(act2, F32),
        vm(act2),
    ]
    attn_outs = [
        sds((full, width)),
        sds((full, 2 * inner)),
        sds(act1),
        sds(exps_shape),
        sds(act1, F32),
        sds(act1),
        sds(act2, F32),
        sds(act2),
    ]
    enc_a, enc_pair, enc_query, enc_exps, enc_inv, enc_mix, enc_h1, enc_b, enc_g, enc_s, enc_h2, encoded, enc_small = call(
        functools.partial(self_fwd_kernel, False, "ffn"),
        "enc_fwd",
        (info, *enc_blocks, row(enc_gain1), enc_qkv, enc_proj, enc_table, row(enc_gain2), enc_wi, enc_wo, row(enc_gainf)),
        attn_outs + [sds((rows, hid)), sds((rows, hid)), sds(act2, F32), sds(act2), sds((32, width), F32)],
        attn_scratch
        + [
            vm((width, hid)),
            vm((hid, width)),
            vm((rows, hid), F32),
            vm((rows, hid)),
            vm((rows, hid)),
            vm(act2, F32),
            sems((19,)),
        ],
        [SCALARS] + [SMALL] * 5 + [ANY, ANY, SMALL, SMALL, ANY, ANY, SMALL],
        [ANY] * 11 + [SMALL] * 2,
        6_000_000_000,
        20_000_000,
    )
    encoded, top_from = barrier((encoded, top_from))
    encoded_blocks = gather_row(encoded)
    top_low = swap_rows(top_from)

    dec_a, dec_pair, dec_query, dec_exps, dec_inv, dec_mix, dec_h1, dec_c, cross_query, dec_small = call(
        functools.partial(self_fwd_kernel, True, "query"),
        "dec_fwd",
        (info, *dec_blocks, row(dec_gain1), dec_qkv, dec_proj, dec_table, row(dec_gain2), cross_q),
        attn_outs + [sds(act1), sds((16, width), F32)],
        attn_scratch + [vm((width, inner)), sems((19,))],
        [SCALARS] + [SMALL] * 5 + [ANY, ANY, SMALL, SMALL, ANY],
        [ANY] * 8 + [SMALL] * 2,
        4_000_000_000,
        16_000_000,
    )

    def wide_blocks(*shapes):
        total = sum(block_rows(shape, dp, seq) for shape in shapes)
        return [sds((dp // 2, seq, total, LANES))] * 2

    ffn_shapes = ((hid, width), (width, hid), (inner, width))
    enc_all, cross_pair, cross_exps, cross_inv, cross_mix, dec_out, g_d2, keep, send, cross_small = call(
        functools.partial(cross_kernel, dp=dp, seq=seq),
        "cross_fwd",
        (info, *encoded_blocks, cross_query, dec_h1, top_low, cross_kv, cross_proj, row(dec_gain3), dec_wi, dec_wo),
        [
            sds((full, width)),
            sds((full, 2 * inner)),
            sds(exps_shape),
            sds(act1, F32),
            sds(act1),
            sds(act2),
            sds(act2, F32),
            *wide_blocks(*ffn_shapes),
            sds((32, width), F32),
        ],
        [
            vm((full, width)),
            vm((full, 2 * inner)),
            vm(act1),
            vm(exps_shape),
            vm(act1, F32),
            vm((2 * rows, full), F32),
            vm((rows, full), F32),
            vm(act1),
            vm(act2, F32),
            vm(act2),
            vm(act2),
            vm((width, 2 * inner)),
            vm((inner, width)),
            vm((width, hid)),
            vm((hid, width)),
            vm((rows, hid), F32),
            vm((rows, hid)),
            vm((rows, hid)),
            vm((rows, hid)),
            vm(act2, F32),
            vm((8, width), F32),
            vm((hid, width)),
            vm((width, hid)),
            vm((inner, width)),
            sems((16,)),
        ],
        [SCALARS] + [SMALL] * 4 + [ANY] * 5 + [SMALL, ANY, ANY],
        [ANY] * 5 + [SMALL] * 2 + [ANY] * 2 + [SMALL],
        7_000_000_000,
        30_000_000,
    )
    tree1 = Tree(keep, send, ffn_shapes)
    dec_output = swap_rows(dec_out)

    def back_scratch(kind):
        out = [
            vm(act2, F32),
            vm(act1, F32),
            vm(act1),
            vm((inner, width)),
            vm(exps_shape),
            vm((full, 2 * inner)),
            vm(act1),
        ]
        if kind == "cross":
            out += [vm((width, 2 * inner))]
        out += [
            vm(act1),
            vm((2 * inner, full)),
            vm((2 * rows, full), F32),
            vm((2 * rows, full)),
            vm((2 * rows, LANES), F32),
        ]
        out += [vm((LANES, full + LANES), F32)] if kind == "self" else [vm((full, width), F32)]
        return out + [sems((8,))]

    part_outs = [sds(act2, F32)] + [sds(act2)] * 3
    pair_outs = [sds(act1), sds((full, 2 * inner))]
    ep0, ep1, ep2, ep3, cross_dq, cross_dkv = call(
        functools.partial(attn_back_kernel, kind="cross"),
        "cross_back",
        (info, g_d2, cross_inv, cross_mix, cross_proj, cross_exps, cross_pair, cross_query, cross_kv),
        part_outs + pair_outs,
        back_scratch("cross"),
        [SCALARS] + [ANY] * 8,
        [SMALL] * 6,
        5_000_000_000,
        15_000_000,
    )
    enc_got = flip(ep2, "dp", 1)
    enc_theirs = PairSum(ep1, flip(ep3, "dp", 1))
    cross_dq, cross_dkv, dec_output = advance("sum_e", [enc_theirs], (cross_dq, cross_dkv, dec_output))

    cross_shapes = ((inner, width), (width, inner), (width, 2 * inner))
    g_d1, keep, send, gain2_small = call(
        functools.partial(cross_weights_kernel, dp=dp, seq=seq),
        "cross_weights",
        (info, cross_dq, cross_dkv, enc_all, dec_c, cross_q, dec_h1, row(dec_gain2), g_d2, dec_mix),
        [sds(act2, F32), *wide_blocks(*cross_shapes), sds((8, width), F32)],
        [
            vm((full, width)),
            vm(act2),
            vm((width, inner)),
            vm(act2, F32),
            vm(act2, F32),
            vm(act1),
            vm(act2, F32),
            vm((8, width), F32),
            vm((inner, width)),
            vm((width, inner)),
            vm((width, 2 * inner)),
            sems((7,)),
        ],
        [SCALARS, SMALL, SMALL] + [ANY] * 4 + [SMALL] + [ANY] * 2,
        [SMALL, ANY, ANY, SMALL],
        3_000_000_000,
        8_000_000,
    )
    tree2 = Tree(keep, send, cross_shapes)
    enc_last, ep0, g_d1 = advance("sum_1", [tree1], (enc_theirs.recv, ep0, g_d1))

    g_e1, keep, send, enc_gain_small = call(
        functools.partial(enc_ffn_back_kernel, dp=dp, seq=seq),
        "enc_ffn_back",
        (info, ep0, enc_got, enc_last, enc_h2, row(enc_gainf), enc_h1, row(enc_gain2), enc_g, enc_s, enc_b, enc_wi, enc_wo, enc_mix),
        [sds(act2, F32), *wide_blocks(*ffn_shapes), sds((16, width), F32)],
        [
            vm(act2, F32),
            vm(act2, F32),
            vm(act2, F32),
            vm((rows, hid)),
            vm((rows, hid)),
            vm(act2),
            vm((width, hid)),
            vm((hid, width)),
            vm(act1),
            vm(act2, F32),
            vm(act2),
            vm((rows, hid), F32),
            vm((rows, hid)),
            vm(act2, F32),
            vm((8, width), F32),
            vm((hid, width)),
            vm((width, hid)),
            vm((inner, width)),
            sems((9,)),
        ],
        [SCALARS] + [SMALL] * 3 + [ANY, SMALL, ANY, SMALL] + [ANY] * 6,
        [SMALL, ANY, ANY, SMALL],
        3_000_000_000,
        14_000_000,
    )
    tree4 = Tree(keep, send, ffn_shapes)
    g_e1 = advance("sum_2", [tree1, tree2], g_e1)

    def self_back(name, grad, inv, mix, proj, exps, pair, query):
        return call(
            functools.partial(attn_back_kernel, kind="self"),
            name,
            (info, grad, inv, mix, proj, exps, pair, query),
            pair_outs + [sds((heads, span), F32)],
            back_scratch("self"),
            [SCALARS] + [ANY] * 7,
            [SMALL] * 3,
            5_000_000_000,
            15_000_000,
        )

    def self_weights(name, dq, dkv, source, qkv, gain):
        return call(
            functools.partial(self_weights_kernel, dp=dp, seq=seq),
            name,
            (info, dq, dkv, source, qkv, row(gain)),
            part_outs + [*wide_blocks((width, 3 * inner)), sds((8, width), F32)],
            [
                vm((full, width)),
                vm((width, 3 * inner)),
                vm((full, width), F32),
                vm((width, inner)),
                vm((width, 2 * inner)),
                sems((3,)),
            ],
            [SCALARS, SMALL, SMALL, ANY, ANY, SMALL],
            [SMALL] * 4 + [ANY] * 2 + [SMALL],
            4_000_000_000,
            8_000_000,
        )

    qkv_shapes = ((width, 3 * inner),)
    enc_dq, enc_dkv, enc_spread = self_back("enc_back", g_e1, enc_inv, enc_mix, enc_proj, enc_exps, enc_pair, enc_query)
    enc_dq, enc_dkv, g_d1 = advance("sum_3", [tree1, tree2, tree4], (enc_dq, enc_dkv, g_d1))
    xp0, xp1, xp2, xp3, keep, send, enc_first_small = self_weights("enc_weights", enc_dq, enc_dkv, enc_a, enc_qkv, enc_gain1)
    tree5 = Tree(keep, send, qkv_shapes)
    enc_mine = flip(xp2, "dp", 1)
    enc_pass = PairSum(xp1, flip(xp3, "dp", 1))
    g_d1 = advance("sum_4", [enc_pass, tree1, tree2, tree4], g_d1)

    dec_dq, dec_dkv, dec_spread = self_back("dec_back", g_d1, dec_inv, dec_mix, dec_proj, dec_exps, dec_pair, dec_query)

    def finish(name, own, got, last, x, gain, g):
        return call(
            finish_kernel,
            name,
            (own, got, last, x, row(gain), g),
            [sds(act2)],
            [vm(act2, F32)] * 3 + [vm((8, width), F32)],
            [SMALL] * 6,
            [SMALL],
            2_000_000,
            2_000_000,
        )[0]

    dec_dq, dec_dkv = advance("sum_5", [tree2, tree4, tree5], (dec_dq, dec_dkv))
    dp0, dp1, dp2, dp3, keep, send, dec_first_small = self_weights("dec_weights", dec_dq, dec_dkv, dec_a, dec_qkv, dec_gain1)
    tree3 = Tree(keep, send, qkv_shapes)
    dec_mine = flip(dp2, "dp", 1)
    dec_pass = PairSum(dp1, flip(dp3, "dp", 1))
    gain_count = 6
    packed = call(
        lambda e, d, c, g0, g1, g2, g3, s0, s1, oh, out: pack_kernel(
            e, d, c, ((g0, 0), (g1, 1), (g1, 0), (g2, 0), (g3, 0), (c, 3)), (s0, s1), oh, out
        ),
        "pack",
        (enc_small, dec_small, cross_small, enc_first_small, enc_gain_small, dec_first_small, gain2_small, enc_spread, dec_spread, onehot),
        [sds((4 * gain_count + bucket_count, LANES), F32)],
        [],
        [SMALL] * 10,
        [SMALL],
        2_000_000,
        500_000,
    )[0]
    small = SmallSum(packed)
    encoder_grad = swap_rows(finish("enc_finish", xp0, enc_mine, enc_pass.recv, enc_own, enc_gain1, g_e1))
    items = [dec_pass, tree4, tree5]
    encoder_grad = advance("sum_6", items, encoder_grad)
    decoder_grad = None
    later = [item for item in (tree1, tree2, tree3, tree4, tree5, small) if item.done is None]
    step = 7
    while later:
        hold = advance(f"sum_{step}", later, (encoder_grad,))
        encoder_grad = hold[0]
        if decoder_grad is None:
            decoder_grad = swap_rows(finish("dec_finish", dp0, dec_mine, dec_pass.recv, dec_own, dec_gain1, g_d1))
        later = [item for item in later if item.done is None]
        step += 1

    sums = small.done

    def gain_of(i):
        return sums[4 * i : 4 * i + 4].reshape(-1)

    base = 4 * gain_count
    stats = sums[base : base + 8, LANES // 2]
    token_total = float(rows * width * dp * seq)
    sublayer_rms = jnp.sqrt(stats / token_total)
    dec_wo_g, dec_wi_g, cross_proj_g = tree1.done
    dec_proj_g, cross_q_g, cross_kv_g = tree2.done
    (dec_qkv_g,) = tree3.done
    enc_wo_g, enc_wi_g, enc_proj_g = tree4.done
    (enc_qkv_g,) = tree5.done
    return (
        dec_output[None],
        encoder_grad[None],
        decoder_grad[None],
        sublayer_rms,
        gain_of(0),
        enc_qkv_g,
        enc_proj_g,
        sums[base : base + bucket_count, 0:heads],
        gain_of(1),
        enc_wi_g,
        enc_wo_g,
        gain_of(2),
        gain_of(3),
        dec_qkv_g,
        dec_proj_g,
        sums[base : base + bucket_count, heads : 2 * heads],
        gain_of(4),
        cross_q_g,
        cross_kv_g,
        cross_proj_g,
        gain_of(5),
        dec_wi_g,
        dec_wo_g,
    )


def solution(mesh):
    rows = P("dp", "seq", None)
    both = P("dp", "seq")
    return jax.shard_map(
        on_device,
        mesh=mesh,
        in_specs=(rows, rows, rows, P("dp", None)) + (P(),) * 20,
        out_specs=(
            (rows,) * 3
            + (P(),) * 2
            + (both,) * 2
            + (P(),) * 2
            + (both,) * 2
            + (P(),) * 2
            + (both,) * 2
            + (P(),) * 2
            + (both,) * 3
            + (P(),)
            + (both,) * 2
        ),
        check_vma=False,
    )
```

```python
import functools

import jax
import jax.numpy as jnp
from jax import lax
from jax.experimental import pallas as pl
from jax.experimental.pallas import tpu as pltpu
from jax.sharding import PartitionSpec as P

HEAD_DIM = 64
LANES = 128
BF = jnp.bfloat16
F32 = jnp.float32

eps_norm = 1e-06
negative = -1000000000.0
gelu_in = 0.7978845608028654
gelu_cube = 0.044715

MICROSECOND = 1_150_000_000 * 2
ANY = pl.BlockSpec(memory_space=pltpu.HBM)
SMALL = pl.BlockSpec(memory_space=pltpu.VMEM)
SCALARS = pl.BlockSpec(memory_space=pltpu.SMEM)


def mm(left, right):
    return jnp.dot(left, right, preferred_element_type=F32)


def mm_nt(left, right):
    return lax.dot_general(left, right, (((1,), (1,)), ((), ())), preferred_element_type=F32)


def start(source, target, sem):
    copy = pltpu.make_async_copy(source, target, sem)
    copy.start()
    return copy


def rows_of(step, size):
    return pl.ds(pl.multiple_of(step * size, size), size)


def chunks(count, body, unroll=1):
    def step(i, carry):
        body(i)
        return carry

    lax.fori_loop(0, count, step, 0, unroll=unroll)


def inv_rms(values):
    return lax.rsqrt(jnp.mean(values * values, axis=-1, keepdims=True) + eps_norm)


def norm_into(source, gain, target, rows, chunk=64):
    def body(i):
        at = rows_of(i, chunk)
        v = source[at, :].astype(F32)
        target[at, :] = (v * inv_rms(v) * gain).astype(target.dtype)

    chunks(rows // chunk, body)


def norm_back_into(values, gain, incoming, residual, target, grad_sum, rows, chunk=32):
    grad_sum[...] = jnp.zeros_like(grad_sum)

    def body(i):
        at = rows_of(i, chunk)
        v = values[at, :]
        dy = incoming[at, :]
        r = inv_rms(v)
        hat = v * r
        part = dy * hat
        grad_sum[...] += jnp.sum(part.reshape(chunk // 8, 8, part.shape[-1]), axis=0)
        scaled = dy * gain
        mean = jnp.mean(scaled * hat, axis=-1, keepdims=True)
        out = r * (scaled - hat * mean)
        target[at, :] = out if residual is None else residual[at, :].astype(F32) + out

    chunks(rows // chunk, body)


def square_sum(values):
    rows, width = values.shape
    return jnp.sum((values * values).reshape(rows // 8, 8, width), axis=0)


def gelu_pair(u):
    sq = u * u
    t = jnp.tanh(gelu_in * u * (1.0 + gelu_cube * sq))
    half = 0.5 * (1.0 + t)
    slope = half + 0.5 * u * (1.0 - t * t) * (gelu_in * (1.0 + 3.0 * gelu_cube * sq))
    return u * half, slope


def place_ids(info, shape, axis, base):
    place = lax.broadcasted_iota(jnp.int32, shape, axis) + base
    ids = jnp.zeros(shape, jnp.int32)
    for slot in range(1, 5):
        ids = ids + (place >= info[slot]).astype(jnp.int32)
    return place, ids


def fill_mask(info, mask, causal):
    rows, keys = mask.shape
    first = info[0] * rows
    key_place, key_ids = place_ids(info, (1, keys), 1, 0)

    def body(i):
        place, ids = place_ids(info, (32, 1), 0, first + i * 32)
        allowed = ids == key_ids
        if causal:
            allowed = jnp.logical_and(allowed, key_place <= place)
        mask[rows_of(i, 32), :] = jnp.where(allowed, 0.0, negative)

    chunks(rows // 32, body)


def lane_split(pair):
    low = lax.broadcasted_iota(jnp.int32, pair.shape, 1) < HEAD_DIM
    zero = jnp.zeros_like(pair)
    return jnp.concatenate([jnp.where(low, pair, zero), jnp.where(low, zero, pair)], axis=0)


def lane_join(first, second):
    low = lax.broadcasted_iota(jnp.int32, first.shape, 1) < HEAD_DIM
    return jnp.where(low, first, second)


def attend_fwd(q, kv, table, mask, exps, exps_out, sem, scores, toeplitz, mix, inverse):
    rows, inner = q.shape
    keys = kv.shape[0]
    half = LANES
    low = lax.broadcasted_iota(jnp.int32, (1, LANES), 1) < HEAD_DIM
    for pair in range(inner // LANES):
        lanes = slice(pair * LANES, (pair + 1) * LANES)
        scores[...] = mm_nt(lane_split(q[:, lanes]), kv[:, lanes])
        for side in range(2):
            head = 2 * pair + side
            if table is not None:
                width = table.shape[1]
                row = jnp.broadcast_to(table[head : head + 1, :], (half, width))
                toeplitz[...] = pltpu.roll(row, width - half + 1, 1, stride=1, stride_axis=0)
            for block in range(rows // half):
                shift = half * (rows // half - 1 - block)

                def body(i, side=side, block=block, head=head, shift=shift):
                    at = rows_of(i, 32)
                    whole = pl.ds(pl.multiple_of(side * rows + block * half + i * 32, 32), 32)
                    mine = pl.ds(pl.multiple_of(block * half + i * 32, 32), 32)
                    s = scores[whole, :] + mask[mine, :]
                    if table is not None:
                        s = s + toeplitz[at, shift : shift + keys]
                    exps[head, mine, :] = jnp.exp(s - jnp.max(s, axis=-1, keepdims=True)).astype(BF)

                chunks(half // 32, body, half // 32)
        v_pair = kv[:, inner + pair * LANES : inner + (pair + 1) * LANES]
        one = jnp.ones_like(v_pair)
        first = mm(exps[2 * pair], jnp.where(low, v_pair, one))
        second = mm(exps[2 * pair + 1], jnp.where(low, one, v_pair))
        first_inv = 1.0 / first[:, HEAD_DIM : HEAD_DIM + 1]
        second_inv = 1.0 / second[:, 0:1]
        inv = jnp.where(low, first_inv, second_inv)
        inverse[:, lanes] = inv
        mix[:, lanes] = (lane_join(first, second) * inv).astype(BF)
        at = pl.ds(2 * pair, 2)
        start(exps.at[at], exps_out.at[at], sem)


def attend_back(q, kv, exps, scaled, mix, dq, dkv_t, scores, dscores, delta, skew, spread):
    rows, inner = q.shape
    keys = kv.shape[0]
    half = LANES
    count = keys // LANES
    for pair in range(inner // LANES):
        lanes = slice(pair * LANES, (pair + 1) * LANES)
        later = slice(inner + pair * LANES, inner + (pair + 1) * LANES)
        do_two = lane_split(scaled[:, lanes])
        scores[...] = mm_nt(do_two, kv[:, later])
        both = do_two.astype(F32) * jnp.concatenate([mix[:, lanes], mix[:, lanes]], axis=0).astype(F32)
        delta[...] = jnp.broadcast_to(jnp.sum(both, axis=-1, keepdims=True), delta.shape)
        for side in range(2):
            head = 2 * pair + side

            def body(i, side=side, head=head):
                at = rows_of(i, 32)
                spots = [
                    (
                        pl.ds(pl.multiple_of(side * rows + block * half + i * 32, 32), 32),
                        pl.ds(pl.multiple_of(block * half + i * 32, 32), 32),
                    )
                    for block in range(2)
                ]
                shifts = [delta[whole, :] for whole, _ in spots]
                before = None
                for k in range(count + 1):
                    cols = slice(k * LANES, (k + 1) * LANES)
                    made = []
                    if k < count:
                        for (whole, mine), shift in zip(spots, shifts):
                            ds = exps[head, mine, cols].astype(F32) * (scores[whole, cols] - shift)
                            dscores[whole, cols] = ds.astype(BF)
                            made.append(ds)
                    if skew is not None:
                        terms = made[1:] + ([] if before is None else [before])
                        skew[at, cols] = terms[0] if len(terms) == 1 else terms[0] + terms[1]
                        before = made[0] if made else None

            chunks(half // 32, body, half // 32)
            if skew is not None:
                width = spread.shape[1]
                wide = skew.shape[1]
                total = jnp.zeros((8, width), F32)
                for group in range(half // 8):
                    part = jnp.concatenate(
                        [skew[8 * group : 8 * group + 8, :], jnp.zeros((8, width - wide), F32)], axis=1
                    )
                    by = half - 8 - 8 * group
                    total = total + (pltpu.roll(part, by, 1) if by else part)
                left = 7 - lax.broadcasted_iota(jnp.int32, (8, width), 0)
                for bit in (1, 2, 4):
                    total = jnp.where((left & bit) != 0, pltpu.roll(total, bit, 1), total)
                spread[head : head + 1, :] = jnp.sum(total, axis=0, keepdims=True)
        k_pair = kv[:, lanes]
        dq[:, lanes] = lane_join(mm(dscores[0:rows, :], k_pair), mm(dscores[rows:, :], k_pair)).astype(BF)
        q_two = lane_split(q[:, lanes])
        dkv_t[lanes, :] = mm(q_two.T, dscores[...]).astype(BF)
        dv = mm(do_two[0:rows].T, exps[2 * pair]) + mm(do_two[rows:].T, exps[2 * pair + 1])
        dkv_t[later, :] = dv.astype(BF)


class Blocks:
    def __init__(self, info, keep, send, dp, seq):
        self.info, self.keep, self.send, self.dp, self.seq = info, keep, send, dp, seq

    def put(self, grad, base, sem):
        rows, cols = grad.shape
        tall, wide = rows // self.dp, cols // self.seq
        me, place = self.info[5], self.info[6]

        def body(j):
            for s in range(self.seq):
                for ch in range(wide // LANES):
                    col = pl.ds(pl.multiple_of((place ^ s) * wide + ch * LANES, LANES), LANES)
                    to = pl.ds(base + ch * tall, tall)
                    for target, flip_core in ((self.keep, 0), (self.send, 1)):
                        row = pl.ds(pl.multiple_of((me ^ (2 * j) ^ flip_core) * tall, tall), tall)
                        start(grad.at[row, col], target.at[j, s, to, :], sem)

        chunks(self.dp // 2, body)

    def wait(self, sem):
        for target in (self.keep, self.send):
            pltpu.make_async_copy(target, target, sem).wait()


def block_rows(shape, dp, seq):
    return shape[0] * shape[1] // (dp * seq * LANES)


def put_columns(blocks, grads, base, sem):
    rows = grads[0].shape[0]
    cols = grads[0].shape[1] + grads[1].shape[1]
    tall, wide = rows // blocks.dp, cols // blocks.seq
    per = wide // LANES
    me, place = blocks.info[5], blocks.info[6]

    def body(j):
        for chunk in range(cols // LANES):
            s = (chunk // per) ^ place
            to = pl.ds(base + (chunk % per) * tall, tall)
            first = chunk * LANES
            grad, col = (grads[0], first) if first < grads[0].shape[1] else (grads[1], first - grads[0].shape[1])
            for target, flip_core in ((blocks.keep, 0), (blocks.send, 1)):
                row = pl.ds(pl.multiple_of((me ^ (2 * j) ^ flip_core) * tall, tall), tall)
                start(grad.at[row, pl.ds(col, LANES)], target.at[j, s, to, :], sem)

    chunks(blocks.dp // 2, body)


def total_of(own, got, last, at, target):
    rows, width = own.shape
    for k in range(width // LANES):
        cols = slice(k * LANES, (k + 1) * LANES)
        target[:, cols] = (
            own[:, cols]
            + got[0:rows, cols].astype(F32)
            + last[at + k * rows : at + (k + 1) * rows, :].astype(F32)
        )


def load_all(names, sems, base=0):
    return [start(src, dst, sems.at[base + j]) for j, (src, dst) in enumerate(names)]


def wait_all(copies):
    for copy in copies:
        copy.wait()


def self_fwd_kernel(causal, last, info, x0, x1, x2, x3, gain, w_qkv, w_proj, table, *rest):
    if last == "ffn":
        (gain2, w_in, w_out, gainf), rest = rest[:4], rest[4:]
        (a_out, kv_out, q_out, e_out, inv_out, o_out, h1_out, b_out, g_out, s_out, h2_out, fin_out, small), rest = rest[:13], rest[13:]
        (wq, wp, a, kv, q, exps, inv, scores, toeplitz, mask, mix, h1, normed, wi, wo, hidden, act, slope, h2, sems) = rest
    else:
        (gain2, w_in), rest = rest[:2], rest[2:]
        (a_out, kv_out, q_out, e_out, inv_out, o_out, h1_out, b_out, fin_out, small), rest = rest[:10], rest[10:]
        (wq, wp, a, kv, q, exps, inv, scores, toeplitz, mask, mix, h1, normed, wi, sems) = rest
    rows = h1.shape[0]
    inner = w_proj.shape[0]
    quarter = info[0]
    load_q = start(w_qkv, wq, sems.at[4])
    load_p = start(w_proj, wp, sems.at[5])
    load_i = start(w_in, wi, sems.at[6])
    if last == "ffn":
        load_o = start(w_out, wo, sems.at[7])
    fill_mask(info, mask, causal)
    for j, block in enumerate((x0, x1, x2, x3)):
        norm_into(block, gain[...], a.at[rows_of(quarter ^ j, rows)], rows)
    saves = [start(a, a_out, sems.at[8])]
    load_q.wait()
    q[...] = mm(a[rows_of(quarter, rows), :], wq[:, 0:inner]).astype(BF)

    def project(i):
        at = rows_of(i, rows)
        kv[at, :] = mm(a[at, :], wq[:, inner:]).astype(BF)

    chunks(4, project)
    saves += [start(kv, kv_out, sems.at[9]), start(q, q_out, sems.at[10])]
    attend_fwd(q, kv, table, mask, exps, e_out, sems.at[11], scores, toeplitz, mix, inv)
    saves.append(pltpu.make_async_copy(exps, e_out, sems.at[11]))
    saves += [start(mix, o_out, sems.at[12]), start(inv, inv_out, sems.at[18])]
    load_p.wait()
    att = mm(mix[...], wp[...])
    small[0:8, :] = square_sum(att)
    first = x0[...].astype(F32) + att
    h1[...] = first
    small[8:16, :] = square_sum(first)
    saves.append(start(h1, h1_out, sems.at[13]))
    norm_into(h1, gain2[...], normed, rows)
    saves.append(start(normed, b_out, sems.at[14]))
    load_i.wait()
    if last == "ffn":
        hidden[...] = mm(normed[...], wi[...])
        activate(hidden, act, slope)
        saves += [start(act, g_out, sems.at[15]), start(slope, s_out, sems.at[16])]
        load_o.wait()
        ffn = mm(act[...], wo[...])
        small[16:24, :] = square_sum(ffn)
        second = h1[...] + ffn
        h2[...] = second
        small[24:32, :] = square_sum(second)
        saves.append(start(h2, h2_out, sems.at[17]))
        norm_into(h2, gainf[...], fin_out, rows)
    else:
        fin_out[...] = mm(normed[...], wi[...]).astype(BF)
    wait_all(saves)


def activate(hidden, act, slope):
    def body(i):
        at = rows_of(i, 16)
        value, rate = gelu_pair(hidden[at, :])
        act[at, :] = value.astype(BF)
        slope[at, :] = rate.astype(BF)

    chunks(hidden.shape[0] // 16, body)


def ffn_back(blocks, base, top, act, slope, normed, wi, wo, hidden, du, back, grad_wo, grad_wi, sem):
    rows = top.shape[0]
    hidden[...] = mm_nt(top[...], wo[...])

    def slide(i):
        at = rows_of(i, 16)
        du[at, :] = (hidden[at, :] * slope[at, :].astype(F32)).astype(BF)

    chunks(rows // 16, slide)
    back[...] = mm_nt(du[...], wi[...])
    grad_wo[...] = mm(act[...].T, top[...]).astype(BF)
    blocks.put(grad_wo, base, sem)
    grad_wi[...] = mm(normed[...].T, du[...]).astype(BF)
    blocks.put(grad_wi, base + block_rows(grad_wo.shape, blocks.dp, blocks.seq), sem)


def cross_kernel(
    info, e0, e1, e2, e3, q_in, d1_in, top_in, w_kv, w_proj, gain, w_in, w_out,
    enc_out, kv_out, e_out, inv_out, o_out, out_out, g2_out, keep, send, small,
    enc, kv, q, exps, inv, scores, mask, mix, h, top, normed, wkv, wp, wi, wo, hidden, act, slope, du, back, gsum, grad_a, grad_b, grad_p, sems,
    dp, seq,
):
    rows = h.shape[0]
    quarter = info[0]
    load_kv = start(w_kv, wkv, sems.at[4])
    load_q = start(q_in, q, sems.at[5])
    load_p = start(w_proj, wp, sems.at[6])
    load_d = start(d1_in, h, sems.at[7])
    load_i = start(w_in, wi, sems.at[8])
    load_o = start(w_out, wo, sems.at[9])
    load_t = start(top_in, top, sems.at[10])
    fill_mask(info, mask, False)
    load_kv.wait()
    for j, block in enumerate((e0, e1, e2, e3)):
        at = rows_of(quarter ^ j, rows)
        enc[at, :] = block[...]
        kv[at, :] = mm(block[...], wkv[...]).astype(BF)
    saves = [start(enc, enc_out, sems.at[11]), start(kv, kv_out, sems.at[12])]
    load_q.wait()
    attend_fwd(q, kv, None, mask, exps, e_out, sems.at[13], scores, None, mix, inv)
    saves.append(pltpu.make_async_copy(exps, e_out, sems.at[13]))
    saves += [start(mix, o_out, sems.at[14]), start(inv, inv_out, sems.at[0])]
    load_p.wait()
    load_d.wait()
    att = mm(mix[...], wp[...])
    small[0:8, :] = square_sum(att)
    h[...] = h[...] + att
    norm_into(h, gain[...], normed, rows)
    load_i.wait()
    hidden[...] = mm(normed[...], wi[...])
    activate(hidden, act, slope)
    load_o.wait()
    ffn = mm(act[...], wo[...])
    small[8:16, :] = square_sum(ffn)
    third = h[...] + ffn
    small[16:24, :] = square_sum(third)
    out_out[...] = third.astype(BF)
    load_t.wait()
    blocks = Blocks(info, keep, send, dp, seq)
    ffn_back(blocks, 0, top, act, slope, normed, wi, wo, hidden, du, back, grad_a, grad_b, sems.at[15])
    norm_back_into(h, gain[...], back, top, g2_out, gsum, rows)
    small[24:32, :] = gsum[...]
    grad_p[...] = mm(mix[...].T, g2_out[...].astype(BF)).astype(BF)
    blocks.put(grad_p, block_rows(grad_a.shape, dp, seq) + block_rows(grad_b.shape, dp, seq), sems.at[15])
    wait_all(saves)
    blocks.wait(sems.at[15])


def enc_ffn_back_kernel(
    info, own, got, last, h2_in, gainf, h1_in, gain2, act_in, slope_in, normed_in, w_in, w_out, mix_in,
    g1_out, keep, send, small,
    up, h2, h1, act, slope, normed, wi, wo, mix, g2, top, hidden, du, back, gsum, grad_a, grad_b, grad_p, sems,
    dp, seq, at,
):
    rows = h1.shape[0]
    loads = load_all(
        ((h2_in, h2), (w_out, wo), (slope_in, slope), (act_in, act), (w_in, wi), (normed_in, normed), (h1_in, h1), (mix_in, mix)),
        sems,
    )
    total_of(own, got, last, at, up)
    loads[0].wait()
    norm_back_into(h2, gainf[...], up, None, g2, gsum, rows)
    small[0:8, :] = gsum[...]
    top[...] = g2[...].astype(BF)
    wait_all(loads[1:])
    blocks = Blocks(info, keep, send, dp, seq)
    ffn_back(blocks, 0, top, act, slope, normed, wi, wo, hidden, du, back, grad_a, grad_b, sems.at[8])
    norm_back_into(h1, gain2[...], back, g2, g1_out, gsum, rows)
    small[8:16, :] = gsum[...]
    grad_p[...] = mm(mix[...].T, g1_out[...].astype(BF)).astype(BF)
    blocks.put(grad_p, block_rows(grad_a.shape, dp, seq) + block_rows(grad_b.shape, dp, seq), sems.at[8])
    blocks.wait(sems.at[8])


def attn_back_kernel(info, g_in, inv_in, o_in, w_proj, e_in, kv_in, q_in, w_kv, *rest, kind):
    spread = skew = None
    if kind == "self":
        (a_in, gain, p0, p1, p23, dq, dkv, spread, small), rest = rest[:9], rest[9:]
        (inv, mix, wp, exps, kv, q, wkv, scaled, dkv_t, scores, dscores, delta, wide, skew, a, sems) = rest
    else:
        (p0, p1, p23, dq, dkv), rest = rest[:5], rest[5:]
        (inv, mix, wp, exps, kv, q, wkv, scaled, dkv_t, scores, dscores, delta, wide, sems) = rest
    rows = g_in.shape[0]
    inner = dq.shape[1]
    quarter = info[0]
    names = [(w_proj, wp), (inv_in, inv), (o_in, mix), (q_in, q), (kv_in, kv), (e_in, exps), (w_kv, wkv)]
    if kind == "self":
        names.append((a_in, a))
    loads = load_all(names, sems)
    wait_all(loads[:2])
    scaled[...] = (mm_nt(g_in[...].astype(BF), wp[...]) * inv[...]).astype(BF)
    wait_all(loads[2:6])
    attend_back(q, kv, exps, scaled, mix, dq, dkv_t, scores, dscores, delta, skew, spread)
    dkv[...] = dkv_t[...].T
    wait_all(loads[6:])
    first = wkv.shape[1] - dkv.shape[1]

    def project(i):
        at = rows_of(i, rows)
        wide[at, :] = mm_nt(dkv[at, :], wkv[:, first:])

    chunks(4, project)
    own = rows_of(quarter, rows)
    if kind == "self":
        wide[own, :] = wide[own, :] + mm_nt(dq[...], wkv[:, 0:inner])
    p1[...] = wide[rows_of(quarter ^ 1, rows), :].astype(BF)
    p23[0:rows, :] = wide[rows_of(quarter ^ 2, rows), :].astype(BF)
    p23[rows:, :] = wide[rows_of(quarter ^ 3, rows), :].astype(BF)
    p0[...] = wide[own, :]
    if kind == "self":
        small[...] = jnp.zeros_like(small)

        def gain_part(i):
            at = rows_of(i, 64)
            part = wide[at, :] * a[at, :].astype(F32)
            small[...] += jnp.sum(part.reshape(8, 8, part.shape[-1]), axis=0)

        chunks(4 * rows // 64, gain_part)
        small[...] = small[...] / gain[...]


def cross_weights_kernel(
    info, dq, dkv, enc_in, c_in, w_q, d1_in, gain, g2_in, mix_in,
    g1_out, keep, send, small,
    enc, c, wq, d1, mix, part, gsum, grad_p, grad_q, grad_kv, sems,
    dp, seq,
):
    rows = d1.shape[0]
    loads = load_all(((w_q, wq), (d1_in, d1), (c_in, c), (mix_in, mix), (enc_in, enc)), sems)
    loads[0].wait()
    part[...] = mm_nt(dq[...], wq[...])
    wait_all(loads[1:])
    norm_back_into(d1, gain[...], part, g2_in, g1_out, gsum, rows)
    small[...] = gsum[...]
    blocks = Blocks(info, keep, send, dp, seq)
    grad_p[...] = mm(mix[...].T, g1_out[...].astype(BF)).astype(BF)
    blocks.put(grad_p, 0, sems.at[6])
    base = block_rows(grad_p.shape, dp, seq)
    grad_q[...] = mm(c[...].T, dq[...]).astype(BF)
    blocks.put(grad_q, base, sems.at[6])
    grad_kv[...] = mm(enc[...].T, dkv[...]).astype(BF)
    blocks.put(grad_kv, base + block_rows(grad_q.shape, dp, seq), sems.at[6])
    blocks.wait(sems.at[6])


def self_weights_kernel(info, dq, dkv, a_in, keep, send, a, grad_q, grad_kv, sems, dp, seq):
    rows = dq.shape[0]
    load_a = start(a_in, a, sems.at[0])
    load_a.wait()
    blocks = Blocks(info, keep, send, dp, seq)
    grad_q[...] = mm(a[rows_of(info[0], rows), :].T, dq[...]).astype(BF)
    grad_kv[...] = mm(a[...].T, dkv[...]).astype(BF)
    put_columns(blocks, (grad_q, grad_kv), 0, sems.at[1])
    blocks.wait(sems.at[1])


def finish_kernel(own, got, last, x, gain, g, out, value, up, res, gsum, at):
    rows = x.shape[0]
    value[...] = x[...].astype(F32)
    total_of(own, got, last, at, up)
    norm_back_into(value, gain[...], up, g, res, gsum, rows)
    out[...] = res[...].astype(BF)


def pack_kernel(enc_s, dec_s, cross_s, gains, rels, onehot, out):
    for i, (small, index) in enumerate(gains):
        line = jnp.sum(small[8 * index : 8 * index + 8, :], axis=0, keepdims=True)
        for k in range(line.shape[1] // LANES):
            out[4 * i + k : 4 * i + k + 1, :] = line[:, k * LANES : (k + 1) * LANES]
    base = 4 * len(gains)
    count = onehot.shape[0]
    lane = lax.broadcasted_iota(jnp.int32, (count, LANES), 1)
    line = lax.broadcasted_iota(jnp.int32, (count, LANES), 0)
    rest = jnp.zeros((count, LANES), F32)
    for i, spread in enumerate(rels):
        heads = spread.shape[0]
        rel = lax.dot_general(
            onehot[...], spread[...], (((1,), (1,)), ((), ())), precision=lax.Precision.HIGHEST, preferred_element_type=F32
        )
        rel = jnp.concatenate([rel, jnp.zeros((count, LANES - heads), F32)], axis=1)
        rest = rest + (pltpu.roll(rel, i * heads, 1) if i else rel)
    terms = [(enc_s, j) for j in range(4)] + [(dec_s, 0)] + [(cross_s, j) for j in range(3)]
    for k, (small, j) in enumerate(terms):
        rest = jnp.where(jnp.logical_and(line == k, lane == 2 * LANES // 4), 0.0, rest)
        value = jnp.sum(small[8 * j : 8 * j + 8, :])
        rest = jnp.where(jnp.logical_and(line == k, lane == LANES // 2), value, rest)
    out[base : base + count, :] = rest


def size_of(item):
    total = jnp.dtype(item.dtype).itemsize
    for n in item.shape:
        total *= n
    return total


def call(kernel, name, args, outs, scratch, specs, out_specs, flops, bytes_accessed):
    grant = 3 << 20
    for item in scratch:
        if hasattr(item, "shape") and item.memory_space == pltpu.VMEM:
            grant += size_of(item)
    for item, spec in list(zip(args, specs)) + list(zip(outs, out_specs)):
        if spec is SMALL:
            grant += size_of(item) + (32 << 10)
    args = [pltpu.with_memory_space_constraint(a, pltpu.HBM) if s is ANY else a for a, s in zip(args, specs)]
    outs = [pltpu.HBM(o.shape, o.dtype) if s is ANY else o for o, s in zip(outs, out_specs)]
    return pl.pallas_call(
        kernel,
        out_shape=outs,
        in_specs=specs,
        out_specs=out_specs,
        scratch_shapes=scratch,
        name=name,
        compiler_params=pltpu.CompilerParams(vmem_limit_bytes=grant),
        cost_estimate=pl.CostEstimate(flops=int(flops), bytes_accessed=bytes_accessed, transcendentals=0),
    )(*args)


def sds(shape, dtype=BF):
    return jax.ShapeDtypeStruct(shape, dtype)


def vm(shape, dtype=BF):
    return pltpu.VMEM(shape, dtype)


def flip(value, axis, bit):
    count = lax.axis_size(axis)
    return lax.ppermute(value, axis, [(i, i ^ bit) for i in range(count)])


def swap_rows(value, beside=0):
    dp, seq = lax.axis_size("dp"), lax.axis_size("seq")
    half = seq // 2
    pairs = []
    for d in range(dp):
        for s in range(seq):
            move = (d & 1) != (s >= half)
            to, place = (d ^ 1, s ^ half) if move else (d, s)
            pairs.append((d * seq + s, to * seq + (place ^ beside)))
    return lax.ppermute(value, ("dp", "seq"), pairs)


class Tree:
    def __init__(self, keep, send, shapes, short=False):
        self.dp, self.seq = lax.axis_size("dp"), lax.axis_size("seq")
        bits = self.dp.bit_length() - 2
        rows = keep.shape[2]
        axes = [("dp", 2 << b) for b in range(bits)]
        if short:
            orders = [axes, axes[::-1]]
            self.last = [("seq", k) for k in range(1, self.seq)]
        else:
            axes = axes + [("seq", 1)]
            turn = max(len(axes) // 3, 1)
            orders = [axes[p * turn :] + axes[: p * turn] for p in range(3)]
            self.last = [("seq", 2)]
        self.steps = len(axes)
        unit = 16 if rows % 16 == 0 else 8
        cuts = [rows // unit * p // len(orders) * unit for p in range(len(orders) + 1)]
        self.parts = [((a, b), order) for a, b, order in zip(cuts, cuts[1:], orders) if b > a]
        left = [("dp", 2 << b) for b in range(bits - 1, -1, -1)] + [("seq", 2), ("seq", 1)]
        self.left = [list(left) for _ in self.parts]
        self.rows, self.shapes = rows, shapes
        self.stage = 0
        self.keep = [(keep.reshape(-1, LANES), 0)]
        self.recv = [(flip(send, "dp", 1).reshape(-1, LANES), 0)]
        self.done = None

    def task(self):
        stage = self.stage
        ins = self.keep + self.recv
        if stage > self.steps:
            outs = [sds((s[0] // self.dp, s[1] // self.seq), F32) for s in self.shapes]

            def last(ins, outs, sends):
                base = 0
                for out in outs:
                    tall = out.shape[0]
                    for ch in range(out.shape[1] // LANES):
                        total = 0.0
                        for ref, at in ins:
                            total = total + ref[at + base : at + base + tall, :].astype(F32)
                        out[:, ch * LANES : (ch + 1) * LANES] = total
                        base += tall

            return ins, outs, [], last
        count = len(self.keep)
        plans, outs, sends = [], [], []
        for p, (span, order) in enumerate(self.parts):
            tall = span[1] - span[0]
            left = self.left[p]
            src, step, first = (0, self.rows, span[0]) if stage == 0 else (p, tall, 0)
            if stage < self.steps:
                lead = 1 << (len(left) - 1)
                plans.append((src, step, first, tall, len(left), left.index(order[stage]), p))
                outs.append(sds((lead * tall, LANES)))
                sends.append((order[stage], lead * tall))
            else:
                plans.append((src, step, first, tall, len(left), None, span[0]))
        if stage == self.steps:
            outs = [sds((self.rows, LANES))]
            sends = [(key, self.rows) for key in self.last]

        def body(ins, outs, sends):
            for src, step, first, tall, n, pos, slot in plans:
                (keep, at), (recv, at_recv) = ins[src], ins[count + src]
                for m in range(1 << n):
                    row = m * step + first
                    one = keep[at + row : at + row + tall, :].astype(F32)
                    two = recv[at_recv + row : at_recv + row + tall, :].astype(F32)
                    if pos is None:
                        to, base = (outs[0], 0) if m == 0 else sends[m - 1]
                        base += slot
                    else:
                        low = n - 1 - pos
                        index = ((m >> (low + 1)) << low) | (m & ((1 << low) - 1))
                        to, base = sends[slot] if (m >> low) & 1 else (outs[slot], 0)
                        base += index * tall
                    to[base : base + tall, :] = (one + two).astype(BF)

        return ins, outs, sends, body

    def accept(self, outs, recv):
        if self.stage > self.steps:
            self.done = outs
            return
        if self.stage < self.steps:
            for p, (_, order) in enumerate(self.parts):
                self.left[p].remove(order[self.stage])
        self.keep = [(out, 0) for out in outs]
        self.recv = recv
        self.stage += 1


class SmallSum:
    def __init__(self, value):
        self.value = value
        self.bits = lax.axis_size("dp").bit_length() - 1
        self.seq = lax.axis_size("seq")
        self.stage = 0
        self.recv = [(flip(value, "dp", 1), 0)]
        self.done = None

    def task(self):
        rows = self.value.shape[0]
        whole = self.stage == 0
        if self.stage == self.bits:
            keys = []
        elif self.stage + 1 < self.bits:
            keys = [("dp", 2 << self.stage)]
        else:
            keys = [("seq", s) for s in range(1, self.seq)]

        def body(ins, outs, sends):
            total = ins[0][0][...]
            for ref, at in ins[1:]:
                total = total + ref[at : at + rows, :].astype(F32)
                if not whole:
                    total = total + ref[at + rows : at + 2 * rows, :].astype(F32)
            outs[0][...] = total
            high = total.astype(BF)
            low = (total - high.astype(F32)).astype(BF)
            for ref, at in sends:
                ref[at : at + rows, :] = high
                ref[at + rows : at + 2 * rows, :] = low

        return [(self.value, 0)] + self.recv, [sds(self.value.shape, F32)], [(key, 2 * rows) for key in keys], body

    def accept(self, outs, recv):
        if self.stage == self.bits:
            self.done = outs[0]
            return
        self.value, self.recv = outs[0], recv
        self.stage += 1


class PairSum:
    def __init__(self, one, two, at):
        self.ins = [(one, 0), (two, at)]
        self.done = None

    def task(self):
        rows, width = self.ins[0][0].shape

        def body(ins, outs, sends):
            (one, _), (two, at) = ins
            ref, base = sends[0]
            for k in range(width // LANES):
                cols = slice(k * LANES, (k + 1) * LANES)
                total = one[:, cols].astype(F32) + two[at : at + rows, cols].astype(F32)
                ref[base + k * rows : base + (k + 1) * rows, :] = total.astype(BF)

        return self.ins, [], [(("seq", 1), rows * width // LANES)], body

    def accept(self, outs, recv):
        self.done = recv[0]


def advance(name, items, hold):
    items = [item for item in items if item.done is None]
    tasks = [item.task() for item in items]
    arrays, spots = [], []
    for ins, _, _, _ in tasks:
        mine = []
        for array, at in ins:
            known = [k for k, other in enumerate(arrays) if other is array]
            if not known:
                arrays.append(array)
            mine.append((known[0] if known else len(arrays) - 1, at))
        spots.append(mine)
    kept = [out for _, outs, _, _ in tasks for out in outs]
    sizes, slots = {}, []
    for _, _, sends, _ in tasks:
        mine = []
        for key, rows in sends:
            mine.append((key, sizes.get(key, 0)))
            sizes[key] = sizes.get(key, 0) + rows
        slots.append(mine)
    keys = sorted(sizes, key=lambda key: (key[0] != "seq", key[1]))
    mails = [sds((sizes[key], LANES)) for key in keys]

    def kernel(*refs):
        inputs, outs, mail = refs[: len(arrays)], refs[len(arrays) : len(arrays) + len(kept)], refs[len(arrays) + len(kept) :]
        for (_, task_outs, _, body), mine, to in zip(tasks, spots, slots):
            body(
                [(inputs[k], at) for k, at in mine],
                outs[: len(task_outs)],
                [(mail[keys.index(key)], at) for key, at in to],
            )
            outs = outs[len(task_outs) :]

    total = sum(size_of(a) for a in arrays + kept + mails)
    count = len(kept) + len(mails)
    results = call(kernel, name, arrays, kept + mails, [], [SMALL] * len(arrays), [SMALL] * count, total // 2_000_000 * MICROSECOND, total)
    outs, mail = list(results[: len(kept)]), list(results[len(kept) :])
    hold, mail = lax.optimization_barrier((hold, mail))
    got = {key: flip(array, *key) for key, array in zip(keys, mail)}
    for item, (_, task_outs, _, _), to in zip(items, tasks, slots):
        item.accept(outs[: len(task_outs)], [(got[key], at) for key, at in to])
        outs = outs[len(task_outs) :]
    return hold


def settle(items, hold):
    waiting = []
    for item in items:
        for array, _ in item.recv:
            if not any(array is other for other in waiting):
                waiting.append(array)
    hold, arrived = lax.optimization_barrier((hold, waiting))
    for item in items:
        item.recv = [
            (next(new for old, new in zip(waiting, arrived) if old is array), at) for array, at in item.recv
        ]
    return hold


def on_device(
    encoder_input,
    decoder_input,
    output_grad,
    segment_lengths,
    bucket_table,
    enc_gain1,
    enc_qkv,
    enc_proj,
    enc_rel,
    enc_gain2,
    enc_wi,
    enc_wo,
    enc_gainf,
    dec_gain1,
    dec_qkv,
    dec_proj,
    dec_rel,
    dec_gain2,
    cross_q,
    cross_kv,
    cross_proj,
    dec_gain3,
    dec_wi,
    dec_wo,
):
    dp, seq = lax.axis_size("dp"), lax.axis_size("seq")
    _, rows, width = encoder_input.shape
    full = rows * seq
    inner = enc_proj.shape[0]
    heads = enc_rel.shape[1]
    hid = enc_wi.shape[1]
    bucket_count = enc_rel.shape[0]
    me, place = lax.axis_index("dp"), lax.axis_index("seq")
    core = me & 1
    quarter = (place & 1) + 2 * core
    first_pos = quarter * rows
    barrier = lax.optimization_barrier

    def row(vec):
        return vec.reshape(1, -1)

    lengths = jnp.where(core == place // 2, segment_lengths, flip(segment_lengths, "dp", 1))[0]
    enc_own, enc_other = swap_rows(encoder_input[0]), swap_rows(encoder_input[0], 1)

    end1 = lengths[0]
    end2 = end1 + lengths[1]
    end3 = end2 + lengths[2]
    end4 = end3 + lengths[3]
    info = jnp.stack([quarter, end1, end2, end3, end4, me, place, me]).astype(jnp.int32)
    span = full + rows
    window = lax.dynamic_slice_in_dim(jnp.pad(bucket_table, (0, 1)), full - first_pos - rows, span)
    onehot = (jnp.arange(bucket_count, dtype=jnp.int32)[:, None] == window[None, :]).astype(F32)

    def offsets_of(rel):
        return lax.dot_general(rel, onehot, (((0,), (0,)), ((), ())), precision=lax.Precision.HIGHEST)

    enc_table, dec_table = offsets_of(enc_rel), offsets_of(dec_rel)
    enc_table, dec_table, dec_from, top_from = barrier((enc_table, dec_table, decoder_input[0], output_grad[0]))
    dec_top, dec_other = swap_rows(jnp.concatenate([dec_from, top_from])), swap_rows(dec_from, 1)
    enc_own, enc_other, info = barrier((enc_own, enc_other, info))
    enc_blocks = [enc_own, enc_other, flip(enc_own, "dp", 1), flip(enc_other, "dp", 1)]

    exps_shape = (heads, rows, full)
    sems = pltpu.SemaphoreType.DMA
    act2, act1 = (rows, width), (rows, inner)

    attn_scratch = [
        vm((width, 3 * inner)),
        vm((inner, width)),
        vm((full, width)),
        vm((full, 2 * inner)),
        vm(act1),
        vm(exps_shape),
        vm(act1, F32),
        vm((2 * rows, full), F32),
        vm((LANES, full + rows), F32),
        vm((rows, full), F32),
        vm(act1),
        vm(act2, F32),
        vm(act2),
    ]
    attn_outs = [
        sds((full, width)),
        sds((full, 2 * inner)),
        sds(act1),
        sds(exps_shape),
        sds(act1, F32),
        sds(act1),
        sds(act2, F32),
        sds(act2),
    ]
    enc_a, enc_pair, enc_query, enc_exps, enc_inv, enc_mix, enc_h1, enc_b, enc_g, enc_s, enc_h2, encoded, enc_small = call(
        functools.partial(self_fwd_kernel, False, "ffn"),
        "enc_fwd",
        (info, *enc_blocks, row(enc_gain1), enc_qkv, enc_proj, enc_table, row(enc_gain2), enc_wi, enc_wo, row(enc_gainf)),
        attn_outs + [sds((rows, hid)), sds((rows, hid)), sds(act2, F32), sds(act2), sds((32, width), F32)],
        attn_scratch
        + [
            vm((width, hid)),
            vm((hid, width)),
            vm((rows, hid), F32),
            vm((rows, hid)),
            vm((rows, hid)),
            vm(act2, F32),
            sems((19,)),
        ],
        [SCALARS] + [SMALL] * 5 + [ANY, ANY, SMALL, SMALL, ANY, ANY, SMALL],
        [ANY] * 11 + [SMALL] * 2,
        14.2 * MICROSECOND,
        20_000_000,
    )
    encoded, dec_top, dec_other = barrier((encoded, dec_top, dec_other))
    dec_own, top_low = dec_top[:rows], dec_top[rows:]
    dec_blocks = [dec_own, dec_other, flip(dec_own, "dp", 1), flip(dec_other, "dp", 1)]
    encoded_other = flip(encoded, "seq", 1)
    encoded_core = flip(encoded, "dp", 1)

    dec_a, dec_pair, dec_query, dec_exps, dec_inv, dec_mix, dec_h1, dec_c, cross_query, dec_small = call(
        functools.partial(self_fwd_kernel, True, "query"),
        "dec_fwd",
        (info, *dec_blocks, row(dec_gain1), dec_qkv, dec_proj, dec_table, row(dec_gain2), cross_q),
        attn_outs + [sds(act1), sds((16, width), F32)],
        attn_scratch + [vm((width, inner)), sems((19,))],
        [SCALARS] + [SMALL] * 5 + [ANY, ANY, SMALL, SMALL, ANY],
        [ANY] * 8 + [SMALL] * 2,
        11.3 * MICROSECOND,
        16_000_000,
    )

    encoded_other, cross_query = barrier((encoded_other, cross_query))
    encoded_blocks = [encoded, encoded_other, encoded_core, flip(encoded_other, "dp", 1)]

    def wide_blocks(*shapes):
        total = sum(block_rows(shape, dp, seq) for shape in shapes)
        return [sds((dp // 2, seq, total, LANES))] * 2

    ffn_shapes = ((hid, width), (width, hid), (inner, width))
    enc_all, cross_pair, cross_exps, cross_inv, cross_mix, dec_out, g_d2, keep, send, cross_small = call(
        functools.partial(cross_kernel, dp=dp, seq=seq),
        "cross_fwd",
        (info, *encoded_blocks, cross_query, dec_h1, top_low, cross_kv, cross_proj, row(dec_gain3), dec_wi, dec_wo),
        [
            sds((full, width)),
            sds((full, 2 * inner)),
            sds(exps_shape),
            sds(act1, F32),
            sds(act1),
            sds(act2),
            sds(act2, F32),
            *wide_blocks(*ffn_shapes),
            sds((32, width), F32),
        ],
        [
            vm((full, width)),
            vm((full, 2 * inner)),
            vm(act1),
            vm(exps_shape),
            vm(act1, F32),
            vm((2 * rows, full), F32),
            vm((rows, full), F32),
            vm(act1),
            vm(act2, F32),
            vm(act2),
            vm(act2),
            vm((width, 2 * inner)),
            vm((inner, width)),
            vm((width, hid)),
            vm((hid, width)),
            vm((rows, hid), F32),
            vm((rows, hid)),
            vm((rows, hid)),
            vm((rows, hid)),
            vm(act2, F32),
            vm((8, width), F32),
            vm((hid, width)),
            vm((width, hid)),
            vm((inner, width)),
            sems((16,)),
        ],
        [SCALARS] + [SMALL] * 4 + [ANY] * 5 + [SMALL, ANY, ANY],
        [ANY] * 5 + [SMALL] * 2 + [ANY] * 2 + [SMALL],
        17 * MICROSECOND,
        30_000_000,
    )
    tree1 = Tree(keep, send, ffn_shapes)

    def back_scratch(kind):
        out = [
            vm(act1, F32),
            vm(act1),
            vm((inner, width)),
            vm(exps_shape),
            vm((full, 2 * inner)),
            vm(act1),
        ]
        out += [
            vm((width, 2 * inner)) if kind == "cross" else vm((width, 3 * inner)),
            vm(act1),
            vm((2 * inner, full)),
            vm((2 * rows, full), F32),
            vm((2 * rows, full)),
            vm((2 * rows, LANES), F32),
            vm((full, width), F32),
        ]
        if kind == "self":
            out += [vm((LANES, full + LANES), F32), vm((full, width))]
        return out + [sems((8,))]

    part_outs = [sds(act2, F32), sds(act2), sds((2 * rows, width))]
    pair_outs = [sds(act1), sds((full, 2 * inner))]
    ep0, ep1, ep23, cross_dq, cross_dkv = call(
        functools.partial(attn_back_kernel, kind="cross"),
        "cross_back",
        (info, g_d2, cross_inv, cross_mix, cross_proj, cross_exps, cross_pair, cross_query, cross_kv),
        part_outs + pair_outs,
        back_scratch("cross"),
        [SCALARS, SMALL] + [ANY] * 7,
        [SMALL] * 5,
        10.2 * MICROSECOND,
        15_000_000,
    )
    enc_got = flip(ep23, "dp", 1)
    enc_pass = PairSum(ep1, enc_got, rows)
    cross_dq, cross_dkv = advance("sum_1", [enc_pass], (cross_dq, cross_dkv))

    cross_shapes = ((inner, width), (width, inner), (width, 2 * inner))
    g_d1, keep, send, gain2_small = call(
        functools.partial(cross_weights_kernel, dp=dp, seq=seq),
        "cross_weights",
        (info, cross_dq, cross_dkv, enc_all, dec_c, cross_q, dec_h1, row(dec_gain2), g_d2, dec_mix),
        [sds(act2, F32), *wide_blocks(*cross_shapes), sds((8, width), F32)],
        [
            vm((full, width)),
            vm(act2),
            vm((width, inner)),
            vm(act2, F32),
            vm(act1),
            vm(act2, F32),
            vm((8, width), F32),
            vm((inner, width)),
            vm((width, inner)),
            vm((width, 2 * inner)),
            sems((7,)),
        ],
        [SCALARS, SMALL, SMALL] + [ANY] * 4 + [SMALL, SMALL, ANY],
        [SMALL, ANY, ANY, SMALL],
        7 * MICROSECOND,
        8_000_000,
    )
    tree2 = Tree(keep, send, cross_shapes)
    enc_last, enc_last_at = enc_pass.done
    enc_last, ep0, g_d1, dec_out = advance("sum_2", [tree1], (enc_last, ep0, g_d1, dec_out))
    dec_output = swap_rows(dec_out)

    g_e1, keep, send, enc_gain_small = call(
        functools.partial(enc_ffn_back_kernel, dp=dp, seq=seq, at=enc_last_at),
        "enc_ffn_back",
        (info, ep0, enc_got, enc_last, enc_h2, row(enc_gainf), enc_h1, row(enc_gain2), enc_g, enc_s, enc_b, enc_wi, enc_wo, enc_mix),
        [sds(act2, F32), *wide_blocks(*ffn_shapes), sds((16, width), F32)],
        [
            vm(act2, F32),
            vm(act2, F32),
            vm(act2, F32),
            vm((rows, hid)),
            vm((rows, hid)),
            vm(act2),
            vm((width, hid)),
            vm((hid, width)),
            vm(act1),
            vm(act2, F32),
            vm(act2),
            vm((rows, hid), F32),
            vm((rows, hid)),
            vm(act2, F32),
            vm((8, width), F32),
            vm((hid, width)),
            vm((width, hid)),
            vm((inner, width)),
            sems((9,)),
        ],
        [SCALARS] + [SMALL] * 3 + [ANY, SMALL, ANY, SMALL] + [ANY] * 6,
        [SMALL, ANY, ANY, SMALL],
        9.9 * MICROSECOND,
        14_000_000,
    )
    tree4 = Tree(keep, send, ffn_shapes)
    g_e1 = advance("sum_3", [tree1, tree2], g_e1)

    def self_back(name, grad, inv, mix, proj, exps, pair, query, qkv, source, gain):
        return call(
            functools.partial(attn_back_kernel, kind="self"),
            name,
            (info, grad, inv, mix, proj, exps, pair, query, qkv, source, row(gain)),
            part_outs + pair_outs + [sds((heads, span), F32), sds((8, width), F32)],
            back_scratch("self"),
            [SCALARS, SMALL] + [ANY] * 8 + [SMALL],
            [SMALL] * 7,
            11 * MICROSECOND,
            15_000_000,
        )

    def self_weights(name, dq, dkv, source):
        return call(
            functools.partial(self_weights_kernel, dp=dp, seq=seq),
            name,
            (info, dq, dkv, source),
            wide_blocks((width, 3 * inner)),
            [vm((full, width)), vm((width, inner)), vm((width, 2 * inner)), sems((2,))],
            [SCALARS, SMALL, SMALL, ANY],
            [ANY] * 2,
            5 * MICROSECOND,
            8_000_000,
        )

    qkv_shapes = ((width, 3 * inner),)
    xp0, xp1, xp23, enc_dq, enc_dkv, enc_spread, enc_first_small = self_back(
        "enc_back", g_e1, enc_inv, enc_mix, enc_proj, enc_exps, enc_pair, enc_query, enc_qkv, enc_a, enc_gain1
    )
    enc_mine = flip(xp23, "dp", 1)
    enc_pass = PairSum(xp1, enc_mine, rows)
    enc_dq, enc_dkv, g_d1, dec_output = advance(
        "sum_4", [tree1, tree2, tree4], (enc_dq, enc_dkv, g_d1, dec_output)
    )
    dp0, dp1, dp23, dec_dq, dec_dkv, dec_spread, dec_first_small = self_back(
        "dec_back", g_d1, dec_inv, dec_mix, dec_proj, dec_exps, dec_pair, dec_query, dec_qkv, dec_a, dec_gain1
    )
    dec_mine = flip(dp23, "dp", 1)
    dec_pass = PairSum(dp1, dec_mine, rows)

    def finish(name, own, got, done, x, gain, g):
        last, at = done
        return call(
            functools.partial(finish_kernel, at=at),
            name,
            (own, got, last, x, row(gain), g),
            [sds(act2)],
            [vm(act2, F32)] * 3 + [vm((8, width), F32)],
            [SMALL] * 6,
            [SMALL],
            1.6 * MICROSECOND,
            2_000_000,
        )[0]

    gain_count = 6
    packed = call(
        lambda e, d, c, g0, g1, g2, g3, s0, s1, oh, out: pack_kernel(
            e, d, c, ((g0, 0), (g1, 1), (g1, 0), (g2, 0), (g3, 0), (c, 3)), (s0, s1), oh, out
        ),
        "pack",
        (enc_small, dec_small, cross_small, enc_first_small, enc_gain_small, dec_first_small, gain2_small, enc_spread, dec_spread, onehot),
        [sds((4 * gain_count + bucket_count, LANES), F32)],
        [],
        [SMALL] * 10,
        [SMALL],
        1 * MICROSECOND,
        500_000,
    )[0]
    enc_dq, dec_dq, packed = advance("sum_5", [enc_pass, tree1, tree2, tree4], (enc_dq, dec_dq, packed))
    small = SmallSum(packed)
    tree5 = Tree(*self_weights("enc_weights", enc_dq, enc_dkv, enc_a), qkv_shapes, True)
    dec_dq, xp0 = settle([tree1, tree2, tree4], (dec_dq, xp0))
    encoder_grad = swap_rows(finish("enc_finish", xp0, enc_mine, enc_pass.done, enc_own, enc_gain1, g_e1))
    tree3 = Tree(*self_weights("dec_weights", dec_dq, dec_dkv, dec_a), qkv_shapes, True)
    dp0, packed = advance("sum_6", [dec_pass, tree1, tree2, tree4, tree5, tree3, small], (dp0, packed))
    (packed,) = advance("sum_7", [tree1, tree2, tree4, tree5, tree3, small], (packed,))
    decoder_grad = swap_rows(finish("dec_finish", dp0, dec_mine, dec_pass.done, dec_own, dec_gain1, g_d1))
    step = 8
    while later := [item for item in (tree1, tree2, tree4, tree5, tree3, small) if item.done is None]:
        (packed,) = advance(f"sum_{step}", later, (packed,))
        step += 1

    sums = small.done

    def gain_of(i):
        return sums[4 * i : 4 * i + 4].reshape(-1)

    base = 4 * gain_count
    stats = sums[base : base + 8, LANES // 2]
    token_total = float(rows * width * dp * seq)
    sublayer_rms = jnp.sqrt(stats / token_total)
    dec_wo_g, dec_wi_g, cross_proj_g = tree1.done
    dec_proj_g, cross_q_g, cross_kv_g = tree2.done
    (dec_qkv_g,) = tree3.done
    enc_wo_g, enc_wi_g, enc_proj_g = tree4.done
    (enc_qkv_g,) = tree5.done
    return (
        dec_output[None],
        encoder_grad[None],
        decoder_grad[None],
        sublayer_rms,
        gain_of(0),
        enc_qkv_g,
        enc_proj_g,
        sums[base : base + bucket_count, 0:heads],
        gain_of(1),
        enc_wi_g,
        enc_wo_g,
        gain_of(2),
        gain_of(3),
        dec_qkv_g,
        dec_proj_g,
        sums[base : base + bucket_count, heads : 2 * heads],
        gain_of(4),
        cross_q_g,
        cross_kv_g,
        cross_proj_g,
        gain_of(5),
        dec_wi_g,
        dec_wo_g,
    )


def solution(mesh):
    rows = P("dp", "seq", None)
    both = P("dp", "seq")
    return jax.shard_map(
        on_device,
        mesh=mesh,
        in_specs=(rows, rows, rows, P("dp", None)) + (P(),) * 20,
        out_specs=(
            (rows,) * 3
            + (P(),) * 2
            + (both,) * 2
            + (P(),) * 2
            + (both,) * 2
            + (P(),) * 2
            + (both,) * 2
            + (P(),) * 2
            + (both,) * 3
            + (P(),)
            + (both,) * 2
        ),
        check_vma=False,
    )
```

```python
import functools

import jax
import jax.numpy as jnp
from jax import lax
from jax.experimental import pallas as pl
from jax.experimental.pallas import tpu as pltpu
from jax.sharding import PartitionSpec as P

HEAD_DIM = 64
LANES = 128
BF = jnp.bfloat16
F32 = jnp.float32

eps_norm = 1e-06
negative = -1000000000.0
gelu_in = 0.7978845608028654
gelu_cube = 0.044715

MICROSECOND = 1_150_000_000 * 2
ANY = pl.BlockSpec(memory_space=pltpu.HBM)
SMALL = pl.BlockSpec(memory_space=pltpu.VMEM)
KEPT = pl.BlockSpec(memory_space=pltpu.VMEM)
SCALARS = pl.BlockSpec(memory_space=pltpu.SMEM)


def mm(left, right):
    return jnp.dot(left, right, preferred_element_type=F32)


def mm_nt(left, right):
    return lax.dot_general(left, right, (((1,), (1,)), ((), ())), preferred_element_type=F32)


def start(source, target, sem):
    copy = pltpu.make_async_copy(source, target, sem)
    copy.start()
    return copy


def rows_of(step, size):
    return pl.ds(pl.multiple_of(step * size, size), size)


def chunks(count, body, unroll=1):
    def step(i, carry):
        body(i)
        return carry

    lax.fori_loop(0, count, step, 0, unroll=unroll)


def inv_rms(values):
    return lax.rsqrt(jnp.mean(values * values, axis=-1, keepdims=True) + eps_norm)


def norm_into(source, gain, target, rows, chunk=64):
    def body(i):
        at = rows_of(i, chunk)
        v = source[at, :].astype(F32)
        target[at, :] = (v * inv_rms(v) * gain).astype(target.dtype)

    chunks(rows // chunk, body, 2)


def norm_back_into(values, gain, incoming, residual, target, grad_sum, rows, chunk=32):
    grad_sum[...] = jnp.zeros_like(grad_sum)

    def body(i):
        at = rows_of(i, chunk)
        v = values[at, :]
        dy = incoming[at, :]
        r = inv_rms(v)
        hat = v * r
        part = dy * hat
        grad_sum[...] += jnp.sum(part.reshape(chunk // 8, 8, part.shape[-1]), axis=0)
        scaled = dy * gain
        mean = jnp.mean(scaled * hat, axis=-1, keepdims=True)
        out = r * (scaled - hat * mean)
        target[at, :] = out if residual is None else residual[at, :].astype(F32) + out

    chunks(rows // chunk, body, 4)


def square_sum(values):
    rows, width = values.shape
    return jnp.sum((values * values).reshape(rows // 8, 8, width), axis=0)


def gelu_pair(u):
    sq = u * u
    t = jnp.tanh(gelu_in * u * (1.0 + gelu_cube * sq))
    half = 0.5 * (1.0 + t)
    slope = half + 0.5 * u * (1.0 - t * t) * (gelu_in * (1.0 + 3.0 * gelu_cube * sq))
    return u * half, slope


def place_ids(info, shape, axis, base):
    place = lax.broadcasted_iota(jnp.int32, shape, axis) + base
    ids = jnp.zeros(shape, jnp.int32)
    for slot in range(1, 5):
        ids = ids + (place >= info[slot]).astype(jnp.int32)
    return place, ids


def fill_mask(info, mask, causal):
    rows, keys = mask.shape
    first = info[0] * rows
    key_place, key_ids = place_ids(info, (1, keys), 1, 0)

    def body(i):
        place, ids = place_ids(info, (32, 1), 0, first + i * 32)
        allowed = ids == key_ids
        if causal:
            allowed = jnp.logical_and(allowed, key_place <= place)
        mask[rows_of(i, 32), :] = jnp.where(allowed, 0.0, negative)

    chunks(rows // 32, body)


def lane_split(pair):
    low = lax.broadcasted_iota(jnp.int32, pair.shape, 1) < HEAD_DIM
    zero = jnp.zeros_like(pair)
    return jnp.concatenate([jnp.where(low, pair, zero), jnp.where(low, zero, pair)], axis=0)


def lane_join(first, second):
    low = lax.broadcasted_iota(jnp.int32, first.shape, 1) < HEAD_DIM
    return jnp.where(low, first, second)


def attend_fwd(q, kv, table, mask, exps, scores, toeplitz, mix, inverse):
    rows, inner = q.shape
    keys = kv.shape[0]
    half = LANES
    low = lax.broadcasted_iota(jnp.int32, (1, LANES), 1) < HEAD_DIM
    for pair in range(inner // LANES):
        lanes = slice(pair * LANES, (pair + 1) * LANES)
        scores[...] = mm_nt(lane_split(q[:, lanes]), kv[:, lanes])
        for side in range(2):
            head = 2 * pair + side
            if table is not None:
                width = table.shape[1]
                row = jnp.broadcast_to(table[head : head + 1, :], (half, width))
                toeplitz[...] = pltpu.roll(row, width - half + 1, 1, stride=1, stride_axis=0)
            for block in range(rows // half):
                shift = half * (rows // half - 1 - block)

                def body(i, side=side, block=block, head=head, shift=shift):
                    at = rows_of(i, 32)
                    whole = pl.ds(pl.multiple_of(side * rows + block * half + i * 32, 32), 32)
                    mine = pl.ds(pl.multiple_of(block * half + i * 32, 32), 32)
                    s = scores[whole, :] + mask[mine, :]
                    if table is not None:
                        s = s + toeplitz[at, shift : shift + keys]
                    exps[head, mine, :] = jnp.exp(s - jnp.max(s, axis=-1, keepdims=True)).astype(BF)

                chunks(half // 32, body, half // 32)
        v_pair = kv[:, inner + pair * LANES : inner + (pair + 1) * LANES]
        one = jnp.ones_like(v_pair)
        first = mm(exps[2 * pair], jnp.where(low, v_pair, one))
        second = mm(exps[2 * pair + 1], jnp.where(low, one, v_pair))
        first_inv = 1.0 / first[:, HEAD_DIM : HEAD_DIM + 1]
        second_inv = 1.0 / second[:, 0:1]
        inv = jnp.where(low, first_inv, second_inv)
        inverse[:, lanes] = inv
        mix[:, lanes] = (lane_join(first, second) * inv).astype(BF)


def attend_back(q, kv, exps, scaled, mix, dq, dkv_t, scores, dscores, delta, skew, spread):
    rows, inner = q.shape
    keys = kv.shape[0]
    half = LANES
    count = keys // LANES
    for pair in range(inner // LANES):
        lanes = slice(pair * LANES, (pair + 1) * LANES)
        later = slice(inner + pair * LANES, inner + (pair + 1) * LANES)
        do_two = lane_split(scaled[:, lanes])
        scores[...] = mm_nt(do_two, kv[:, later])
        both = do_two.astype(F32) * jnp.concatenate([mix[:, lanes], mix[:, lanes]], axis=0).astype(F32)
        delta[...] = jnp.broadcast_to(jnp.sum(both, axis=-1, keepdims=True), delta.shape)
        for side in range(2):
            head = 2 * pair + side

            def body(i, side=side, head=head):
                at = rows_of(i, 32)
                spots = [
                    (
                        pl.ds(pl.multiple_of(side * rows + block * half + i * 32, 32), 32),
                        pl.ds(pl.multiple_of(block * half + i * 32, 32), 32),
                    )
                    for block in range(2)
                ]
                shifts = [delta[whole, :] for whole, _ in spots]
                before = None
                for k in range(count + 1):
                    cols = slice(k * LANES, (k + 1) * LANES)
                    made = []
                    if k < count:
                        for (whole, mine), shift in zip(spots, shifts):
                            ds = exps[head, mine, cols].astype(F32) * (scores[whole, cols] - shift)
                            dscores[whole, cols] = ds.astype(BF)
                            made.append(ds)
                    if skew is not None:
                        terms = made[1:] + ([] if before is None else [before])
                        skew[at, cols] = terms[0] if len(terms) == 1 else terms[0] + terms[1]
                        before = made[0] if made else None

            chunks(half // 32, body, half // 32)
            if skew is not None:
                width = spread.shape[1]
                wide = skew.shape[1]
                total = jnp.zeros((8, width), F32)
                for group in range(half // 8):
                    part = jnp.concatenate(
                        [skew[8 * group : 8 * group + 8, :], jnp.zeros((8, width - wide), F32)], axis=1
                    )
                    by = half - 8 - 8 * group
                    total = total + (pltpu.roll(part, by, 1) if by else part)
                left = 7 - lax.broadcasted_iota(jnp.int32, (8, width), 0)
                for bit in (1, 2, 4):
                    total = jnp.where((left & bit) != 0, pltpu.roll(total, bit, 1), total)
                spread[head : head + 1, :] = jnp.sum(total, axis=0, keepdims=True)
        k_pair = kv[:, lanes]
        dq[:, lanes] = lane_join(mm(dscores[0:rows, :], k_pair), mm(dscores[rows:, :], k_pair)).astype(BF)
        q_two = lane_split(q[:, lanes])
        dkv_t[lanes, :] = mm(q_two.T, dscores[...]).astype(BF)
        dv = mm(do_two[0:rows].T, exps[2 * pair]) + mm(do_two[rows:].T, exps[2 * pair + 1])
        dkv_t[later, :] = dv.astype(BF)


class Blocks:
    def __init__(self, info, keep, send, dp, seq):
        self.info, self.keep, self.send, self.dp, self.seq = info, keep, send, dp, seq

    def put(self, grad, base, sem):
        rows, cols = grad.shape
        tall, wide = rows // self.dp, cols // self.seq
        me, place = self.info[5], self.info[6]

        def body(j):
            for s in range(self.seq):
                for ch in range(wide // LANES):
                    col = pl.ds(pl.multiple_of((place ^ s) * wide + ch * LANES, LANES), LANES)
                    to = pl.ds(base + ch * tall, tall)
                    for target, flip_core in ((self.keep, 0), (self.send, 1)):
                        row = pl.ds(pl.multiple_of((me ^ (2 * j) ^ flip_core) * tall, tall), tall)
                        start(grad.at[row, col], target.at[j, s, to, :], sem)

        chunks(self.dp // 2, body, self.dp // 2 if self.dp <= 8 else 1)

    def wait(self, sem):
        for target in (self.keep, self.send):
            pltpu.make_async_copy(target, target, sem).wait()


def block_rows(shape, dp, seq):
    return shape[0] * shape[1] // (dp * seq * LANES)


def put_columns(blocks, grads, base, sem):
    rows = grads[0].shape[0]
    cols = grads[0].shape[1] + grads[1].shape[1]
    tall, wide = rows // blocks.dp, cols // blocks.seq
    per = wide // LANES
    me, place = blocks.info[5], blocks.info[6]

    def body(j):
        for chunk in range(cols // LANES):
            s = (chunk // per) ^ place
            to = pl.ds(base + (chunk % per) * tall, tall)
            first = chunk * LANES
            grad, col = (grads[0], first) if first < grads[0].shape[1] else (grads[1], first - grads[0].shape[1])
            for target, flip_core in ((blocks.keep, 0), (blocks.send, 1)):
                row = pl.ds(pl.multiple_of((me ^ (2 * j) ^ flip_core) * tall, tall), tall)
                start(grad.at[row, pl.ds(col, LANES)], target.at[j, s, to, :], sem)

    chunks(blocks.dp // 2, body, blocks.dp // 2 if blocks.dp <= 8 else 1)


def total_of(own, got, last, at, target):
    rows, width = own.shape
    for k in range(width // LANES):
        cols = slice(k * LANES, (k + 1) * LANES)
        target[:, cols] = (
            own[:, cols]
            + got[0:rows, cols].astype(F32)
            + last[at + k * rows : at + (k + 1) * rows, :].astype(F32)
        )


def load_all(names, sems, base=0):
    return [start(src, dst, sems.at[base + j]) for j, (src, dst) in enumerate(names)]


def wait_all(copies):
    for copy in copies:
        copy.wait()


def self_fwd_kernel(causal, last, info, x0, x1, x2, x3, gain, w_qkv, w_proj, table, *rest):
    if last == "ffn":
        (gain2, w_in, w_out, gainf), rest = rest[:4], rest[4:]
        (a_out, kv, q_out, exps, inv_out, o_out, h1_out, b_out, g_out, s_out, h2_out, fin_out, small), rest = rest[:13], rest[13:]
        (wq, wp, a, q, inv, scores, toeplitz, mask, mix, h1, normed, wi, wo, hidden, act, slope, h2, sems) = rest
    else:
        (gain2, w_in), rest = rest[:2], rest[2:]
        (a_out, kv, q_out, exps, inv_out, o_out, h1_out, b_out, fin_out, small), rest = rest[:10], rest[10:]
        (wq, wp, a, q, inv, scores, toeplitz, mask, mix, h1, normed, wi, sems) = rest
    rows = h1.shape[0]
    inner = w_proj.shape[0]
    quarter = info[0]
    load_q = start(w_qkv, wq, sems.at[4])
    load_p = start(w_proj, wp, sems.at[5])
    load_i = start(w_in, wi, sems.at[6])
    if last == "ffn":
        load_o = start(w_out, wo, sems.at[7])
    fill_mask(info, mask, causal)
    for j, block in enumerate((x0, x1, x2, x3)):
        norm_into(block, gain[...], a.at[rows_of(quarter ^ j, rows)], rows)
    saves = [start(a, a_out, sems.at[8])]
    load_q.wait()
    q[...] = mm(a[rows_of(quarter, rows), :], wq[:, 0:inner]).astype(BF)

    def project(i):
        at = rows_of(i, rows)
        kv[at, :] = mm(a[at, :], wq[:, inner:]).astype(BF)

    chunks(4, project, 4)
    saves.append(start(q, q_out, sems.at[10]))
    attend_fwd(q, kv, table, mask, exps, scores, toeplitz, mix, inv)
    saves += [start(mix, o_out, sems.at[12]), start(inv, inv_out, sems.at[18])]
    load_p.wait()
    att = mm(mix[...], wp[...])
    small[0:8, :] = square_sum(att)
    first = x0[...].astype(F32) + att
    h1[...] = first
    small[8:16, :] = square_sum(first)
    saves.append(start(h1, h1_out, sems.at[13]))
    norm_into(h1, gain2[...], normed, rows)
    saves.append(start(normed, b_out, sems.at[14]))
    load_i.wait()
    if last == "ffn":
        hidden[...] = mm(normed[...], wi[...])
        activate(hidden, act, slope)
        saves += [start(act, g_out, sems.at[15]), start(slope, s_out, sems.at[16])]
        load_o.wait()
        ffn = mm(act[...], wo[...])
        small[16:24, :] = square_sum(ffn)
        second = h1[...] + ffn
        h2[...] = second
        small[24:32, :] = square_sum(second)
        saves.append(start(h2, h2_out, sems.at[17]))
        norm_into(h2, gainf[...], fin_out, rows)
    else:
        fin_out[...] = mm(normed[...], wi[...]).astype(BF)
    wait_all(saves)


def activate(hidden, act, slope):
    def body(i):
        at = rows_of(i, 16)
        value, rate = gelu_pair(hidden[at, :])
        act[at, :] = value.astype(BF)
        slope[at, :] = rate.astype(BF)

    chunks(hidden.shape[0] // 16, body, 16)


def ffn_back(blocks, base, top, act, slope, normed, wi, wo, hidden, du, back, grad_wo, grad_wi, sem, loads=()):
    rows = top.shape[0]
    wait_all(loads[:1])
    hidden[...] = mm_nt(top[...], wo[...])
    wait_all(loads[1:3])
    grad_wo[...] = mm(act[...].T, top[...]).astype(BF)
    blocks.put(grad_wo, base, sem)

    def slide(i):
        at = rows_of(i, 16)
        du[at, :] = (hidden[at, :] * slope[at, :].astype(F32)).astype(BF)

    chunks(rows // 16, slide, 16)
    wait_all(loads[3:])
    grad_wi[...] = mm(normed[...].T, du[...]).astype(BF)
    blocks.put(grad_wi, base + block_rows(grad_wo.shape, blocks.dp, blocks.seq), sem)
    back[...] = mm_nt(du[...], wi[...])


def cross_kernel(
    info, e0, e1, e2, e3, q_in, d1_in, top_in, w_kv, w_proj, gain, w_in, w_out,
    enc_out, kv, exps, inv_out, o_out, out_out, g2_out, keep, send, small,
    enc, q, inv, scores, mask, mix, h, top, normed, wkv, wp, wi, wo, hidden, act, slope, du, back, gsum, grad_a, grad_b, grad_p, sems,
    dp, seq,
):
    rows = h.shape[0]
    quarter = info[0]
    load_kv = start(w_kv, wkv, sems.at[4])
    load_q = start(q_in, q, sems.at[5])
    load_p = start(w_proj, wp, sems.at[6])
    load_d = start(d1_in, h, sems.at[7])
    load_i = start(w_in, wi, sems.at[8])
    load_o = start(w_out, wo, sems.at[9])
    load_t = start(top_in, top, sems.at[10])
    fill_mask(info, mask, False)
    load_kv.wait()
    for j, block in enumerate((e0, e1, e2, e3)):
        at = rows_of(quarter ^ j, rows)
        enc[at, :] = block[...]
        kv[at, :] = mm(block[...], wkv[...]).astype(BF)
    saves = [start(enc, enc_out, sems.at[11])]
    load_q.wait()
    attend_fwd(q, kv, None, mask, exps, scores, None, mix, inv)
    saves += [start(mix, o_out, sems.at[14]), start(inv, inv_out, sems.at[0])]
    load_p.wait()
    load_d.wait()
    att = mm(mix[...], wp[...])
    small[0:8, :] = square_sum(att)
    h[...] = h[...] + att
    norm_into(h, gain[...], normed, rows)
    load_i.wait()
    hidden[...] = mm(normed[...], wi[...])
    activate(hidden, act, slope)
    load_o.wait()
    ffn = mm(act[...], wo[...])
    small[8:16, :] = square_sum(ffn)
    third = h[...] + ffn
    small[16:24, :] = square_sum(third)
    out_out[...] = third.astype(BF)
    load_t.wait()
    blocks = Blocks(info, keep, send, dp, seq)
    ffn_back(blocks, 0, top, act, slope, normed, wi, wo, hidden, du, back, grad_a, grad_b, sems.at[15])
    norm_back_into(h, gain[...], back, top, g2_out, gsum, rows)
    small[24:32, :] = gsum[...]
    grad_p[...] = mm(mix[...].T, g2_out[...].astype(BF)).astype(BF)
    blocks.put(grad_p, block_rows(grad_a.shape, dp, seq) + block_rows(grad_b.shape, dp, seq), sems.at[15])
    wait_all(saves)
    blocks.wait(sems.at[15])


def enc_ffn_back_kernel(
    info, own, got, last, h2_in, gainf, h1_in, gain2, act_in, slope_in, normed_in, w_in, w_out, mix_in,
    g1_out, keep, send, small,
    up, h2, h1, act, slope, normed, wi, wo, mix, g2, top, hidden, du, back, gsum, grad_a, grad_b, grad_p, sems,
    dp, seq, at,
):
    rows = h1.shape[0]
    loads = load_all(
        ((h2_in, h2), (w_out, wo), (slope_in, slope), (act_in, act), (w_in, wi), (normed_in, normed), (h1_in, h1), (mix_in, mix)),
        sems,
    )
    total_of(own, got, last, at, up)
    loads[0].wait()
    norm_back_into(h2, gainf[...], up, None, g2, gsum, rows)
    small[0:8, :] = gsum[...]
    top[...] = g2[...].astype(BF)
    blocks = Blocks(info, keep, send, dp, seq)
    ffn_back(blocks, 0, top, act, slope, normed, wi, wo, hidden, du, back, grad_a, grad_b, sems.at[8], loads[1:6])
    wait_all(loads[6:])
    norm_back_into(h1, gain2[...], back, g2, g1_out, gsum, rows)
    small[8:16, :] = gsum[...]
    grad_p[...] = mm(mix[...].T, g1_out[...].astype(BF)).astype(BF)
    blocks.put(grad_p, block_rows(grad_a.shape, dp, seq) + block_rows(grad_b.shape, dp, seq), sems.at[8])
    blocks.wait(sems.at[8])


def attn_back_kernel(info, g_in, inv_in, o_in, w_proj, exps, kv, q_in, w_kv, *rest, kind):
    spread = skew = None
    if kind == "self":
        (a_in, gain, p0, p1, p23, dq, dkv, spread, small), rest = rest[:9], rest[9:]
        (inv, mix, wp, q, wkv, scaled, dkv_t, scores, dscores, delta, wide, skew, a, sems) = rest
    else:
        (p0, p1, p23, dq, dkv), rest = rest[:5], rest[5:]
        (inv, mix, wp, q, wkv, scaled, dkv_t, scores, dscores, delta, wide, sems) = rest
    rows = g_in.shape[0]
    inner = dq.shape[1]
    quarter = info[0]
    names = [(w_proj, wp), (inv_in, inv), (o_in, mix), (q_in, q), (w_kv, wkv)]
    if kind == "self":
        names.append((a_in, a))
    loads = load_all(names, sems)
    wait_all(loads[:2])
    scaled[...] = (mm_nt(g_in[...].astype(BF), wp[...]) * inv[...]).astype(BF)
    wait_all(loads[2:4])
    attend_back(q, kv, exps, scaled, mix, dq, dkv_t, scores, dscores, delta, skew, spread)
    dkv[...] = dkv_t[...].T
    wait_all(loads[4:])
    first = wkv.shape[1] - dkv.shape[1]

    def project(i):
        at = rows_of(i, rows)
        wide[at, :] = mm_nt(dkv[at, :], wkv[:, first:])

    chunks(4, project, 4)
    own = rows_of(quarter, rows)
    if kind == "self":
        wide[own, :] = wide[own, :] + mm_nt(dq[...], wkv[:, 0:inner])
    p1[...] = wide[rows_of(quarter ^ 1, rows), :].astype(BF)
    p23[0:rows, :] = wide[rows_of(quarter ^ 2, rows), :].astype(BF)
    p23[rows:, :] = wide[rows_of(quarter ^ 3, rows), :].astype(BF)
    p0[...] = wide[own, :]
    if kind == "self":
        small[...] = jnp.zeros_like(small)

        def gain_part(i):
            at = rows_of(i, 64)
            part = wide[at, :] * a[at, :].astype(F32)
            small[...] += jnp.sum(part.reshape(8, 8, part.shape[-1]), axis=0)

        chunks(4 * rows // 64, gain_part, 4)
        small[...] = small[...] / gain[...]


def cross_weights_kernel(
    info, dq, dkv, enc_in, c_in, w_q, d1_in, gain, g2_in, mix_in,
    g1_out, keep, send, small,
    enc, c, wq, d1, mix, part, gsum, grad_p, grad_q, grad_kv, sems,
    dp, seq,
):
    rows = d1.shape[0]
    loads = load_all(((w_q, wq), (d1_in, d1), (c_in, c), (mix_in, mix), (enc_in, enc)), sems)
    loads[0].wait()
    part[...] = mm_nt(dq[...], wq[...])
    wait_all(loads[1:])
    norm_back_into(d1, gain[...], part, g2_in, g1_out, gsum, rows)
    small[...] = gsum[...]
    blocks = Blocks(info, keep, send, dp, seq)
    grad_p[...] = mm(mix[...].T, g1_out[...].astype(BF)).astype(BF)
    blocks.put(grad_p, 0, sems.at[6])
    base = block_rows(grad_p.shape, dp, seq)
    grad_q[...] = mm(c[...].T, dq[...]).astype(BF)
    blocks.put(grad_q, base, sems.at[6])
    grad_kv[...] = mm(enc[...].T, dkv[...]).astype(BF)
    blocks.put(grad_kv, base + block_rows(grad_q.shape, dp, seq), sems.at[6])
    blocks.wait(sems.at[6])


def self_weights_kernel(info, dq, dkv, a_in, keep, send, a, grad_q, grad_kv, sems, dp, seq):
    rows = dq.shape[0]
    load_a = start(a_in, a, sems.at[0])
    load_a.wait()
    blocks = Blocks(info, keep, send, dp, seq)
    grad_q[...] = mm(a[rows_of(info[0], rows), :].T, dq[...]).astype(BF)
    grad_kv[...] = mm(a[...].T, dkv[...]).astype(BF)
    put_columns(blocks, (grad_q, grad_kv), 0, sems.at[1])
    blocks.wait(sems.at[1])


def finish_kernel(own, got, last, x, gain, g, out, value, up, res, gsum, at):
    rows = x.shape[0]
    value[...] = x[...].astype(F32)
    total_of(own, got, last, at, up)
    norm_back_into(value, gain[...], up, g, res, gsum, rows)
    out[...] = res[...].astype(BF)


def pack_kernel(enc_s, dec_s, cross_s, gains, rels, onehot, out):
    for i, (small, index) in enumerate(gains):
        line = jnp.sum(small[8 * index : 8 * index + 8, :], axis=0, keepdims=True)
        for k in range(line.shape[1] // LANES):
            out[4 * i + k : 4 * i + k + 1, :] = line[:, k * LANES : (k + 1) * LANES]
    base = 4 * len(gains)
    count, buckets = out.shape[0] - base, onehot.shape[0]
    lane = lax.broadcasted_iota(jnp.int32, (count, LANES), 1)
    line = lax.broadcasted_iota(jnp.int32, (count, LANES), 0)
    parts = []
    for spread in rels:
        rel = lax.dot_general(
            spread[...], onehot[...], (((1,), (1,)), ((), ())), precision=lax.Precision.HIGHEST, preferred_element_type=F32
        )
        parts.append(jnp.concatenate([rel, jnp.zeros((rel.shape[0], LANES - buckets), F32)], axis=1))
    left = count - sum(part.shape[0] for part in parts)
    rest = jnp.concatenate(parts + [jnp.zeros((left, LANES), F32)], axis=0)
    terms = [(enc_s, j) for j in range(4)] + [(dec_s, 0)] + [(cross_s, j) for j in range(3)]
    for k, (small, j) in enumerate(terms):
        value = jnp.sum(small[8 * j : 8 * j + 8, :])
        rest = jnp.where(jnp.logical_and(line == 0, lane == LANES // 2 + k), value, rest)
    out[base : base + count, :] = rest


def size_of(item):
    total = jnp.dtype(item.dtype).itemsize
    for n in item.shape:
        total *= n
    return total


def call(kernel, name, args, outs, scratch, specs, out_specs, flops, bytes_accessed):
    grant = 3 << 20
    for item in scratch:
        if hasattr(item, "shape") and item.memory_space == pltpu.VMEM:
            grant += size_of(item)
    for item, spec in list(zip(args, specs)) + list(zip(outs, out_specs)):
        if spec is SMALL:
            grant += size_of(item) + (32 << 10)
    spaces = {id(ANY): pltpu.HBM, id(KEPT): pltpu.VMEM}
    args = [
        pltpu.with_memory_space_constraint(a, spaces[id(s)]) if id(s) in spaces else a for a, s in zip(args, specs)
    ]
    outs = [spaces[id(s)](o.shape, o.dtype) if id(s) in spaces else o for o, s in zip(outs, out_specs)]
    return pl.pallas_call(
        kernel,
        out_shape=outs,
        in_specs=specs,
        out_specs=out_specs,
        scratch_shapes=scratch,
        name=name,
        compiler_params=pltpu.CompilerParams(vmem_limit_bytes=grant),
        cost_estimate=pl.CostEstimate(flops=int(flops), bytes_accessed=bytes_accessed, transcendentals=0),
    )(*args)


def sds(shape, dtype=BF):
    return jax.ShapeDtypeStruct(shape, dtype)


def vm(shape, dtype=BF):
    return pltpu.VMEM(shape, dtype)


def flip(value, axis, bit):
    count = lax.axis_size(axis)
    return lax.ppermute(value, axis, [(i, i ^ bit) for i in range(count)])


def swap_rows(value, beside=0):
    dp, seq = lax.axis_size("dp"), lax.axis_size("seq")
    half = seq // 2
    pairs = []
    for d in range(dp):
        for s in range(seq):
            move = (d & 1) != (s >= half)
            to, place = (d ^ 1, s ^ half) if move else (d, s)
            pairs.append((d * seq + s, to * seq + (place ^ beside)))
    return lax.ppermute(value, ("dp", "seq"), pairs)


class Tree:
    def __init__(self, keep, send, shapes, short=False):
        self.dp, self.seq = lax.axis_size("dp"), lax.axis_size("seq")
        bits = self.dp.bit_length() - 2
        rows = keep.shape[2]
        axes = [("dp", 2 << b) for b in range(bits)]
        if short:
            orders = [axes, axes[::-1]]
            self.last = [("seq", k) for k in range(1, self.seq)]
        else:
            axes = axes + [("seq", 1)]
            turn = max(len(axes) // 3, 1)
            orders = [axes[p * turn :] + axes[: p * turn] for p in range(3)]
            self.last = [("seq", 2)]
        self.steps = len(axes)
        unit = 16 if rows % 16 == 0 else 8
        cuts = [rows // unit * p // len(orders) * unit for p in range(len(orders) + 1)]
        self.parts = [((a, b), order) for a, b, order in zip(cuts, cuts[1:], orders) if b > a]
        left = [("dp", 2 << b) for b in range(bits - 1, -1, -1)] + [("seq", 2), ("seq", 1)]
        self.left = [list(left) for _ in self.parts]
        self.rows, self.shapes = rows, shapes
        self.stage = 0
        self.keep = [(keep.reshape(-1, LANES), 0)]
        self.recv = [(flip(send, "dp", 1).reshape(-1, LANES), 0)]
        self.done = None

    def task(self):
        stage = self.stage
        ins = self.keep + self.recv
        if stage > self.steps:
            outs = [sds((s[0] // self.dp, s[1] // self.seq), F32) for s in self.shapes]

            def last(ins, outs, sends):
                base = 0
                for out in outs:
                    tall = out.shape[0]
                    for ch in range(out.shape[1] // LANES):
                        total = 0.0
                        for ref, at in ins:
                            total = total + ref[at + base : at + base + tall, :].astype(F32)
                        out[:, ch * LANES : (ch + 1) * LANES] = total
                        base += tall

            return ins, outs, [], last
        count = len(self.keep)
        plans, outs, sends = [], [], []
        for p, (span, order) in enumerate(self.parts):
            tall = span[1] - span[0]
            left = self.left[p]
            src, step, first = (0, self.rows, span[0]) if stage == 0 else (p, tall, 0)
            if stage < self.steps:
                lead = 1 << (len(left) - 1)
                plans.append((src, step, first, tall, len(left), left.index(order[stage]), p))
                outs.append(sds((lead * tall, LANES)))
                sends.append((order[stage], lead * tall))
            else:
                plans.append((src, step, first, tall, len(left), None, span[0]))
        if stage == self.steps:
            outs = [sds((self.rows, LANES))]
            sends = [(key, self.rows) for key in self.last]

        def body(ins, outs, sends):
            for src, step, first, tall, n, pos, slot in plans:
                (keep, at), (recv, at_recv) = ins[src], ins[count + src]
                for m in range(1 << n):
                    row = m * step + first
                    one = keep[at + row : at + row + tall, :].astype(F32)
                    two = recv[at_recv + row : at_recv + row + tall, :].astype(F32)
                    if pos is None:
                        to, base = (outs[0], 0) if m == 0 else sends[m - 1]
                        base += slot
                    else:
                        low = n - 1 - pos
                        index = ((m >> (low + 1)) << low) | (m & ((1 << low) - 1))
                        to, base = sends[slot] if (m >> low) & 1 else (outs[slot], 0)
                        base += index * tall
                    to[base : base + tall, :] = (one + two).astype(BF)

        return ins, outs, sends, body

    def accept(self, outs, recv):
        if self.stage > self.steps:
            self.done = outs
            return
        if self.stage < self.steps:
            for p, (_, order) in enumerate(self.parts):
                self.left[p].remove(order[self.stage])
        self.keep = [(out, 0) for out in outs]
        self.recv = recv
        self.stage += 1


class SmallSum:
    def __init__(self, value, gains, width, heads, buckets, tokens):
        self.value = value
        self.form = (gains, width, heads, buckets, tokens)
        self.bits = lax.axis_size("dp").bit_length() - 1
        self.seq = lax.axis_size("seq")
        self.stage = 0
        self.recv = [(flip(value, "dp", 1), 0)]
        self.done = None

    def task(self):
        rows = self.value.shape[0]
        whole = self.stage == 0
        final = self.stage == self.bits
        gains, width, heads, buckets, tokens = self.form
        per = width // LANES
        outs = [sds((1, width), F32)] * gains + [sds((heads, buckets), F32)] * 2 + [sds((1, 8), F32)]
        if self.stage == self.bits:
            keys = []
        elif self.stage + 1 < self.bits:
            keys = [("dp", 2 << self.stage)]
        else:
            keys = [("seq", s) for s in range(1, self.seq)]

        def body(ins, outs, sends):
            total = ins[0][0][...]
            for ref, at in ins[1:]:
                total = total + ref[at : at + rows, :].astype(F32)
                if not whole:
                    total = total + ref[at + rows : at + 2 * rows, :].astype(F32)
            if final:
                for i in range(gains):
                    for k in range(per):
                        row = i * per + k
                        outs[i][:, k * LANES : (k + 1) * LANES] = total[row : row + 1, :]
                base = gains * per
                outs[gains][...] = total[base : base + heads, 0:buckets]
                outs[gains + 1][...] = total[base + heads : base + 2 * heads, 0:buckets]
                outs[gains + 2][...] = jnp.sqrt(total[base : base + 1, LANES // 2 : LANES // 2 + 8] / tokens)
                return
            outs[0][...] = total
            high = total.astype(BF)
            low = (total - high.astype(F32)).astype(BF)
            for ref, at in sends:
                ref[at : at + rows, :] = high
                ref[at + rows : at + 2 * rows, :] = low

        outs = outs if final else [sds(self.value.shape, F32)]
        return [(self.value, 0)] + self.recv, outs, [(key, 2 * rows) for key in keys], body

    def accept(self, outs, recv):
        if self.stage == self.bits:
            self.done = outs
            return
        self.value, self.recv = outs[0], recv
        self.stage += 1


class PairSum:
    def __init__(self, one, two, at):
        self.ins = [(one, 0), (two, at)]
        self.done = None

    def task(self):
        rows, width = self.ins[0][0].shape

        def body(ins, outs, sends):
            (one, _), (two, at) = ins
            ref, base = sends[0]
            for k in range(width // LANES):
                cols = slice(k * LANES, (k + 1) * LANES)
                total = one[:, cols].astype(F32) + two[at : at + rows, cols].astype(F32)
                ref[base + k * rows : base + (k + 1) * rows, :] = total.astype(BF)

        return self.ins, [], [(("seq", 1, "rows"), rows * width // LANES)], body

    def accept(self, outs, recv):
        self.done = recv[0]


class Copy:
    recv = ()

    def __init__(self, value):
        self.value = value
        self.done = None

    def task(self):
        def body(ins, outs, sends):
            outs[0][...] = ins[0][0][...]

        return [(self.value, 0)], [sds(self.value.shape)], [], body

    def accept(self, outs, recv):
        self.done = outs[0]


def advance(name, items, hold):
    items = [item for item in items if item.done is None]
    tasks = [item.task() for item in items]
    arrays, spots = [], []
    for ins, _, _, _ in tasks:
        mine = []
        for array, at in ins:
            known = [k for k, other in enumerate(arrays) if other is array]
            if not known:
                arrays.append(array)
            mine.append((known[0] if known else len(arrays) - 1, at))
        spots.append(mine)
    kept = [out for _, outs, _, _ in tasks for out in outs]
    sizes, slots = {}, []
    for _, _, sends, _ in tasks:
        mine = []
        for key, rows in sends:
            mine.append((key, sizes.get(key, 0)))
            sizes[key] = sizes.get(key, 0) + rows
        slots.append(mine)
    keys = sorted(sizes, key=lambda key: (len(key), key[0] == "seq", key[1]))
    mails = [sds((sizes[key], LANES)) for key in keys]

    def kernel(*refs):
        inputs, outs, mail = refs[: len(arrays)], refs[len(arrays) : len(arrays) + len(kept)], refs[len(arrays) + len(kept) :]
        for (_, task_outs, _, body), mine, to in zip(tasks, spots, slots):
            body(
                [(inputs[k], at) for k, at in mine],
                outs[: len(task_outs)],
                [(mail[keys.index(key)], at) for key, at in to],
            )
            outs = outs[len(task_outs) :]

    total = sum(size_of(a) for a in arrays + kept + mails)
    count = len(kept) + len(mails)
    results = call(kernel, name, arrays, kept + mails, [], [SMALL] * len(arrays), [SMALL] * count, total // 2_000_000 * MICROSECOND, total)
    outs, mail = list(results[: len(kept)]), list(results[len(kept) :])
    hold, mail = lax.optimization_barrier((hold, mail))
    got = {key: flip(array, *key[:2]) for key, array in zip(keys, mail)}
    for item, (_, task_outs, _, _), to in zip(items, tasks, slots):
        item.accept(outs[: len(task_outs)], [(got[key], at) for key, at in to])
        outs = outs[len(task_outs) :]
    return hold


def settle(items, hold):
    waiting = []
    for item in items:
        for array, _ in item.recv:
            if not any(array is other for other in waiting):
                waiting.append(array)
    hold, arrived = lax.optimization_barrier((hold, waiting))
    for item in items:
        item.recv = [
            (next(new for old, new in zip(waiting, arrived) if old is array), at) for array, at in item.recv
        ]
    return hold


def on_device(
    encoder_input,
    decoder_input,
    output_grad,
    segment_lengths,
    bucket_table,
    enc_gain1,
    enc_qkv,
    enc_proj,
    enc_rel,
    enc_gain2,
    enc_wi,
    enc_wo,
    enc_gainf,
    dec_gain1,
    dec_qkv,
    dec_proj,
    dec_rel,
    dec_gain2,
    cross_q,
    cross_kv,
    cross_proj,
    dec_gain3,
    dec_wi,
    dec_wo,
):
    dp, seq = lax.axis_size("dp"), lax.axis_size("seq")
    _, rows, width = encoder_input.shape
    full = rows * seq
    inner = enc_proj.shape[0]
    heads = enc_rel.shape[1]
    hid = enc_wi.shape[1]
    bucket_count = enc_rel.shape[0]
    me, place = lax.axis_index("dp"), lax.axis_index("seq")
    core = me & 1
    quarter = (place & 1) + 2 * core
    first_pos = quarter * rows
    barrier = lax.optimization_barrier

    def row(vec):
        return vec.reshape(1, -1)

    lengths = jnp.where(core == place // 2, segment_lengths, flip(segment_lengths, "dp", 1))[0]
    enc_own, enc_other = swap_rows(encoder_input[0]), swap_rows(encoder_input[0], 1)

    end1 = lengths[0]
    end2 = end1 + lengths[1]
    end3 = end2 + lengths[2]
    end4 = end3 + lengths[3]
    info = jnp.stack([quarter, end1, end2, end3, end4, me, place, me]).astype(jnp.int32)
    span = full + rows
    window = lax.dynamic_slice_in_dim(jnp.pad(bucket_table, (0, 1)), full - first_pos - rows, span)
    onehot = (jnp.arange(bucket_count, dtype=jnp.int32)[:, None] == window[None, :]).astype(F32)

    def offsets_of(rel):
        return lax.dot_general(rel, onehot, (((0,), (0,)), ((), ())), precision=lax.Precision.HIGHEST)

    enc_table, dec_table = offsets_of(enc_rel), offsets_of(dec_rel)
    enc_table, dec_table, dec_from, top_from = barrier((enc_table, dec_table, decoder_input[0], output_grad[0]))
    dec_top, dec_other = swap_rows(jnp.concatenate([dec_from, top_from])), swap_rows(dec_from, 1)
    enc_own, enc_other, info = barrier((enc_own, enc_other, info))
    enc_blocks = [enc_own, enc_other, flip(enc_own, "dp", 1), flip(enc_other, "dp", 1)]

    exps_shape = (heads, rows, full)
    sems = pltpu.SemaphoreType.DMA
    act2, act1 = (rows, width), (rows, inner)

    attn_scratch = [
        vm((width, 3 * inner)),
        vm((inner, width)),
        vm((full, width)),
        vm(act1),
        vm(act1, F32),
        vm((2 * rows, full), F32),
        vm((LANES, full + rows), F32),
        vm((rows, full), F32),
        vm(act1),
        vm(act2, F32),
        vm(act2),
    ]
    attn_outs = [
        sds((full, width)),
        sds((full, 2 * inner)),
        sds(act1),
        sds(exps_shape),
        sds(act1, F32),
        sds(act1),
        sds(act2, F32),
        sds(act2),
    ]
    enc_a, enc_pair, enc_query, enc_exps, enc_inv, enc_mix, enc_h1, enc_b, enc_g, enc_s, enc_h2, encoded, enc_small = call(
        functools.partial(self_fwd_kernel, False, "ffn"),
        "enc_fwd",
        (info, *enc_blocks, row(enc_gain1), enc_qkv, enc_proj, enc_table, row(enc_gain2), enc_wi, enc_wo, row(enc_gainf)),
        attn_outs + [sds((rows, hid)), sds((rows, hid)), sds(act2, F32), sds(act2), sds((32, width), F32)],
        attn_scratch
        + [
            vm((width, hid)),
            vm((hid, width)),
            vm((rows, hid), F32),
            vm((rows, hid)),
            vm((rows, hid)),
            vm(act2, F32),
            sems((19,)),
        ],
        [SCALARS] + [SMALL] * 5 + [ANY, ANY, SMALL, SMALL, ANY, ANY, SMALL],
        [ANY, KEPT, ANY, KEPT] + [ANY] * 7 + [SMALL] * 2,
        14.2 * MICROSECOND,
        20_000_000,
    )
    encoded, dec_top, dec_other = barrier((encoded, dec_top, dec_other))
    dec_own, top_low = dec_top[:rows], dec_top[rows:]
    dec_blocks = [dec_own, dec_other, flip(dec_own, "dp", 1), flip(dec_other, "dp", 1)]
    encoded_other = flip(encoded, "seq", 1)
    encoded_core = flip(encoded, "dp", 1)

    dec_a, dec_pair, dec_query, dec_exps, dec_inv, dec_mix, dec_h1, dec_c, cross_query, dec_small = call(
        functools.partial(self_fwd_kernel, True, "query"),
        "dec_fwd",
        (info, *dec_blocks, row(dec_gain1), dec_qkv, dec_proj, dec_table, row(dec_gain2), cross_q),
        attn_outs + [sds(act1), sds((16, width), F32)],
        attn_scratch + [vm((width, inner)), sems((19,))],
        [SCALARS] + [SMALL] * 5 + [ANY, ANY, SMALL, SMALL, ANY],
        [ANY, KEPT, ANY, KEPT] + [ANY] * 4 + [SMALL] * 2,
        11.3 * MICROSECOND,
        16_000_000,
    )

    encoded_other, cross_query = barrier((encoded_other, cross_query))
    encoded_blocks = [encoded, encoded_other, encoded_core, flip(encoded_other, "dp", 1)]

    def wide_blocks(*shapes):
        total = sum(block_rows(shape, dp, seq) for shape in shapes)
        return [sds((dp // 2, seq, total, LANES))] * 2

    ffn_shapes = ((hid, width), (width, hid), (inner, width))
    enc_all, cross_pair, cross_exps, cross_inv, cross_mix, dec_out, g_d2, keep, send, cross_small = call(
        functools.partial(cross_kernel, dp=dp, seq=seq),
        "cross_fwd",
        (info, *encoded_blocks, cross_query, dec_h1, top_low, cross_kv, cross_proj, row(dec_gain3), dec_wi, dec_wo),
        [
            sds((full, width)),
            sds((full, 2 * inner)),
            sds(exps_shape),
            sds(act1, F32),
            sds(act1),
            sds(act2),
            sds(act2, F32),
            *wide_blocks(*ffn_shapes),
            sds((32, width), F32),
        ],
        [
            vm((full, width)),
            vm(act1),
            vm(act1, F32),
            vm((2 * rows, full), F32),
            vm((rows, full), F32),
            vm(act1),
            vm(act2, F32),
            vm(act2),
            vm(act2),
            vm((width, 2 * inner)),
            vm((inner, width)),
            vm((width, hid)),
            vm((hid, width)),
            vm((rows, hid), F32),
            vm((rows, hid)),
            vm((rows, hid)),
            vm((rows, hid)),
            vm(act2, F32),
            vm((8, width), F32),
            vm((hid, width)),
            vm((width, hid)),
            vm((inner, width)),
            sems((16,)),
        ],
        [SCALARS] + [SMALL] * 4 + [ANY] * 5 + [SMALL, ANY, ANY],
        [ANY, KEPT, KEPT, ANY, ANY] + [SMALL] * 2 + [ANY] * 2 + [SMALL],
        17 * MICROSECOND,
        30_000_000,
    )
    tree1 = Tree(keep, send, ffn_shapes)

    def back_scratch(kind):
        out = [
            vm(act1, F32),
            vm(act1),
            vm((inner, width)),
            vm(act1),
        ]
        out += [
            vm((width, 2 * inner)) if kind == "cross" else vm((width, 3 * inner)),
            vm(act1),
            vm((2 * inner, full)),
            vm((2 * rows, full), F32),
            vm((2 * rows, full)),
            vm((2 * rows, LANES), F32),
            vm((full, width), F32),
        ]
        if kind == "self":
            out += [vm((LANES, full + LANES), F32), vm((full, width))]
        return out + [sems((8,))]

    part_outs = [sds(act2, F32), sds(act2), sds((2 * rows, width))]
    pair_outs = [sds(act1), sds((full, 2 * inner))]
    ep0, ep1, ep23, cross_dq, cross_dkv = call(
        functools.partial(attn_back_kernel, kind="cross"),
        "cross_back",
        (info, g_d2, cross_inv, cross_mix, cross_proj, cross_exps, cross_pair, cross_query, cross_kv),
        part_outs + pair_outs,
        back_scratch("cross"),
        [SCALARS, SMALL] + [ANY] * 3 + [KEPT] * 2 + [ANY] * 2,
        [SMALL] * 5,
        10.2 * MICROSECOND,
        15_000_000,
    )
    enc_got = flip(ep23, "dp", 1)
    enc_pass = PairSum(ep1, enc_got, rows)
    cross_dq, cross_dkv = advance("sum_1", [enc_pass], (cross_dq, cross_dkv))

    cross_shapes = ((inner, width), (width, inner), (width, 2 * inner))
    g_d1, keep, send, gain2_small = call(
        functools.partial(cross_weights_kernel, dp=dp, seq=seq),
        "cross_weights",
        (info, cross_dq, cross_dkv, enc_all, dec_c, cross_q, dec_h1, row(dec_gain2), g_d2, dec_mix),
        [sds(act2, F32), *wide_blocks(*cross_shapes), sds((8, width), F32)],
        [
            vm((full, width)),
            vm(act2),
            vm((width, inner)),
            vm(act2, F32),
            vm(act1),
            vm(act2, F32),
            vm((8, width), F32),
            vm((inner, width)),
            vm((width, inner)),
            vm((width, 2 * inner)),
            sems((7,)),
        ],
        [SCALARS, SMALL, SMALL] + [ANY] * 4 + [SMALL, SMALL, ANY],
        [SMALL, ANY, ANY, SMALL],
        7 * MICROSECOND,
        8_000_000,
    )
    tree2 = Tree(keep, send, cross_shapes)
    enc_last, enc_last_at = enc_pass.done
    enc_last, ep0, g_d1, dec_out = advance("sum_2", [tree1], (enc_last, ep0, g_d1, dec_out))
    dec_output = swap_rows(dec_out)

    g_e1, keep, send, enc_gain_small = call(
        functools.partial(enc_ffn_back_kernel, dp=dp, seq=seq, at=enc_last_at),
        "enc_ffn_back",
        (info, ep0, enc_got, enc_last, enc_h2, row(enc_gainf), enc_h1, row(enc_gain2), enc_g, enc_s, enc_b, enc_wi, enc_wo, enc_mix),
        [sds(act2, F32), *wide_blocks(*ffn_shapes), sds((16, width), F32)],
        [
            vm(act2, F32),
            vm(act2, F32),
            vm(act2, F32),
            vm((rows, hid)),
            vm((rows, hid)),
            vm(act2),
            vm((width, hid)),
            vm((hid, width)),
            vm(act1),
            vm(act2, F32),
            vm(act2),
            vm((rows, hid), F32),
            vm((rows, hid)),
            vm(act2, F32),
            vm((8, width), F32),
            vm((hid, width)),
            vm((width, hid)),
            vm((inner, width)),
            sems((9,)),
        ],
        [SCALARS] + [SMALL] * 3 + [ANY, SMALL, ANY, SMALL] + [ANY] * 6,
        [SMALL, ANY, ANY, SMALL],
        9.9 * MICROSECOND,
        14_000_000,
    )
    tree4 = Tree(keep, send, ffn_shapes)
    g_e1 = advance("sum_3", [tree1, tree2], g_e1)

    def self_back(name, grad, inv, mix, proj, exps, pair, query, qkv, source, gain):
        return call(
            functools.partial(attn_back_kernel, kind="self"),
            name,
            (info, grad, inv, mix, proj, exps, pair, query, qkv, source, row(gain)),
            part_outs + pair_outs + [sds((heads, span), F32), sds((8, width), F32)],
            back_scratch("self"),
            [SCALARS, SMALL] + [ANY] * 3 + [KEPT] * 2 + [ANY] * 3 + [SMALL],
            [SMALL] * 7,
            11 * MICROSECOND,
            15_000_000,
        )

    def self_weights(name, dq, dkv, source, cost):
        return call(
            functools.partial(self_weights_kernel, dp=dp, seq=seq),
            name,
            (info, dq, dkv, source),
            wide_blocks((width, 3 * inner)),
            [vm((full, width)), vm((width, inner)), vm((width, 2 * inner)), sems((2,))],
            [SCALARS, SMALL, SMALL, ANY],
            [ANY] * 2,
            cost * MICROSECOND,
            800_000,
        )

    qkv_shapes = ((width, 3 * inner),)
    xp0, xp1, xp23, enc_dq, enc_dkv, enc_spread, enc_first_small = self_back(
        "enc_back", g_e1, enc_inv, enc_mix, enc_proj, enc_exps, enc_pair, enc_query, enc_qkv, enc_a, enc_gain1
    )
    enc_mine = flip(xp23, "dp", 1)
    enc_pass = PairSum(xp1, enc_mine, rows)
    enc_dq, enc_dkv, g_d1, dec_output = advance(
        "sum_4", [tree1, tree2, tree4], (enc_dq, enc_dkv, g_d1, dec_output)
    )
    dp0, dp1, dp23, dec_dq, dec_dkv, dec_spread, dec_first_small = self_back(
        "dec_back", g_d1, dec_inv, dec_mix, dec_proj, dec_exps, dec_pair, dec_query, dec_qkv, dec_a, dec_gain1
    )
    dec_mine = flip(dp23, "dp", 1)
    dec_pass = PairSum(dp1, dec_mine, rows)

    def finish(name, own, got, done, x, gain, g):
        last, at = done
        return call(
            functools.partial(finish_kernel, at=at),
            name,
            (own, got, last, x, row(gain), g),
            [sds(act2)],
            [vm(act2, F32)] * 3 + [vm((8, width), F32)],
            [SMALL] * 6,
            [SMALL],
            1.6 * MICROSECOND,
            2_000_000,
        )[0]

    gain_count = 6
    packed = call(
        lambda e, d, c, g0, g1, g2, g3, s0, s1, oh, out: pack_kernel(
            e, d, c, ((g0, 0), (g1, 1), (g1, 0), (g2, 0), (g3, 0), (c, 3)), (s0, s1), oh, out
        ),
        "pack",
        (enc_small, dec_small, cross_small, enc_first_small, enc_gain_small, dec_first_small, gain2_small, enc_spread, dec_spread, onehot),
        [sds((4 * gain_count + 3 * heads, LANES), F32)],
        [],
        [SMALL] * 10,
        [SMALL],
        1 * MICROSECOND,
        500_000,
    )[0]
    early = [tree1, tree2, tree4]
    small = SmallSum(packed, gain_count, width, heads, bucket_count, float(rows * width * dp * seq))
    out_copy = Copy(dec_output)
    tree5 = Tree(*self_weights("enc_weights", enc_dq, enc_dkv, enc_a, 0.2), qkv_shapes, True)
    dec_dq, xp0 = advance("sum_5", [enc_pass, out_copy] + early, (dec_dq, xp0))
    tree3 = Tree(*self_weights("dec_weights", dec_dq, dec_dkv, dec_a, 5), qkv_shapes, True)
    dp0, xp0 = advance("sum_6", [tree5, tree3, small, dec_pass], (dp0, xp0))
    enc_grad = finish("enc_finish", xp0, enc_mine, enc_pass.done, enc_own, enc_gain1, g_e1)
    dp0, enc_grad = advance("sum_7", [tree5, tree3, small] + early, (dp0, enc_grad))
    encoder_grad = swap_rows(enc_grad)
    decoder_grad = swap_rows(finish("dec_finish", dp0, dec_mine, dec_pass.done, dec_own, dec_gain1, g_d1))
    dp0, encoder_grad = advance("sum_8", [tree5, tree3, small] + early, (dp0, encoder_grad))
    enc_copy, dec_copy = Copy(encoder_grad), Copy(decoder_grad)
    step = 9
    while later := [item for item in early + [tree5, tree3, small, enc_copy, dec_copy] if item.done is None]:
        (dp0,) = advance(f"sum_{step}", later, (dp0,))
        step += 1

    gain_sums, (enc_rel_sum, dec_rel_sum, rms) = small.done[:gain_count], small.done[gain_count:]

    def gain_of(i):
        return gain_sums[i].reshape(-1)

    dec_wo_g, dec_wi_g, cross_proj_g = tree1.done
    dec_proj_g, cross_q_g, cross_kv_g = tree2.done
    (dec_qkv_g,) = tree3.done
    (enc_qkv_g,) = tree5.done
    enc_wo_g, enc_wi_g, enc_proj_g = tree4.done
    return (
        out_copy.done[None],
        enc_copy.done[None],
        dec_copy.done[None],
        rms.reshape(-1),
        gain_of(0),
        enc_qkv_g,
        enc_proj_g,
        enc_rel_sum.T,
        gain_of(1),
        enc_wi_g,
        enc_wo_g,
        gain_of(2),
        gain_of(3),
        dec_qkv_g,
        dec_proj_g,
        dec_rel_sum.T,
        gain_of(4),
        cross_q_g,
        cross_kv_g,
        cross_proj_g,
        gain_of(5),
        dec_wi_g,
        dec_wo_g,
    )


def solution(mesh):
    rows = P("dp", "seq", None)
    both = P("dp", "seq")
    return jax.shard_map(
        on_device,
        mesh=mesh,
        in_specs=(rows, rows, rows, P("dp", None)) + (P(),) * 20,
        out_specs=(
            (rows,) * 3
            + (P(),) * 2
            + (both,) * 2
            + (P(),) * 2
            + (both,) * 2
            + (P(),) * 2
            + (both,) * 2
            + (P(),) * 2
            + (both,) * 3
            + (P(),)
            + (both,) * 2
        ),
        check_vma=False,
    )
```

```python
import functools

import jax
import jax.numpy as jnp
from jax import lax
from jax.experimental import pallas as pl
from jax.experimental.pallas import tpu as pltpu
from jax.sharding import PartitionSpec as P

HEAD_DIM = 64
LANES = 128
BF = jnp.bfloat16
F32 = jnp.float32

eps_norm = 1e-06
negative = -1000000000.0
gelu_in = 0.7978845608028654
gelu_cube = 0.044715

MICROSECOND = 1_150_000_000 * 2
ANY = pl.BlockSpec(memory_space=pltpu.HBM)
SMALL = pl.BlockSpec(memory_space=pltpu.VMEM)
KEPT = pl.BlockSpec(memory_space=pltpu.VMEM)
SCALARS = pl.BlockSpec(memory_space=pltpu.SMEM)


def mm(left, right):
    return jnp.dot(left, right, preferred_element_type=F32)


def mm_nt(left, right):
    return lax.dot_general(left, right, (((1,), (1,)), ((), ())), preferred_element_type=F32)


def start(source, target, sem):
    copy = pltpu.make_async_copy(source, target, sem)
    copy.start()
    return copy


def rows_of(step, size):
    return pl.ds(pl.multiple_of(step * size, size), size)


def chunks(count, body, unroll=1):
    def step(i, carry):
        body(i)
        return carry

    lax.fori_loop(0, count, step, 0, unroll=unroll)


def inv_rms(values):
    return lax.rsqrt(jnp.mean(values * values, axis=-1, keepdims=True) + eps_norm)


def norm_into(source, gain, target, rows, chunk=64):
    def body(i):
        at = rows_of(i, chunk)
        v = source[at, :].astype(F32)
        target[at, :] = (v * inv_rms(v) * gain).astype(target.dtype)

    chunks(rows // chunk, body, 2)


def norm_back_into(values, gain, incoming, residual, target, grad_sum, rows, chunk=32):
    grad_sum[...] = jnp.zeros_like(grad_sum)

    def body(i):
        at = rows_of(i, chunk)
        v = values[at, :]
        dy = incoming[at, :]
        r = inv_rms(v)
        hat = v * r
        part = dy * hat
        grad_sum[...] += jnp.sum(part.reshape(chunk // 8, 8, part.shape[-1]), axis=0)
        scaled = dy * gain
        mean = jnp.mean(scaled * hat, axis=-1, keepdims=True)
        out = r * (scaled - hat * mean)
        target[at, :] = out if residual is None else residual[at, :].astype(F32) + out

    chunks(rows // chunk, body, 4)


def square_sum(values):
    rows, width = values.shape
    return jnp.sum((values * values).reshape(rows // 8, 8, width), axis=0)


def gelu_pair(u):
    sq = u * u
    t = jnp.tanh(gelu_in * u * (1.0 + gelu_cube * sq))
    half = 0.5 * (1.0 + t)
    slope = half + 0.5 * u * (1.0 - t * t) * (gelu_in * (1.0 + 3.0 * gelu_cube * sq))
    return u * half, slope


def place_ids(info, shape, axis, base):
    place = lax.broadcasted_iota(jnp.int32, shape, axis) + base
    ids = jnp.zeros(shape, jnp.int32)
    for slot in range(1, 5):
        ids = ids + (place >= info[slot]).astype(jnp.int32)
    return place, ids


def fill_mask(info, mask, causal):
    rows, keys = mask.shape
    first = info[0] * rows
    key_place, key_ids = place_ids(info, (1, keys), 1, 0)

    def body(i):
        place, ids = place_ids(info, (32, 1), 0, first + i * 32)
        allowed = ids == key_ids
        if causal:
            allowed = jnp.logical_and(allowed, key_place <= place)
        mask[rows_of(i, 32), :] = jnp.where(allowed, 0.0, negative)

    chunks(rows // 32, body)


def lane_split(pair):
    low = lax.broadcasted_iota(jnp.int32, pair.shape, 1) < HEAD_DIM
    zero = jnp.zeros_like(pair)
    return jnp.concatenate([jnp.where(low, pair, zero), jnp.where(low, zero, pair)], axis=0)


def lane_join(first, second):
    low = lax.broadcasted_iota(jnp.int32, first.shape, 1) < HEAD_DIM
    return jnp.where(low, first, second)


def attend_fwd(q, kv, table, mask, exps, scores, toeplitz, mix, inverse):
    rows, inner = q.shape
    keys = kv.shape[0]
    half = LANES
    low = lax.broadcasted_iota(jnp.int32, (1, LANES), 1) < HEAD_DIM
    for pair in range(inner // LANES):
        lanes = slice(pair * LANES, (pair + 1) * LANES)
        scores[...] = mm_nt(lane_split(q[:, lanes]), kv[:, lanes])
        for side in range(2):
            head = 2 * pair + side
            if table is not None:
                width = table.shape[1]
                row = jnp.broadcast_to(table[head : head + 1, :], (half, width))
                toeplitz[...] = pltpu.roll(row, width - half + 1, 1, stride=1, stride_axis=0)
            for block in range(rows // half):
                shift = half * (rows // half - 1 - block)

                def body(i, side=side, block=block, head=head, shift=shift):
                    at = rows_of(i, 32)
                    whole = pl.ds(pl.multiple_of(side * rows + block * half + i * 32, 32), 32)
                    mine = pl.ds(pl.multiple_of(block * half + i * 32, 32), 32)
                    s = scores[whole, :] + mask[mine, :]
                    if table is not None:
                        s = s + toeplitz[at, shift : shift + keys]
                    exps[head, mine, :] = jnp.exp(s - jnp.max(s, axis=-1, keepdims=True)).astype(BF)

                chunks(half // 32, body, half // 32)
        v_pair = kv[:, inner + pair * LANES : inner + (pair + 1) * LANES]
        one = jnp.ones_like(v_pair)
        first = mm(exps[2 * pair], jnp.where(low, v_pair, one))
        second = mm(exps[2 * pair + 1], jnp.where(low, one, v_pair))
        first_inv = 1.0 / first[:, HEAD_DIM : HEAD_DIM + 1]
        second_inv = 1.0 / second[:, 0:1]
        inv = jnp.where(low, first_inv, second_inv)
        inverse[:, lanes] = inv
        mix[:, lanes] = (lane_join(first, second) * inv).astype(BF)


def attend_back(q, kv, exps, scaled, mix, dq, dkv_t, scores, dscores, delta, skew, spread):
    rows, inner = q.shape
    keys = kv.shape[0]
    half = LANES
    count = keys // LANES
    for pair in range(inner // LANES):
        lanes = slice(pair * LANES, (pair + 1) * LANES)
        later = slice(inner + pair * LANES, inner + (pair + 1) * LANES)
        do_two = lane_split(scaled[:, lanes])
        scores[...] = mm_nt(do_two, kv[:, later])
        both = do_two.astype(F32) * jnp.concatenate([mix[:, lanes], mix[:, lanes]], axis=0).astype(F32)
        delta[...] = jnp.broadcast_to(jnp.sum(both, axis=-1, keepdims=True), delta.shape)
        for side in range(2):
            head = 2 * pair + side

            def body(i, side=side, head=head):
                at = rows_of(i, 32)
                spots = [
                    (
                        pl.ds(pl.multiple_of(side * rows + block * half + i * 32, 32), 32),
                        pl.ds(pl.multiple_of(block * half + i * 32, 32), 32),
                    )
                    for block in range(2)
                ]
                shifts = [delta[whole, :] for whole, _ in spots]
                before = None
                for k in range(count + 1):
                    cols = slice(k * LANES, (k + 1) * LANES)
                    made = []
                    if k < count:
                        for (whole, mine), shift in zip(spots, shifts):
                            ds = exps[head, mine, cols].astype(F32) * (scores[whole, cols] - shift)
                            dscores[whole, cols] = ds.astype(BF)
                            made.append(ds)
                    if skew is not None:
                        terms = made[1:] + ([] if before is None else [before])
                        skew[at, cols] = terms[0] if len(terms) == 1 else terms[0] + terms[1]
                        before = made[0] if made else None

            chunks(half // 32, body, half // 32)
            if skew is not None:
                width = spread.shape[1]
                wide = skew.shape[1]
                total = jnp.zeros((8, width), F32)
                for group in range(half // 8):
                    part = jnp.concatenate(
                        [skew[8 * group : 8 * group + 8, :], jnp.zeros((8, width - wide), F32)], axis=1
                    )
                    by = half - 8 - 8 * group
                    total = total + (pltpu.roll(part, by, 1) if by else part)
                left = 7 - lax.broadcasted_iota(jnp.int32, (8, width), 0)
                for bit in (1, 2, 4):
                    total = jnp.where((left & bit) != 0, pltpu.roll(total, bit, 1), total)
                spread[head : head + 1, :] = jnp.sum(total, axis=0, keepdims=True)
        k_pair = kv[:, lanes]
        dq[:, lanes] = lane_join(mm(dscores[0:rows, :], k_pair), mm(dscores[rows:, :], k_pair)).astype(BF)
        q_two = lane_split(q[:, lanes])
        dkv_t[lanes, :] = mm(q_two.T, dscores[...]).astype(BF)
        dv = mm(do_two[0:rows].T, exps[2 * pair]) + mm(do_two[rows:].T, exps[2 * pair + 1])
        dkv_t[later, :] = dv.astype(BF)


class Blocks:
    def __init__(self, info, keep, send, dp, seq):
        self.info, self.keep, self.send, self.dp, self.seq = info, keep, send, dp, seq

    def put(self, grad, base, sem):
        rows, cols = grad.shape
        tall, wide = rows // self.dp, cols // self.seq
        me, place = self.info[5], self.info[6]

        def body(j):
            for s in range(self.seq):
                for ch in range(wide // LANES):
                    col = pl.ds(pl.multiple_of((place ^ s) * wide + ch * LANES, LANES), LANES)
                    to = pl.ds(base + ch * tall, tall)
                    for target, flip_core in ((self.keep, 0), (self.send, 1)):
                        row = pl.ds(pl.multiple_of((me ^ (2 * j) ^ flip_core) * tall, tall), tall)
                        start(grad.at[row, col], target.at[j, s, to, :], sem)

        chunks(self.dp // 2, body, self.dp // 2 if self.dp <= 8 else 1)

    def wait(self, sem):
        for target in (self.keep, self.send):
            pltpu.make_async_copy(target, target, sem).wait()


def block_rows(shape, dp, seq):
    return shape[0] * shape[1] // (dp * seq * LANES)


def put_columns(blocks, grads, base, sem):
    rows = grads[0].shape[0]
    cols = grads[0].shape[1] + grads[1].shape[1]
    tall, wide = rows // blocks.dp, cols // blocks.seq
    per = wide // LANES
    me, place = blocks.info[5], blocks.info[6]

    def body(j):
        for chunk in range(cols // LANES):
            s = (chunk // per) ^ place
            to = pl.ds(base + (chunk % per) * tall, tall)
            first = chunk * LANES
            grad, col = (grads[0], first) if first < grads[0].shape[1] else (grads[1], first - grads[0].shape[1])
            for target, flip_core in ((blocks.keep, 0), (blocks.send, 1)):
                row = pl.ds(pl.multiple_of((me ^ (2 * j) ^ flip_core) * tall, tall), tall)
                start(grad.at[row, pl.ds(col, LANES)], target.at[j, s, to, :], sem)

    chunks(blocks.dp // 2, body, blocks.dp // 2 if blocks.dp <= 8 else 1)


def total_of(own, got, last, at, target):
    rows, width = own.shape
    for k in range(width // LANES):
        cols = slice(k * LANES, (k + 1) * LANES)
        target[:, cols] = (
            own[:, cols]
            + got[0:rows, cols].astype(F32)
            + last[at + k * rows : at + (k + 1) * rows, :].astype(F32)
        )


def load_all(names, sems, base=0):
    return [start(src, dst, sems.at[base + j]) for j, (src, dst) in enumerate(names)]


def wait_all(copies):
    for copy in copies:
        copy.wait()


def self_fwd_kernel(causal, last, info, x0, x1, x2, x3, gain, w_qkv, w_proj, table, *rest):
    if last == "ffn":
        (gain2, w_in, w_out, gainf), rest = rest[:4], rest[4:]
        (a_out, kv, q_out, exps, inv_out, o_out, h1_out, b_out, g_out, s_out, h2_out, fin_out, small), rest = rest[:13], rest[13:]
        (wq, wp, a, q, inv, scores, toeplitz, mask, mix, h1, normed, wi, wo, hidden, act, slope, h2, sems) = rest
    else:
        (gain2, w_in), rest = rest[:2], rest[2:]
        (a_out, kv, q_out, exps, inv_out, o_out, h1_out, b_out, fin_out, small), rest = rest[:10], rest[10:]
        (wq, wp, a, q, inv, scores, toeplitz, mask, mix, h1, normed, wi, sems) = rest
    rows = h1.shape[0]
    inner = w_proj.shape[0]
    quarter = info[0]
    load_q = start(w_qkv, wq, sems.at[4])
    load_p = start(w_proj, wp, sems.at[5])
    load_i = start(w_in, wi, sems.at[6])
    if last == "ffn":
        load_o = start(w_out, wo, sems.at[7])
    fill_mask(info, mask, causal)
    for j, block in enumerate((x0, x1, x2, x3)):
        norm_into(block.at[0:rows], gain[...], a.at[rows_of(quarter ^ j, rows)], rows)
    saves = [start(a, a_out, sems.at[8])]
    load_q.wait()
    q[...] = mm(a[rows_of(quarter, rows), :], wq[:, 0:inner]).astype(BF)

    def project(i):
        at = rows_of(i, rows)
        kv[at, :] = mm(a[at, :], wq[:, inner:]).astype(BF)

    chunks(4, project, 4)
    saves.append(start(q, q_out, sems.at[10]))
    attend_fwd(q, kv, table, mask, exps, scores, toeplitz, mix, inv)
    saves += [start(mix, o_out, sems.at[12]), start(inv, inv_out, sems.at[18])]
    load_p.wait()
    att = mm(mix[...], wp[...])
    small[0:8, :] = square_sum(att)
    first = x0[0:rows, :].astype(F32) + att
    h1[...] = first
    small[8:16, :] = square_sum(first)
    saves.append(start(h1, h1_out, sems.at[13]))
    norm_into(h1, gain2[...], normed, rows)
    saves.append(start(normed, b_out, sems.at[14]))
    load_i.wait()
    if last == "ffn":
        hidden[...] = mm(normed[...], wi[...])
        activate(hidden, act, slope)
        saves += [start(act, g_out, sems.at[15]), start(slope, s_out, sems.at[16])]
        load_o.wait()
        ffn = mm(act[...], wo[...])
        small[16:24, :] = square_sum(ffn)
        second = h1[...] + ffn
        h2[...] = second
        small[24:32, :] = square_sum(second)
        saves.append(start(h2, h2_out, sems.at[17]))
        norm_into(h2, gainf[...], fin_out, rows)
    else:
        fin_out[...] = mm(normed[...], wi[...]).astype(BF)
    wait_all(saves)


def activate(hidden, act, slope):
    def body(i):
        at = rows_of(i, 16)
        value, rate = gelu_pair(hidden[at, :])
        act[at, :] = value.astype(BF)
        slope[at, :] = rate.astype(BF)

    chunks(hidden.shape[0] // 16, body, 16)


def ffn_back(blocks, base, top, act, slope, normed, wi, wo, hidden, du, back, grad_wo, grad_wi, sem, loads=()):
    rows = top.shape[0]
    wait_all(loads[:1])
    hidden[...] = mm_nt(top[...], wo[...])
    wait_all(loads[1:3])
    grad_wo[...] = mm(act[...].T, top[...]).astype(BF)
    blocks.put(grad_wo, base, sem)

    def slide(i):
        at = rows_of(i, 16)
        du[at, :] = (hidden[at, :] * slope[at, :].astype(F32)).astype(BF)

    chunks(rows // 16, slide, 16)
    wait_all(loads[3:])
    grad_wi[...] = mm(normed[...].T, du[...]).astype(BF)
    blocks.put(grad_wi, base + block_rows(grad_wo.shape, blocks.dp, blocks.seq), sem)
    back[...] = mm_nt(du[...], wi[...])


def cross_kernel(
    info, e0, e1, e2, e3, q_in, d1_in, top_in, w_kv, w_proj, gain, w_in, w_out,
    enc_out, kv, exps, inv_out, o_out, out_out, g2_out, keep, send, small,
    enc, q, inv, scores, mask, mix, h, top, normed, wkv, wp, wi, wo, hidden, act, slope, du, back, gsum, grad_a, grad_b, grad_p, sems,
    dp, seq,
):
    rows = h.shape[0]
    quarter = info[0]
    load_kv = start(w_kv, wkv, sems.at[4])
    load_q = start(q_in, q, sems.at[5])
    load_p = start(w_proj, wp, sems.at[6])
    load_d = start(d1_in, h, sems.at[7])
    load_i = start(w_in, wi, sems.at[8])
    load_o = start(w_out, wo, sems.at[9])
    load_t = start(top_in.at[rows : 2 * rows], top, sems.at[10])
    fill_mask(info, mask, False)
    load_kv.wait()
    for j, block in enumerate((e0, e1, e2, e3)):
        at = rows_of(quarter ^ j, rows)
        enc[at, :] = block[...]
        kv[at, :] = mm(block[...], wkv[...]).astype(BF)
    saves = [start(enc, enc_out, sems.at[11])]
    load_q.wait()
    attend_fwd(q, kv, None, mask, exps, scores, None, mix, inv)
    saves += [start(mix, o_out, sems.at[14]), start(inv, inv_out, sems.at[0])]
    load_p.wait()
    load_d.wait()
    att = mm(mix[...], wp[...])
    small[0:8, :] = square_sum(att)
    h[...] = h[...] + att
    norm_into(h, gain[...], normed, rows)
    load_i.wait()
    hidden[...] = mm(normed[...], wi[...])
    activate(hidden, act, slope)
    load_o.wait()
    ffn = mm(act[...], wo[...])
    small[8:16, :] = square_sum(ffn)
    third = h[...] + ffn
    small[16:24, :] = square_sum(third)
    out_out[...] = third.astype(BF)
    load_t.wait()
    blocks = Blocks(info, keep, send, dp, seq)
    ffn_back(blocks, 0, top, act, slope, normed, wi, wo, hidden, du, back, grad_a, grad_b, sems.at[15])
    norm_back_into(h, gain[...], back, top, g2_out, gsum, rows)
    small[24:32, :] = gsum[...]
    grad_p[...] = mm(mix[...].T, g2_out[...].astype(BF)).astype(BF)
    blocks.put(grad_p, block_rows(grad_a.shape, dp, seq) + block_rows(grad_b.shape, dp, seq), sems.at[15])
    wait_all(saves)
    blocks.wait(sems.at[15])


def enc_ffn_back_kernel(
    info, own, got, last, h2_in, gainf, h1_in, gain2, act_in, slope_in, normed_in, w_in, w_out, mix_in,
    g1_out, keep, send, small,
    up, h2, h1, act, slope, normed, wi, wo, mix, g2, top, hidden, du, back, gsum, grad_a, grad_b, grad_p, sems,
    dp, seq, at,
):
    rows = h1.shape[0]
    loads = load_all(
        ((h2_in, h2), (w_out, wo), (slope_in, slope), (act_in, act), (w_in, wi), (normed_in, normed), (h1_in, h1), (mix_in, mix)),
        sems,
    )
    total_of(own, got, last, at, up)
    loads[0].wait()
    norm_back_into(h2, gainf[...], up, None, g2, gsum, rows)
    small[0:8, :] = gsum[...]
    top[...] = g2[...].astype(BF)
    blocks = Blocks(info, keep, send, dp, seq)
    ffn_back(blocks, 0, top, act, slope, normed, wi, wo, hidden, du, back, grad_a, grad_b, sems.at[8], loads[1:6])
    wait_all(loads[6:])
    norm_back_into(h1, gain2[...], back, g2, g1_out, gsum, rows)
    small[8:16, :] = gsum[...]
    grad_p[...] = mm(mix[...].T, g1_out[...].astype(BF)).astype(BF)
    blocks.put(grad_p, block_rows(grad_a.shape, dp, seq) + block_rows(grad_b.shape, dp, seq), sems.at[8])
    blocks.wait(sems.at[8])


def attn_back_kernel(info, g_in, inv_in, o_in, w_proj, exps, kv, q_in, w_kv, *rest, kind):
    spread = skew = None
    if kind == "self":
        (a_in, gain, p0, p1, p23, dq, dkv, spread, small), rest = rest[:9], rest[9:]
        (inv, mix, wp, q, wkv, scaled, dkv_t, scores, dscores, delta, wide, skew, a, sems) = rest
    else:
        (p0, p1, p23, dq, dkv), rest = rest[:5], rest[5:]
        (inv, mix, wp, q, wkv, scaled, dkv_t, scores, dscores, delta, wide, sems) = rest
    rows = g_in.shape[0]
    inner = dq.shape[1]
    quarter = info[0]
    names = [(w_proj, wp), (inv_in, inv), (o_in, mix), (q_in, q), (w_kv, wkv)]
    if kind == "self":
        names.append((a_in, a))
    loads = load_all(names, sems)
    wait_all(loads[:2])
    scaled[...] = (mm_nt(g_in[...].astype(BF), wp[...]) * inv[...]).astype(BF)
    wait_all(loads[2:4])
    attend_back(q, kv, exps, scaled, mix, dq, dkv_t, scores, dscores, delta, skew, spread)
    dkv[...] = dkv_t[...].T
    wait_all(loads[4:])
    first = wkv.shape[1] - dkv.shape[1]

    def project(i):
        at = rows_of(i, rows)
        wide[at, :] = mm_nt(dkv[at, :], wkv[:, first:])

    chunks(4, project, 4)
    own = rows_of(quarter, rows)
    if kind == "self":
        wide[own, :] = wide[own, :] + mm_nt(dq[...], wkv[:, 0:inner])
    p1[...] = wide[rows_of(quarter ^ 1, rows), :].astype(BF)
    p23[0:rows, :] = wide[rows_of(quarter ^ 2, rows), :].astype(BF)
    p23[rows:, :] = wide[rows_of(quarter ^ 3, rows), :].astype(BF)
    p0[...] = wide[own, :]
    if kind == "self":
        small[...] = jnp.zeros_like(small)

        def gain_part(i):
            at = rows_of(i, 64)
            part = wide[at, :] * a[at, :].astype(F32)
            small[...] += jnp.sum(part.reshape(8, 8, part.shape[-1]), axis=0)

        chunks(4 * rows // 64, gain_part, 4)
        small[...] = small[...] / gain[...]


def cross_weights_kernel(
    info, dq, dkv, enc_in, c_in, w_q, d1_in, gain, g2_in, mix_in,
    g1_out, keep, send, small,
    enc, c, wq, d1, mix, part, gsum, grad_p, grad_q, grad_kv, sems,
    dp, seq,
):
    rows = d1.shape[0]
    loads = load_all(((w_q, wq), (d1_in, d1), (c_in, c), (mix_in, mix), (enc_in, enc)), sems)
    loads[0].wait()
    part[...] = mm_nt(dq[...], wq[...])
    wait_all(loads[1:])
    norm_back_into(d1, gain[...], part, g2_in, g1_out, gsum, rows)
    small[...] = gsum[...]
    blocks = Blocks(info, keep, send, dp, seq)
    grad_p[...] = mm(mix[...].T, g1_out[...].astype(BF)).astype(BF)
    blocks.put(grad_p, 0, sems.at[6])
    base = block_rows(grad_p.shape, dp, seq)
    grad_q[...] = mm(c[...].T, dq[...]).astype(BF)
    blocks.put(grad_q, base, sems.at[6])
    grad_kv[...] = mm(enc[...].T, dkv[...]).astype(BF)
    blocks.put(grad_kv, base + block_rows(grad_q.shape, dp, seq), sems.at[6])
    blocks.wait(sems.at[6])


def self_weights_kernel(info, dq, dkv, a_in, keep, send, a, grad_q, grad_kv, sems, dp, seq):
    rows = dq.shape[0]
    load_a = start(a_in, a, sems.at[0])
    load_a.wait()
    blocks = Blocks(info, keep, send, dp, seq)
    grad_q[...] = mm(a[rows_of(info[0], rows), :].T, dq[...]).astype(BF)
    grad_kv[...] = mm(a[...].T, dkv[...]).astype(BF)
    put_columns(blocks, (grad_q, grad_kv), 0, sems.at[1])
    blocks.wait(sems.at[1])


def finish_kernel(own, got, last, x, gain, g, out, value, up, res, gsum, at):
    rows = g.shape[0]
    value[...] = x[0:rows, :].astype(F32)
    total_of(own, got, last, at, up)
    norm_back_into(value, gain[...], up, g, res, gsum, rows)
    out[...] = res[...].astype(BF)


def pack_kernel(enc_s, dec_s, cross_s, gains, rels, onehot, out):
    for i, (small, index) in enumerate(gains):
        line = jnp.sum(small[8 * index : 8 * index + 8, :], axis=0, keepdims=True)
        for k in range(line.shape[1] // LANES):
            out[4 * i + k : 4 * i + k + 1, :] = line[:, k * LANES : (k + 1) * LANES]
    base = 4 * len(gains)
    count, buckets = out.shape[0] - base, onehot.shape[0]
    lane = lax.broadcasted_iota(jnp.int32, (count, LANES), 1)
    line = lax.broadcasted_iota(jnp.int32, (count, LANES), 0)
    parts = []
    for spread in rels:
        rel = lax.dot_general(
            spread[...], onehot[...], (((1,), (1,)), ((), ())), precision=lax.Precision.HIGHEST, preferred_element_type=F32
        )
        parts.append(jnp.concatenate([rel, jnp.zeros((rel.shape[0], LANES - buckets), F32)], axis=1))
    left = count - sum(part.shape[0] for part in parts)
    rest = jnp.concatenate(parts + [jnp.zeros((left, LANES), F32)], axis=0)
    terms = [(enc_s, j) for j in range(4)] + [(dec_s, 0)] + [(cross_s, j) for j in range(3)]
    for k, (small, j) in enumerate(terms):
        value = jnp.sum(small[8 * j : 8 * j + 8, :])
        rest = jnp.where(jnp.logical_and(line == 0, lane == LANES // 2 + k), value, rest)
    out[base : base + count, :] = rest


def size_of(item):
    total = jnp.dtype(item.dtype).itemsize
    for n in item.shape:
        total *= n
    return total


def call(kernel, name, args, outs, scratch, specs, out_specs, flops, bytes_accessed):
    grant = 3 << 20
    for item in scratch:
        if hasattr(item, "shape") and item.memory_space == pltpu.VMEM:
            grant += size_of(item)
    for item, spec in list(zip(args, specs)) + list(zip(outs, out_specs)):
        if spec is SMALL:
            grant += size_of(item) + (32 << 10)
    spaces = {id(ANY): pltpu.HBM, id(KEPT): pltpu.VMEM}
    args = [
        pltpu.with_memory_space_constraint(a, spaces[id(s)]) if id(s) in spaces else a for a, s in zip(args, specs)
    ]
    outs = [spaces[id(s)](o.shape, o.dtype) if id(s) in spaces else o for o, s in zip(outs, out_specs)]
    return pl.pallas_call(
        kernel,
        out_shape=outs,
        in_specs=specs,
        out_specs=out_specs,
        scratch_shapes=scratch,
        name=name,
        compiler_params=pltpu.CompilerParams(vmem_limit_bytes=grant),
        cost_estimate=pl.CostEstimate(flops=int(flops), bytes_accessed=bytes_accessed, transcendentals=0),
    )(*args)


def sds(shape, dtype=BF):
    return jax.ShapeDtypeStruct(shape, dtype)


def vm(shape, dtype=BF):
    return pltpu.VMEM(shape, dtype)


def flip(value, axis, bit):
    count = lax.axis_size(axis)
    return lax.ppermute(value, axis, [(i, i ^ bit) for i in range(count)])


def swap_rows(value, beside=0):
    dp, seq = lax.axis_size("dp"), lax.axis_size("seq")
    half = seq // 2
    pairs = []
    for d in range(dp):
        for s in range(seq):
            move = (d & 1) != (s >= half)
            to, place = (d ^ 1, s ^ half) if move else (d, s)
            pairs.append((d * seq + s, to * seq + (place ^ beside)))
    return lax.ppermute(value, ("dp", "seq"), pairs)


class Tree:
    def __init__(self, keep, send, shapes, short=False):
        self.dp, self.seq = lax.axis_size("dp"), lax.axis_size("seq")
        bits = self.dp.bit_length() - 2
        rows = keep.shape[2]
        axes = [("dp", 2 << b) for b in range(bits)]
        if short:
            orders = [axes + [("seq", 1)], axes[::-1] + [("seq", 1)]]
        else:
            axes = axes + [("seq", 1)]
            turn = max(len(axes) // 3, 1)
            orders = [axes[p * turn :] + axes[: p * turn] for p in range(3)]
        self.last = [("seq", 2)]
        self.steps = len(orders[0])
        unit = 16 if rows % 16 == 0 else 8
        cuts = [rows // unit * p // len(orders) * unit for p in range(len(orders) + 1)]
        self.parts = [((a, b), order) for a, b, order in zip(cuts, cuts[1:], orders) if b > a]
        left = [("dp", 2 << b) for b in range(bits - 1, -1, -1)] + [("seq", 2), ("seq", 1)]
        self.left = [list(left) for _ in self.parts]
        self.rows, self.shapes = rows, shapes
        self.stage = 0
        self.keep = [(keep.reshape(-1, LANES), 0)]
        self.recv = [(flip(send, "dp", 1).reshape(-1, LANES), 0)]
        self.done = None

    def task(self):
        stage = self.stage
        ins = self.keep + self.recv
        if stage > self.steps:
            outs = [sds((s[0] // self.dp, s[1] // self.seq), F32) for s in self.shapes]

            def last(ins, outs, sends):
                base = 0
                for out in outs:
                    tall = out.shape[0]
                    for ch in range(out.shape[1] // LANES):
                        total = 0.0
                        for ref, at in ins:
                            total = total + ref[at + base : at + base + tall, :].astype(F32)
                        out[:, ch * LANES : (ch + 1) * LANES] = total
                        base += tall

            return ins, outs, [], last
        count = len(self.keep)
        plans, outs, sends = [], [], []
        for p, (span, order) in enumerate(self.parts):
            tall = span[1] - span[0]
            left = self.left[p]
            src, step, first = (0, self.rows, span[0]) if stage == 0 else (p, tall, 0)
            if stage < self.steps:
                lead = 1 << (len(left) - 1)
                plans.append((src, step, first, tall, len(left), left.index(order[stage]), p))
                outs.append(sds((lead * tall, LANES)))
                sends.append((order[stage], lead * tall))
            else:
                plans.append((src, step, first, tall, len(left), None, span[0]))
        if stage == self.steps:
            outs = [sds((self.rows, LANES))]
            sends = [(key, self.rows) for key in self.last]

        def body(ins, outs, sends):
            for src, step, first, tall, n, pos, slot in plans:
                (keep, at), (recv, at_recv) = ins[src], ins[count + src]
                for m in range(1 << n):
                    row = m * step + first
                    one = keep[at + row : at + row + tall, :].astype(F32)
                    two = recv[at_recv + row : at_recv + row + tall, :].astype(F32)
                    if pos is None:
                        to, base = (outs[0], 0) if m == 0 else sends[m - 1]
                        base += slot
                    else:
                        low = n - 1 - pos
                        index = ((m >> (low + 1)) << low) | (m & ((1 << low) - 1))
                        to, base = sends[slot] if (m >> low) & 1 else (outs[slot], 0)
                        base += index * tall
                    to[base : base + tall, :] = (one + two).astype(BF)

        return ins, outs, sends, body

    def accept(self, outs, recv):
        if self.stage > self.steps:
            self.done = outs
            return
        if self.stage < self.steps:
            for p, (_, order) in enumerate(self.parts):
                self.left[p].remove(order[self.stage])
        self.keep = [(out, 0) for out in outs]
        self.recv = recv
        self.stage += 1


class SmallSum:
    def __init__(self, value, gains, width, heads, buckets, tokens):
        self.value = value
        self.form = (gains, width, heads, buckets, tokens)
        self.keys = [("dp", 1 << b) for b in range(lax.axis_size("dp").bit_length() - 1)]
        self.keys += [("seq", 1 << b) for b in range(lax.axis_size("seq").bit_length() - 1)]
        self.bits = len(self.keys) - 1
        self.stage = 0
        self.recv = [(flip(value, "dp", 1), 0)]
        self.done = None

    def task(self):
        rows = self.value.shape[0]
        whole = self.stage == 0
        final = self.stage == self.bits
        gains, width, heads, buckets, tokens = self.form
        per = width // LANES
        outs = [sds((1, width), F32)] * gains + [sds((heads, buckets), F32)] * 2 + [sds((1, 8), F32)]
        keys = self.keys[self.stage + 1 : self.stage + 2]

        def body(ins, outs, sends):
            total = ins[0][0][...]
            for ref, at in ins[1:]:
                total = total + ref[at : at + rows, :].astype(F32)
                if not whole:
                    total = total + ref[at + rows : at + 2 * rows, :].astype(F32)
            if final:
                for i in range(gains):
                    for k in range(per):
                        row = i * per + k
                        outs[i][:, k * LANES : (k + 1) * LANES] = total[row : row + 1, :]
                base = gains * per
                outs[gains][...] = total[base : base + heads, 0:buckets]
                outs[gains + 1][...] = total[base + heads : base + 2 * heads, 0:buckets]
                outs[gains + 2][...] = jnp.sqrt(total[base : base + 1, LANES // 2 : LANES // 2 + 8] / tokens)
                return
            outs[0][...] = total
            high = total.astype(BF)
            low = (total - high.astype(F32)).astype(BF)
            for ref, at in sends:
                ref[at : at + rows, :] = high
                ref[at + rows : at + 2 * rows, :] = low

        outs = outs if final else [sds(self.value.shape, F32)]
        return [(self.value, 0)] + self.recv, outs, [(key, 2 * rows) for key in keys], body

    def accept(self, outs, recv):
        if self.stage == self.bits:
            self.done = outs
            return
        self.value, self.recv = outs[0], recv
        self.stage += 1


class PairSum:
    def __init__(self, one, two, at):
        self.ins = [(one, 0), (two, at)]
        self.done = None

    def task(self):
        rows, width = self.ins[0][0].shape

        def body(ins, outs, sends):
            (one, _), (two, at) = ins
            ref, base = sends[0]
            for k in range(width // LANES):
                cols = slice(k * LANES, (k + 1) * LANES)
                total = one[:, cols].astype(F32) + two[at : at + rows, cols].astype(F32)
                ref[base + k * rows : base + (k + 1) * rows, :] = total.astype(BF)

        return self.ins, [], [(("seq", 1, "rows"), rows * width // LANES)], body

    def accept(self, outs, recv):
        self.done = recv[0]


class Copy:
    recv = ()

    def __init__(self, value):
        self.value = value
        self.done = None

    def task(self):
        def body(ins, outs, sends):
            outs[0][...] = ins[0][0][...]

        return [(self.value, 0)], [sds(self.value.shape)], [], body

    def accept(self, outs, recv):
        self.done = outs[0]


def advance(name, items, hold):
    items = [item for item in items if item.done is None]
    tasks = [item.task() for item in items]
    arrays, spots = [], []
    for ins, _, _, _ in tasks:
        mine = []
        for array, at in ins:
            known = [k for k, other in enumerate(arrays) if other is array]
            if not known:
                arrays.append(array)
            mine.append((known[0] if known else len(arrays) - 1, at))
        spots.append(mine)
    kept = [out for _, outs, _, _ in tasks for out in outs]
    sizes, slots = {}, []
    for _, _, sends, _ in tasks:
        mine = []
        for key, rows in sends:
            mine.append((key, sizes.get(key, 0)))
            sizes[key] = sizes.get(key, 0) + rows
        slots.append(mine)
    keys = sorted(sizes, key=lambda key: (len(key), key[0] == "seq", key[1]))
    mails = [sds((sizes[key], LANES)) for key in keys]

    def kernel(*refs):
        inputs, outs, mail = refs[: len(arrays)], refs[len(arrays) : len(arrays) + len(kept)], refs[len(arrays) + len(kept) :]
        for (_, task_outs, _, body), mine, to in zip(tasks, spots, slots):
            body(
                [(inputs[k], at) for k, at in mine],
                outs[: len(task_outs)],
                [(mail[keys.index(key)], at) for key, at in to],
            )
            outs = outs[len(task_outs) :]

    total = sum(size_of(a) for a in arrays + kept + mails)
    count = len(kept) + len(mails)
    results = call(kernel, name, arrays, kept + mails, [], [SMALL] * len(arrays), [SMALL] * count, total // 2_000_000 * MICROSECOND, total)
    outs, mail = list(results[: len(kept)]), list(results[len(kept) :])
    hold, mail = lax.optimization_barrier((hold, mail))
    got = {key: flip(array, *key[:2]) for key, array in zip(keys, mail)}
    for item, (_, task_outs, _, _), to in zip(items, tasks, slots):
        item.accept(outs[: len(task_outs)], [(got[key], at) for key, at in to])
        outs = outs[len(task_outs) :]
    return hold


def settle(items, hold):
    waiting = []
    for item in items:
        for array, _ in item.recv:
            if not any(array is other for other in waiting):
                waiting.append(array)
    hold, arrived = lax.optimization_barrier((hold, waiting))
    for item in items:
        item.recv = [
            (next(new for old, new in zip(waiting, arrived) if old is array), at) for array, at in item.recv
        ]
    return hold


def on_device(
    encoder_input,
    decoder_input,
    output_grad,
    segment_lengths,
    bucket_table,
    enc_gain1,
    enc_qkv,
    enc_proj,
    enc_rel,
    enc_gain2,
    enc_wi,
    enc_wo,
    enc_gainf,
    dec_gain1,
    dec_qkv,
    dec_proj,
    dec_rel,
    dec_gain2,
    cross_q,
    cross_kv,
    cross_proj,
    dec_gain3,
    dec_wi,
    dec_wo,
):
    dp, seq = lax.axis_size("dp"), lax.axis_size("seq")
    _, rows, width = encoder_input.shape
    full = rows * seq
    inner = enc_proj.shape[0]
    heads = enc_rel.shape[1]
    hid = enc_wi.shape[1]
    bucket_count = enc_rel.shape[0]
    me, place = lax.axis_index("dp"), lax.axis_index("seq")
    core = me & 1
    quarter = (place & 1) + 2 * core
    first_pos = quarter * rows
    barrier = lax.optimization_barrier

    def row(vec):
        return vec.reshape(1, -1)

    lengths = jnp.where(core == place // 2, segment_lengths, flip(segment_lengths, "dp", 1))[0]
    enc_own, enc_other = swap_rows(encoder_input[0]), swap_rows(encoder_input[0], 1)

    end1 = lengths[0]
    end2 = end1 + lengths[1]
    end3 = end2 + lengths[2]
    end4 = end3 + lengths[3]
    info = jnp.stack([quarter, end1, end2, end3, end4, me, place, me]).astype(jnp.int32)
    span = full + rows
    window = lax.dynamic_slice_in_dim(jnp.pad(bucket_table, (0, 1)), full - first_pos - rows, span)
    onehot = (jnp.arange(bucket_count, dtype=jnp.int32)[:, None] == window[None, :]).astype(F32)

    def offsets_of(rel):
        return lax.dot_general(rel, onehot, (((0,), (0,)), ((), ())), precision=lax.Precision.HIGHEST)

    enc_table, dec_table = offsets_of(enc_rel), offsets_of(dec_rel)
    enc_table, dec_table, dec_from, top_from = barrier((enc_table, dec_table, decoder_input[0], output_grad[0]))
    info, enc_table, joined, dec_from = barrier((info, enc_table, jnp.concatenate([dec_from, top_from]), dec_from))
    enc_own, enc_other, info, enc_table = barrier((enc_own, enc_other, info, enc_table))
    dec_top, dec_other = swap_rows(joined), swap_rows(dec_from, 1)
    enc_blocks = [enc_own, enc_other, flip(enc_own, "dp", 1), flip(enc_other, "dp", 1)]

    exps_shape = (heads, rows, full)
    sems = pltpu.SemaphoreType.DMA
    act2, act1 = (rows, width), (rows, inner)

    attn_scratch = [
        vm((width, 3 * inner)),
        vm((inner, width)),
        vm((full, width)),
        vm(act1),
        vm(act1, F32),
        vm((2 * rows, full), F32),
        vm((LANES, full + rows), F32),
        vm((rows, full), F32),
        vm(act1),
        vm(act2, F32),
        vm(act2),
    ]
    attn_outs = [
        sds((full, width)),
        sds((full, 2 * inner)),
        sds(act1),
        sds(exps_shape),
        sds(act1, F32),
        sds(act1),
        sds(act2, F32),
        sds(act2),
    ]
    enc_a, enc_pair, enc_query, enc_exps, enc_inv, enc_mix, enc_h1, enc_b, enc_g, enc_s, enc_h2, encoded, enc_small = call(
        functools.partial(self_fwd_kernel, False, "ffn"),
        "enc_fwd",
        (info, *enc_blocks, row(enc_gain1), enc_qkv, enc_proj, enc_table, row(enc_gain2), enc_wi, enc_wo, row(enc_gainf)),
        attn_outs + [sds((rows, hid)), sds((rows, hid)), sds(act2, F32), sds(act2), sds((32, width), F32)],
        attn_scratch
        + [
            vm((width, hid)),
            vm((hid, width)),
            vm((rows, hid), F32),
            vm((rows, hid)),
            vm((rows, hid)),
            vm(act2, F32),
            sems((19,)),
        ],
        [SCALARS] + [SMALL] * 5 + [ANY, ANY, SMALL, SMALL, ANY, ANY, SMALL],
        [ANY, KEPT, ANY, KEPT] + [ANY] * 7 + [SMALL] * 2,
        0.3 * MICROSECOND,
        20_000_000,
    )
    encoded, dec_top, dec_other = barrier((encoded, dec_top, dec_other))
    dec_blocks = [dec_top, dec_other, flip(dec_top, "dp", 1), flip(dec_other, "dp", 1)]
    encoded_other = flip(encoded, "seq", 1)
    encoded_core = flip(encoded, "dp", 1)

    dec_a, dec_pair, dec_query, dec_exps, dec_inv, dec_mix, dec_h1, dec_c, cross_query, dec_small = call(
        functools.partial(self_fwd_kernel, True, "query"),
        "dec_fwd",
        (info, *dec_blocks, row(dec_gain1), dec_qkv, dec_proj, dec_table, row(dec_gain2), cross_q),
        attn_outs + [sds(act1), sds((16, width), F32)],
        attn_scratch + [vm((width, inner)), sems((19,))],
        [SCALARS] + [SMALL] * 5 + [ANY, ANY, SMALL, SMALL, ANY],
        [ANY, KEPT, ANY, KEPT] + [ANY] * 4 + [SMALL] * 2,
        11.3 * MICROSECOND,
        16_000_000,
    )

    encoded_other, cross_query = barrier((encoded_other, cross_query))
    encoded_blocks = [encoded, encoded_other, encoded_core, flip(encoded_other, "dp", 1)]

    def wide_blocks(*shapes):
        total = sum(block_rows(shape, dp, seq) for shape in shapes)
        return [sds((dp // 2, seq, total, LANES))] * 2

    ffn_shapes = ((hid, width), (width, hid), (inner, width))
    enc_all, cross_pair, cross_exps, cross_inv, cross_mix, dec_out, g_d2, keep, send, cross_small = call(
        functools.partial(cross_kernel, dp=dp, seq=seq),
        "cross_fwd",
        (info, *encoded_blocks, cross_query, dec_h1, dec_top, cross_kv, cross_proj, row(dec_gain3), dec_wi, dec_wo),
        [
            sds((full, width)),
            sds((full, 2 * inner)),
            sds(exps_shape),
            sds(act1, F32),
            sds(act1),
            sds(act2),
            sds(act2, F32),
            *wide_blocks(*ffn_shapes),
            sds((32, width), F32),
        ],
        [
            vm((full, width)),
            vm(act1),
            vm(act1, F32),
            vm((2 * rows, full), F32),
            vm((rows, full), F32),
            vm(act1),
            vm(act2, F32),
            vm(act2),
            vm(act2),
            vm((width, 2 * inner)),
            vm((inner, width)),
            vm((width, hid)),
            vm((hid, width)),
            vm((rows, hid), F32),
            vm((rows, hid)),
            vm((rows, hid)),
            vm((rows, hid)),
            vm(act2, F32),
            vm((8, width), F32),
            vm((hid, width)),
            vm((width, hid)),
            vm((inner, width)),
            sems((16,)),
        ],
        [SCALARS] + [SMALL] * 4 + [ANY] * 5 + [SMALL, ANY, ANY],
        [ANY, KEPT, KEPT, ANY, ANY] + [SMALL] * 2 + [ANY] * 2 + [SMALL],
        17 * MICROSECOND,
        30_000_000,
    )
    tree1 = Tree(keep, send, ffn_shapes)

    def back_scratch(kind):
        out = [
            vm(act1, F32),
            vm(act1),
            vm((inner, width)),
            vm(act1),
        ]
        out += [
            vm((width, 2 * inner)) if kind == "cross" else vm((width, 3 * inner)),
            vm(act1),
            vm((2 * inner, full)),
            vm((2 * rows, full), F32),
            vm((2 * rows, full)),
            vm((2 * rows, LANES), F32),
            vm((full, width), F32),
        ]
        if kind == "self":
            out += [vm((LANES, full + LANES), F32), vm((full, width))]
        return out + [sems((8,))]

    part_outs = [sds(act2, F32), sds(act2), sds((2 * rows, width))]
    pair_outs = [sds(act1), sds((full, 2 * inner))]
    ep0, ep1, ep23, cross_dq, cross_dkv = call(
        functools.partial(attn_back_kernel, kind="cross"),
        "cross_back",
        (info, g_d2, cross_inv, cross_mix, cross_proj, cross_exps, cross_pair, cross_query, cross_kv),
        part_outs + pair_outs,
        back_scratch("cross"),
        [SCALARS, SMALL] + [ANY] * 3 + [KEPT] * 2 + [ANY] * 2,
        [SMALL] * 5,
        10.2 * MICROSECOND,
        15_000_000,
    )
    enc_got = flip(ep23, "dp", 1)
    enc_pass = PairSum(ep1, enc_got, rows)
    cross_dq, cross_dkv = advance("sum_1", [enc_pass], (cross_dq, cross_dkv))

    cross_shapes = ((inner, width), (width, inner), (width, 2 * inner))
    g_d1, keep, send, gain2_small = call(
        functools.partial(cross_weights_kernel, dp=dp, seq=seq),
        "cross_weights",
        (info, cross_dq, cross_dkv, enc_all, dec_c, cross_q, dec_h1, row(dec_gain2), g_d2, dec_mix),
        [sds(act2, F32), *wide_blocks(*cross_shapes), sds((8, width), F32)],
        [
            vm((full, width)),
            vm(act2),
            vm((width, inner)),
            vm(act2, F32),
            vm(act1),
            vm(act2, F32),
            vm((8, width), F32),
            vm((inner, width)),
            vm((width, inner)),
            vm((width, 2 * inner)),
            sems((7,)),
        ],
        [SCALARS, SMALL, SMALL] + [ANY] * 4 + [SMALL, SMALL, ANY],
        [SMALL, ANY, ANY, SMALL],
        7 * MICROSECOND,
        8_000_000,
    )
    tree2 = Tree(keep, send, cross_shapes)
    enc_last, enc_last_at = enc_pass.done
    enc_last, ep0, g_d1, dec_out = advance("sum_2", [tree1], (enc_last, ep0, g_d1, dec_out))
    dec_output = swap_rows(dec_out)

    g_e1, keep, send, enc_gain_small = call(
        functools.partial(enc_ffn_back_kernel, dp=dp, seq=seq, at=enc_last_at),
        "enc_ffn_back",
        (info, ep0, enc_got, enc_last, enc_h2, row(enc_gainf), enc_h1, row(enc_gain2), enc_g, enc_s, enc_b, enc_wi, enc_wo, enc_mix),
        [sds(act2, F32), *wide_blocks(*ffn_shapes), sds((16, width), F32)],
        [
            vm(act2, F32),
            vm(act2, F32),
            vm(act2, F32),
            vm((rows, hid)),
            vm((rows, hid)),
            vm(act2),
            vm((width, hid)),
            vm((hid, width)),
            vm(act1),
            vm(act2, F32),
            vm(act2),
            vm((rows, hid), F32),
            vm((rows, hid)),
            vm(act2, F32),
            vm((8, width), F32),
            vm((hid, width)),
            vm((width, hid)),
            vm((inner, width)),
            sems((9,)),
        ],
        [SCALARS] + [SMALL] * 3 + [ANY, SMALL, ANY, SMALL] + [ANY] * 6,
        [SMALL, ANY, ANY, SMALL],
        9.9 * MICROSECOND,
        14_000_000,
    )
    tree4 = Tree(keep, send, ffn_shapes)
    g_e1 = advance("sum_3", [tree1, tree2], g_e1)

    def self_back(name, grad, inv, mix, proj, exps, pair, query, qkv, source, gain):
        return call(
            functools.partial(attn_back_kernel, kind="self"),
            name,
            (info, grad, inv, mix, proj, exps, pair, query, qkv, source, row(gain)),
            part_outs + pair_outs + [sds((heads, span), F32), sds((8, width), F32)],
            back_scratch("self"),
            [SCALARS, SMALL] + [ANY] * 3 + [KEPT] * 2 + [ANY] * 3 + [SMALL],
            [SMALL] * 7,
            11 * MICROSECOND,
            15_000_000,
        )

    def self_weights(name, dq, dkv, source, cost):
        return call(
            functools.partial(self_weights_kernel, dp=dp, seq=seq),
            name,
            (info, dq, dkv, source),
            wide_blocks((width, 3 * inner)),
            [vm((full, width)), vm((width, inner)), vm((width, 2 * inner)), sems((2,))],
            [SCALARS, SMALL, SMALL, ANY],
            [ANY] * 2,
            cost * MICROSECOND,
            800_000,
        )

    qkv_shapes = ((width, 3 * inner),)
    xp0, xp1, xp23, enc_dq, enc_dkv, enc_spread, enc_first_small = self_back(
        "enc_back", g_e1, enc_inv, enc_mix, enc_proj, enc_exps, enc_pair, enc_query, enc_qkv, enc_a, enc_gain1
    )
    enc_mine = flip(xp23, "dp", 1)
    enc_pass = PairSum(xp1, enc_mine, rows)
    enc_dq, enc_dkv, g_d1, dec_output = advance(
        "sum_4", [tree1, tree2, tree4], (enc_dq, enc_dkv, g_d1, dec_output)
    )
    dp0, dp1, dp23, dec_dq, dec_dkv, dec_spread, dec_first_small = self_back(
        "dec_back", g_d1, dec_inv, dec_mix, dec_proj, dec_exps, dec_pair, dec_query, dec_qkv, dec_a, dec_gain1
    )
    dec_mine = flip(dp23, "dp", 1)
    dec_pass = PairSum(dp1, dec_mine, rows)

    def finish(name, own, got, done, x, gain, g):
        last, at = done
        return call(
            functools.partial(finish_kernel, at=at),
            name,
            (own, got, last, x, row(gain), g),
            [sds(act2)],
            [vm(act2, F32)] * 3 + [vm((8, width), F32)],
            [SMALL] * 6,
            [SMALL],
            1.6 * MICROSECOND,
            2_000_000,
        )[0]

    gain_count = 6
    packed = call(
        lambda e, d, c, g0, g1, g2, g3, s0, s1, oh, out: pack_kernel(
            e, d, c, ((g0, 0), (g1, 1), (g1, 0), (g2, 0), (g3, 0), (c, 3)), (s0, s1), oh, out
        ),
        "pack",
        (enc_small, dec_small, cross_small, enc_first_small, enc_gain_small, dec_first_small, gain2_small, enc_spread, dec_spread, onehot),
        [sds((4 * gain_count + 3 * heads, LANES), F32)],
        [],
        [SMALL] * 10,
        [SMALL],
        1 * MICROSECOND,
        500_000,
    )[0]
    early = [tree1, tree2, tree4]
    small = SmallSum(packed, gain_count, width, heads, bucket_count, float(rows * width * dp * seq))
    out_copy = Copy(dec_output)
    tree5 = Tree(*self_weights("enc_weights", enc_dq, enc_dkv, enc_a, 0.2), qkv_shapes, True)
    dec_dq, xp0 = advance("sum_5", [enc_pass, out_copy] + early, (dec_dq, xp0))
    tree3 = Tree(*self_weights("dec_weights", dec_dq, dec_dkv, dec_a, 5), qkv_shapes, True)
    dp0, xp0 = advance("sum_6", [tree5, tree3, small, dec_pass], (dp0, xp0))
    enc_grad = finish("enc_finish", xp0, enc_mine, enc_pass.done, enc_own, enc_gain1, g_e1)
    dp0, enc_grad = advance("sum_7", [tree5, tree3, small] + early, (dp0, enc_grad))
    encoder_grad = swap_rows(enc_grad)
    dec_grad = finish("dec_finish", dp0, dec_mine, dec_pass.done, dec_top, dec_gain1, g_d1)
    dp0, dec_grad = advance("sum_8", [tree5, tree3, small] + early, (dp0, dec_grad))
    decoder_grad = swap_rows(dec_grad)
    dp0, encoder_grad = advance("sum_9", [tree5, tree3, small], (dp0, encoder_grad))
    enc_copy, dec_copy = Copy(encoder_grad), Copy(decoder_grad)
    step = 10
    while later := [item for item in early + [tree5, tree3, small, enc_copy, dec_copy] if item.done is None]:
        (dp0,) = advance(f"sum_{step}", later, (dp0,))
        step += 1

    gain_sums, (enc_rel_sum, dec_rel_sum, rms) = small.done[:gain_count], small.done[gain_count:]

    def gain_of(i):
        return gain_sums[i].reshape(-1)

    dec_wo_g, dec_wi_g, cross_proj_g = tree1.done
    dec_proj_g, cross_q_g, cross_kv_g = tree2.done
    (dec_qkv_g,) = tree3.done
    (enc_qkv_g,) = tree5.done
    enc_wo_g, enc_wi_g, enc_proj_g = tree4.done
    return (
        out_copy.done[None],
        enc_copy.done[None],
        dec_copy.done[None],
        rms.reshape(-1),
        gain_of(0),
        enc_qkv_g,
        enc_proj_g,
        enc_rel_sum.T,
        gain_of(1),
        enc_wi_g,
        enc_wo_g,
        gain_of(2),
        gain_of(3),
        dec_qkv_g,
        dec_proj_g,
        dec_rel_sum.T,
        gain_of(4),
        cross_q_g,
        cross_kv_g,
        cross_proj_g,
        gain_of(5),
        dec_wi_g,
        dec_wo_g,
    )


def solution(mesh):
    rows = P("dp", "seq", None)
    both = P("dp", "seq")
    return jax.shard_map(
        on_device,
        mesh=mesh,
        in_specs=(rows, rows, rows, P("dp", None)) + (P(),) * 20,
        out_specs=(
            (rows,) * 3
            + (P(),) * 2
            + (both,) * 2
            + (P(),) * 2
            + (both,) * 2
            + (P(),) * 2
            + (both,) * 2
            + (P(),) * 2
            + (both,) * 3
            + (P(),)
            + (both,) * 2
        ),
        check_vma=False,
    )
```

```python
import functools

import jax
import jax.numpy as jnp
from jax import lax
from jax.experimental import pallas as pl
from jax.experimental.pallas import tpu as pltpu
from jax.sharding import PartitionSpec as P

HEAD_DIM = 64
LANES = 128
BF = jnp.bfloat16
F32 = jnp.float32

eps_norm = 1e-06
negative = -1000000000.0
gelu_in = 0.7978845608028654
gelu_cube = 0.044715

MICROSECOND = 1_725_000_000
ANY = pl.BlockSpec(memory_space=pltpu.HBM)
SMALL = pl.BlockSpec(memory_space=pltpu.VMEM)
KEPT = pl.BlockSpec(memory_space=pltpu.VMEM)
SCALARS = pl.BlockSpec(memory_space=pltpu.SMEM)


def mm(left, right):
    return jnp.dot(left, right, preferred_element_type=F32)


def mm_nt(left, right):
    return lax.dot_general(left, right, (((1,), (1,)), ((), ())), preferred_element_type=F32)


def start(source, target, sem):
    copy = pltpu.make_async_copy(source, target, sem)
    copy.start()
    return copy


def rows_of(step, size):
    return pl.ds(pl.multiple_of(step * size, size), size)


def chunks(count, body, unroll=1):
    def step(i, carry):
        body(i)
        return carry

    lax.fori_loop(0, count, step, 0, unroll=unroll)


def inv_rms(values):
    return lax.rsqrt(jnp.mean(values * values, axis=-1, keepdims=True) + eps_norm)


def norm_into(source, gain, target, rows, chunk=64):
    def body(i):
        at = rows_of(i, chunk)
        v = source[at, :].astype(F32)
        target[at, :] = (v * inv_rms(v) * gain).astype(target.dtype)

    chunks(rows // chunk, body, 2)


def norm_back_into(values, gain, incoming, residual, target, grad_sum, rows, chunk=32):
    grad_sum[...] = jnp.zeros_like(grad_sum)

    def body(i):
        at = rows_of(i, chunk)
        v = values[at, :]
        dy = incoming[at, :]
        r = inv_rms(v)
        hat = v * r
        part = dy * hat
        grad_sum[...] += jnp.sum(part.reshape(chunk // 8, 8, part.shape[-1]), axis=0)
        scaled = dy * gain
        mean = jnp.mean(scaled * hat, axis=-1, keepdims=True)
        out = r * (scaled - hat * mean)
        target[at, :] = out if residual is None else residual[at, :].astype(F32) + out

    chunks(rows // chunk, body, 4)


def square_sum(values):
    rows, width = values.shape
    return jnp.sum((values * values).reshape(rows // 8, 8, width), axis=0)


def gelu_pair(u):
    sq = u * u
    t = jnp.tanh(gelu_in * u * (1.0 + gelu_cube * sq))
    half = 0.5 * (1.0 + t)
    slope = half + 0.5 * u * (1.0 - t * t) * (gelu_in * (1.0 + 3.0 * gelu_cube * sq))
    return u * half, slope


def place_ids(info, shape, axis, base):
    place = lax.broadcasted_iota(jnp.int32, shape, axis) + base
    ids = jnp.zeros(shape, jnp.int32)
    for slot in range(1, 5):
        ids = ids + (place >= info[slot]).astype(jnp.int32)
    return place, ids


def fill_mask(info, mask, causal):
    rows, keys = mask.shape
    first = info[0] * rows
    key_place, key_ids = place_ids(info, (1, keys), 1, 0)

    def body(i):
        place, ids = place_ids(info, (32, 1), 0, first + i * 32)
        allowed = ids == key_ids
        if causal:
            allowed = jnp.logical_and(allowed, key_place <= place)
        mask[rows_of(i, 32), :] = jnp.where(allowed, 0.0, negative)

    chunks(rows // 32, body)


def lane_split(pair):
    low = lax.broadcasted_iota(jnp.int32, pair.shape, 1) < HEAD_DIM
    zero = jnp.zeros_like(pair)
    return jnp.concatenate([jnp.where(low, pair, zero), jnp.where(low, zero, pair)], axis=0)


def lane_join(first, second):
    low = lax.broadcasted_iota(jnp.int32, first.shape, 1) < HEAD_DIM
    return jnp.where(low, first, second)


def attend_fwd(q, kv, table, mask, exps, scores, toeplitz, mix, inverse):
    rows, inner = q.shape
    keys = kv.shape[0]
    half = LANES
    pairs = inner // LANES
    low = lax.broadcasted_iota(jnp.int32, (1, LANES), 1) < HEAD_DIM

    def score(pair):
        lanes = slice(pair * LANES, (pair + 1) * LANES)
        scores[pair % 2] = mm_nt(lane_split(q[:, lanes]), kv[:, lanes])

    def soften(pair):
        for side in range(2):
            head = 2 * pair + side
            if table is not None:
                width = table.shape[1]
                row = jnp.broadcast_to(table[head : head + 1, :], (half, width))
                toeplitz[side] = pltpu.roll(row, width - half + 1, 1, stride=1, stride_axis=0)
            for start_row in range(0, rows, 32):
                block, at = divmod(start_row, half)
                shift = half * (rows // half - 1 - block)
                whole = slice(side * rows + start_row, side * rows + start_row + 32)
                mine = slice(start_row, start_row + 32)
                s = scores[pair % 2, whole, :] + mask[mine, :]
                if table is not None:
                    s = s + toeplitz[side, at : at + 32, shift : shift + keys]
                exps[head, mine, :] = jnp.exp(s - jnp.max(s, axis=-1, keepdims=True)).astype(BF)

    def blend(pair):
        lanes = slice(pair * LANES, (pair + 1) * LANES)
        v_pair = kv[:, inner + pair * LANES : inner + (pair + 1) * LANES]
        one = jnp.ones_like(v_pair)
        first = mm(exps[2 * pair], jnp.where(low, v_pair, one))
        second = mm(exps[2 * pair + 1], jnp.where(low, one, v_pair))
        first_inv = 1.0 / first[:, HEAD_DIM : HEAD_DIM + 1]
        second_inv = 1.0 / second[:, 0:1]
        inv = jnp.where(low, first_inv, second_inv)
        inverse[:, lanes] = inv
        mix[:, lanes] = (lane_join(first, second) * inv).astype(BF)

    score(0)
    for pair in range(pairs):
        if pair + 1 < pairs:
            score(pair + 1)
        soften(pair)
        if pair:
            blend(pair - 1)
    blend(pairs - 1)


def attend_back(q, kv, exps, scaled, mix, dq, dkv_t, scores, dscores, delta, skew, spread):
    rows, inner = q.shape
    keys = kv.shape[0]
    half = LANES
    count = keys // LANES
    for pair in range(inner // LANES):
        lanes = slice(pair * LANES, (pair + 1) * LANES)
        later = slice(inner + pair * LANES, inner + (pair + 1) * LANES)
        do_two = lane_split(scaled[:, lanes])
        scores[...] = mm_nt(do_two, kv[:, later])
        both = do_two.astype(F32) * jnp.concatenate([mix[:, lanes], mix[:, lanes]], axis=0).astype(F32)
        delta[...] = jnp.broadcast_to(jnp.sum(both, axis=-1, keepdims=True), delta.shape)
        for side in range(2):
            head = 2 * pair + side

            def body(i, side=side, head=head):
                at = rows_of(i, 32)
                spots = [
                    (
                        pl.ds(pl.multiple_of(side * rows + block * half + i * 32, 32), 32),
                        pl.ds(pl.multiple_of(block * half + i * 32, 32), 32),
                    )
                    for block in range(2)
                ]
                shifts = [delta[whole, :] for whole, _ in spots]
                before = None
                for k in range(count + 1):
                    cols = slice(k * LANES, (k + 1) * LANES)
                    made = []
                    if k < count:
                        for (whole, mine), shift in zip(spots, shifts):
                            ds = exps[head, mine, cols].astype(F32) * (scores[whole, cols] - shift)
                            dscores[whole, cols] = ds.astype(BF)
                            made.append(ds)
                    if skew is not None:
                        terms = made[1:] + ([] if before is None else [before])
                        skew[at, cols] = terms[0] if len(terms) == 1 else terms[0] + terms[1]
                        before = made[0] if made else None

            chunks(half // 32, body, half // 32)
            if skew is not None:
                width = spread.shape[1]
                wide = skew.shape[1]
                total = jnp.zeros((8, width), F32)
                for group in range(half // 8):
                    part = jnp.concatenate(
                        [skew[8 * group : 8 * group + 8, :], jnp.zeros((8, width - wide), F32)], axis=1
                    )
                    by = half - 8 - 8 * group
                    total = total + (pltpu.roll(part, by, 1) if by else part)
                left = 7 - lax.broadcasted_iota(jnp.int32, (8, width), 0)
                for bit in (1, 2, 4):
                    total = jnp.where((left & bit) != 0, pltpu.roll(total, bit, 1), total)
                spread[head : head + 1, :] = jnp.sum(total, axis=0, keepdims=True)
        k_pair = kv[:, lanes]
        dq[:, lanes] = lane_join(mm(dscores[0:rows, :], k_pair), mm(dscores[rows:, :], k_pair)).astype(BF)
        q_two = lane_split(q[:, lanes])
        dkv_t[lanes, :] = mm(q_two.T, dscores[...]).astype(BF)
        dv = mm(do_two[0:rows].T, exps[2 * pair]) + mm(do_two[rows:].T, exps[2 * pair + 1])
        dkv_t[later, :] = dv.astype(BF)


class Blocks:
    def __init__(self, info, keep, send, dp, seq):
        self.info, self.keep, self.send, self.dp, self.seq = info, keep, send, dp, seq

    def put(self, grad, base, sem):
        rows, cols = grad.shape
        tall, wide = rows // self.dp, cols // self.seq
        me, place = self.info[5], self.info[6]

        def body(j):
            for s in range(self.seq):
                for ch in range(wide // LANES):
                    col = pl.ds(pl.multiple_of((place ^ s) * wide + ch * LANES, LANES), LANES)
                    to = pl.ds(base + ch * tall, tall)
                    for target, flip_core in ((self.keep, 0), (self.send, 1)):
                        row = pl.ds(pl.multiple_of((me ^ (2 * j) ^ flip_core) * tall, tall), tall)
                        start(grad.at[row, col], target.at[j, s, to, :], sem)

        chunks(self.dp // 2, body, self.dp // 2 if self.dp <= 8 else 1)

    def wait(self, sem):
        for target in (self.keep, self.send):
            pltpu.make_async_copy(target, target, sem).wait()


def block_rows(shape, dp, seq):
    return shape[0] * shape[1] // (dp * seq * LANES)


def put_columns(blocks, grads, base, sem):
    rows = grads[0].shape[0]
    cols = grads[0].shape[1] + grads[1].shape[1]
    tall, wide = rows // blocks.dp, cols // blocks.seq
    per = wide // LANES
    me, place = blocks.info[5], blocks.info[6]

    def body(j):
        for chunk in range(cols // LANES):
            s = (chunk // per) ^ place
            to = pl.ds(base + (chunk % per) * tall, tall)
            first = chunk * LANES
            grad, col = (grads[0], first) if first < grads[0].shape[1] else (grads[1], first - grads[0].shape[1])
            for target, flip_core in ((blocks.keep, 0), (blocks.send, 1)):
                row = pl.ds(pl.multiple_of((me ^ (2 * j) ^ flip_core) * tall, tall), tall)
                start(grad.at[row, pl.ds(col, LANES)], target.at[j, s, to, :], sem)

    chunks(blocks.dp // 2, body, blocks.dp // 2 if blocks.dp <= 8 else 1)


def total_of(own, got, last, at, target):
    rows, width = own.shape
    for k in range(width // LANES):
        cols = slice(k * LANES, (k + 1) * LANES)
        target[:, cols] = (
            own[:, cols]
            + got[0:rows, cols].astype(F32)
            + last[at + k * rows : at + (k + 1) * rows, :].astype(F32)
        )


def load_all(names, sems, base=0):
    return [start(src, dst, sems.at[base + j]) for j, (src, dst) in enumerate(names)]


def wait_all(copies):
    for copy in copies:
        copy.wait()


def self_fwd_kernel(causal, last, info, x0, x1, x2, x3, gain, w_qkv, w_proj, table, *rest):
    if last == "ffn":
        (gain2, w_in, w_out, gainf), rest = rest[:4], rest[4:]
        (a_out, kv, q_out, exps, inv_out, o_out, h1_out, b_out, g_out, s_out, h2_out, fin_out, small), rest = rest[:13], rest[13:]
        (wq, wp, a, q, inv, scores, toeplitz, mask, mix, h1, normed, wi, wo, hidden, act, slope, h2, sems) = rest
    else:
        (gain2, w_in), rest = rest[:2], rest[2:]
        (a_out, kv, q_out, exps, inv_out, o_out, h1_out, b_out, fin_out, small), rest = rest[:10], rest[10:]
        (wq, wp, a, q, inv, scores, toeplitz, mask, mix, h1, normed, wi, sems) = rest
    rows = h1.shape[0]
    inner = w_proj.shape[0]
    quarter = info[0]
    load_q = start(w_qkv, wq, sems.at[4])
    load_p = start(w_proj, wp, sems.at[5])
    load_i = start(w_in, wi, sems.at[6])
    if last == "ffn":
        load_o = start(w_out, wo, sems.at[7])
    fill_mask(info, mask, causal)
    for j, block in enumerate((x0, x1, x2, x3)):
        norm_into(block.at[0:rows], gain[...], a.at[rows_of(quarter ^ j, rows)], rows)
    saves = [start(a, a_out, sems.at[8])]
    load_q.wait()
    q[...] = mm(a[rows_of(quarter, rows), :], wq[:, 0:inner]).astype(BF)

    def project(i):
        at = rows_of(i, rows)
        kv[at, :] = mm(a[at, :], wq[:, inner:]).astype(BF)

    chunks(4, project, 4)
    saves.append(start(q, q_out, sems.at[10]))
    attend_fwd(q, kv, table, mask, exps, scores, toeplitz, mix, inv)
    saves += [start(mix, o_out, sems.at[12]), start(inv, inv_out, sems.at[18])]
    load_p.wait()
    att = mm(mix[...], wp[...])
    small[0:8, :] = square_sum(att)
    first = x0[0:rows, :].astype(F32) + att
    h1[...] = first
    small[8:16, :] = square_sum(first)
    saves.append(start(h1, h1_out, sems.at[13]))
    norm_into(h1, gain2[...], normed, rows)
    saves.append(start(normed, b_out, sems.at[14]))
    load_i.wait()
    if last == "ffn":
        hidden[...] = mm(normed[...], wi[...])
        activate(hidden, act, slope)
        saves += [start(act, g_out, sems.at[15]), start(slope, s_out, sems.at[16])]
        load_o.wait()
        ffn = mm(act[...], wo[...])
        small[16:24, :] = square_sum(ffn)
        second = h1[...] + ffn
        h2[...] = second
        small[24:32, :] = square_sum(second)
        saves.append(start(h2, h2_out, sems.at[17]))
        norm_into(h2, gainf[...], fin_out, rows)
    else:
        fin_out[...] = mm(normed[...], wi[...]).astype(BF)
    wait_all(saves)


def activate(hidden, act, slope):
    def body(i):
        at = rows_of(i, 16)
        value, rate = gelu_pair(hidden[at, :])
        act[at, :] = value.astype(BF)
        slope[at, :] = rate.astype(BF)

    chunks(hidden.shape[0] // 16, body, 16)


def ffn_back(blocks, base, top, act, slope, normed, wi, wo, hidden, du, back, grad_wo, grad_wi, sem, loads=()):
    rows = top.shape[0]
    wait_all(loads[:1])
    hidden[...] = mm_nt(top[...], wo[...])
    wait_all(loads[1:3])
    grad_wo[...] = mm(act[...].T, top[...]).astype(BF)
    blocks.put(grad_wo, base, sem)

    def slide(i):
        at = rows_of(i, 16)
        du[at, :] = (hidden[at, :] * slope[at, :].astype(F32)).astype(BF)

    chunks(rows // 16, slide, 16)
    wait_all(loads[3:])
    grad_wi[...] = mm(normed[...].T, du[...]).astype(BF)
    blocks.put(grad_wi, base + block_rows(grad_wo.shape, blocks.dp, blocks.seq), sem)
    back[...] = mm_nt(du[...], wi[...])


def cross_kernel(
    info, e0, e1, e2, e3, q_in, d1_in, top_in, w_kv, w_proj, gain, w_in, w_out,
    enc_out, kv, exps, inv_out, o_out, out_out, g2_out, keep, send, small,
    enc, q, inv, scores, mask, mix, h, top, normed, wkv, wp, wi, wo, hidden, act, slope, du, back, gsum, grad_a, grad_b, grad_p, sems,
    dp, seq,
):
    rows = h.shape[0]
    quarter = info[0]
    load_kv = start(w_kv, wkv, sems.at[4])
    load_q = start(q_in, q, sems.at[5])
    load_p = start(w_proj, wp, sems.at[6])
    load_d = start(d1_in, h, sems.at[7])
    load_i = start(w_in, wi, sems.at[8])
    load_o = start(w_out, wo, sems.at[9])
    load_t = start(top_in.at[rows : 2 * rows], top, sems.at[10])
    fill_mask(info, mask, False)
    load_kv.wait()
    for j, block in enumerate((e0, e1, e2, e3)):
        at = rows_of(quarter ^ j, rows)
        enc[at, :] = block[...]
        kv[at, :] = mm(block[...], wkv[...]).astype(BF)
    saves = [start(enc, enc_out, sems.at[11])]
    load_q.wait()
    attend_fwd(q, kv, None, mask, exps, scores, None, mix, inv)
    saves += [start(mix, o_out, sems.at[14]), start(inv, inv_out, sems.at[0])]
    load_p.wait()
    load_d.wait()
    att = mm(mix[...], wp[...])
    small[0:8, :] = square_sum(att)
    h[...] = h[...] + att
    norm_into(h, gain[...], normed, rows)
    load_i.wait()
    hidden[...] = mm(normed[...], wi[...])
    activate(hidden, act, slope)
    load_o.wait()
    ffn = mm(act[...], wo[...])
    small[8:16, :] = square_sum(ffn)
    third = h[...] + ffn
    small[16:24, :] = square_sum(third)
    out_out[...] = third.astype(BF)
    load_t.wait()
    blocks = Blocks(info, keep, send, dp, seq)
    ffn_back(blocks, 0, top, act, slope, normed, wi, wo, hidden, du, back, grad_a, grad_b, sems.at[15])
    norm_back_into(h, gain[...], back, top, g2_out, gsum, rows)
    small[24:32, :] = gsum[...]
    grad_p[...] = mm(mix[...].T, g2_out[...].astype(BF)).astype(BF)
    blocks.put(grad_p, block_rows(grad_a.shape, dp, seq) + block_rows(grad_b.shape, dp, seq), sems.at[15])
    wait_all(saves)
    blocks.wait(sems.at[15])


def enc_ffn_back_kernel(
    info, own, got, last, h2_in, gainf, h1_in, gain2, act_in, slope_in, normed_in, w_in, w_out, mix_in,
    g1_out, keep, send, small,
    up, h2, h1, act, slope, normed, wi, wo, mix, g2, top, hidden, du, back, gsum, grad_a, grad_b, grad_p, sems,
    dp, seq, at,
):
    rows = h1.shape[0]
    loads = load_all(
        ((h2_in, h2), (w_out, wo), (slope_in, slope), (act_in, act), (w_in, wi), (normed_in, normed), (h1_in, h1), (mix_in, mix)),
        sems,
    )
    total_of(own, got, last, at, up)
    loads[0].wait()
    norm_back_into(h2, gainf[...], up, None, g2, gsum, rows)
    small[0:8, :] = gsum[...]
    top[...] = g2[...].astype(BF)
    blocks = Blocks(info, keep, send, dp, seq)
    ffn_back(blocks, 0, top, act, slope, normed, wi, wo, hidden, du, back, grad_a, grad_b, sems.at[8], loads[1:6])
    wait_all(loads[6:])
    norm_back_into(h1, gain2[...], back, g2, g1_out, gsum, rows)
    small[8:16, :] = gsum[...]
    grad_p[...] = mm(mix[...].T, g1_out[...].astype(BF)).astype(BF)
    blocks.put(grad_p, block_rows(grad_a.shape, dp, seq) + block_rows(grad_b.shape, dp, seq), sems.at[8])
    blocks.wait(sems.at[8])


def attn_back_kernel(info, g_in, inv_in, o_in, w_proj, exps, kv, q_in, w_kv, *rest, kind):
    spread = skew = None
    if kind == "self":
        (a_in, gain, p0, p1, p23, dq, dkv, spread, small), rest = rest[:9], rest[9:]
        (inv, mix, wp, q, wkv, scaled, dkv_t, scores, dscores, delta, wide, skew, a, sems) = rest
    else:
        (p0, p1, p23, dq, dkv), rest = rest[:5], rest[5:]
        (inv, mix, wp, q, wkv, scaled, dkv_t, scores, dscores, delta, wide, sems) = rest
    rows = g_in.shape[0]
    inner = dq.shape[1]
    quarter = info[0]
    names = [(w_proj, wp), (inv_in, inv), (o_in, mix), (q_in, q), (w_kv, wkv)]
    if kind == "self":
        names.append((a_in, a))
    loads = load_all(names, sems)
    wait_all(loads[:2])
    scaled[...] = (mm_nt(g_in[...].astype(BF), wp[...]) * inv[...]).astype(BF)
    wait_all(loads[2:4])
    attend_back(q, kv, exps, scaled, mix, dq, dkv_t, scores, dscores, delta, skew, spread)
    dkv[...] = dkv_t[...].T
    wait_all(loads[4:])
    first = wkv.shape[1] - dkv.shape[1]

    def project(i):
        at = rows_of(i, rows)
        wide[at, :] = mm_nt(dkv[at, :], wkv[:, first:])

    chunks(4, project, 4)
    own = rows_of(quarter, rows)
    if kind == "self":
        wide[own, :] = wide[own, :] + mm_nt(dq[...], wkv[:, 0:inner])
    p1[...] = wide[rows_of(quarter ^ 1, rows), :].astype(BF)
    p23[0:rows, :] = wide[rows_of(quarter ^ 2, rows), :].astype(BF)
    p23[rows:, :] = wide[rows_of(quarter ^ 3, rows), :].astype(BF)
    p0[...] = wide[own, :]
    if kind == "self":
        small[...] = jnp.zeros_like(small)

        def gain_part(i):
            at = rows_of(i, 64)
            part = wide[at, :] * a[at, :].astype(F32)
            small[...] += jnp.sum(part.reshape(8, 8, part.shape[-1]), axis=0)

        chunks(4 * rows // 64, gain_part, 4)
        small[...] = small[...] / gain[...]


def cross_weights_kernel(
    info, dq, dkv, enc_in, c_in, w_q, d1_in, gain, g2_in, mix_in,
    g1_out, keep, send, small,
    enc, c, wq, d1, mix, part, gsum, grad_p, grad_q, grad_kv, sems,
    dp, seq,
):
    rows = d1.shape[0]
    loads = load_all(((w_q, wq), (d1_in, d1), (c_in, c), (mix_in, mix), (enc_in, enc)), sems)
    loads[0].wait()
    part[...] = mm_nt(dq[...], wq[...])
    wait_all(loads[1:])
    norm_back_into(d1, gain[...], part, g2_in, g1_out, gsum, rows)
    small[...] = gsum[...]
    blocks = Blocks(info, keep, send, dp, seq)
    grad_p[...] = mm(mix[...].T, g1_out[...].astype(BF)).astype(BF)
    blocks.put(grad_p, 0, sems.at[6])
    base = block_rows(grad_p.shape, dp, seq)
    grad_q[...] = mm(c[...].T, dq[...]).astype(BF)
    blocks.put(grad_q, base, sems.at[6])
    grad_kv[...] = mm(enc[...].T, dkv[...]).astype(BF)
    blocks.put(grad_kv, base + block_rows(grad_q.shape, dp, seq), sems.at[6])
    blocks.wait(sems.at[6])


def self_weights_kernel(info, dq, dkv, a_in, keep, send, a, grad_q, grad_kv, sems, dp, seq):
    rows = dq.shape[0]
    load_a = start(a_in, a, sems.at[0])
    load_a.wait()
    blocks = Blocks(info, keep, send, dp, seq)
    grad_q[...] = mm(a[rows_of(info[0], rows), :].T, dq[...]).astype(BF)
    grad_kv[...] = mm(a[...].T, dkv[...]).astype(BF)
    put_columns(blocks, (grad_q, grad_kv), 0, sems.at[1])
    blocks.wait(sems.at[1])


def finish_kernel(own, got, last, x, gain, g, out, value, up, res, gsum, at):
    rows = g.shape[0]
    value[...] = x[0:rows, :].astype(F32)
    total_of(own, got, last, at, up)
    norm_back_into(value, gain[...], up, g, res, gsum, rows)
    out[...] = res[...].astype(BF)


def pack_kernel(enc_s, dec_s, cross_s, gains, rels, onehot, out):
    for i, (small, index) in enumerate(gains):
        line = jnp.sum(small[8 * index : 8 * index + 8, :], axis=0, keepdims=True)
        for k in range(line.shape[1] // LANES):
            out[4 * i + k : 4 * i + k + 1, :] = line[:, k * LANES : (k + 1) * LANES]
    base = 4 * len(gains)
    count, buckets = out.shape[0] - base, onehot.shape[0]
    lane = lax.broadcasted_iota(jnp.int32, (count, LANES), 1)
    line = lax.broadcasted_iota(jnp.int32, (count, LANES), 0)
    parts = []
    for spread in rels:
        rel = lax.dot_general(
            spread[...], onehot[...], (((1,), (1,)), ((), ())), precision=lax.Precision.HIGHEST, preferred_element_type=F32
        )
        parts.append(jnp.concatenate([rel, jnp.zeros((rel.shape[0], LANES - buckets), F32)], axis=1))
    left = count - sum(part.shape[0] for part in parts)
    rest = jnp.concatenate(parts + [jnp.zeros((left, LANES), F32)], axis=0)
    terms = [(enc_s, j) for j in range(4)] + [(dec_s, 0)] + [(cross_s, j) for j in range(3)]
    for k, (small, j) in enumerate(terms):
        value = jnp.sum(small[8 * j : 8 * j + 8, :])
        rest = jnp.where(jnp.logical_and(line == 0, lane == LANES // 2 + k), value, rest)
    out[base : base + count, :] = rest


def size_of(item):
    total = jnp.dtype(item.dtype).itemsize
    for n in item.shape:
        total *= n
    return total


def call(kernel, name, args, outs, scratch, specs, out_specs, flops, bytes_accessed):
    grant = 3 << 20
    for item in scratch:
        if hasattr(item, "shape") and item.memory_space == pltpu.VMEM:
            grant += size_of(item)
    for item, spec in list(zip(args, specs)) + list(zip(outs, out_specs)):
        if spec is SMALL:
            grant += size_of(item) + (32 << 10)
    spaces = {id(ANY): pltpu.HBM, id(KEPT): pltpu.VMEM}
    args = [
        pltpu.with_memory_space_constraint(a, spaces[id(s)]) if id(s) in spaces else a for a, s in zip(args, specs)
    ]
    outs = [spaces[id(s)](o.shape, o.dtype) if id(s) in spaces else o for o, s in zip(outs, out_specs)]
    return pl.pallas_call(
        kernel,
        out_shape=outs,
        in_specs=specs,
        out_specs=out_specs,
        scratch_shapes=scratch,
        name=name,
        compiler_params=pltpu.CompilerParams(vmem_limit_bytes=grant),
        cost_estimate=pl.CostEstimate(flops=int(flops), bytes_accessed=bytes_accessed, transcendentals=0),
    )(*args)


def sds(shape, dtype=BF):
    return jax.ShapeDtypeStruct(shape, dtype)


def vm(shape, dtype=BF):
    return pltpu.VMEM(shape, dtype)


def flip(value, axis, bit):
    count = lax.axis_size(axis)
    return lax.ppermute(value, axis, [(i, i ^ bit) for i in range(count)])


def swap_rows(value, beside=0):
    dp, seq = lax.axis_size("dp"), lax.axis_size("seq")
    half = seq // 2
    pairs = []
    for d in range(dp):
        for s in range(seq):
            move = (d & 1) != (s >= half)
            to, place = (d ^ 1, s ^ half) if move else (d, s)
            pairs.append((d * seq + s, to * seq + (place ^ beside)))
    return lax.ppermute(value, ("dp", "seq"), pairs)


class Tree:
    def __init__(self, keep, send, shapes, short=False):
        self.dp, self.seq = lax.axis_size("dp"), lax.axis_size("seq")
        bits = self.dp.bit_length() - 2
        rows = keep.shape[2]
        axes = [("dp", 2 << b) for b in range(bits)]
        if short:
            orders = [axes + [("seq", 1)], axes[::-1] + [("seq", 1)]]
        else:
            axes = axes + [("seq", 1)]
            turn = max(len(axes) // 3, 1)
            orders = [axes[p * turn :] + axes[: p * turn] for p in range(3)]
        self.last = [("seq", 2)]
        self.steps = len(orders[0])
        unit = 16 if rows % 16 == 0 else 8
        cuts = [rows // unit * p // len(orders) * unit for p in range(len(orders) + 1)]
        self.parts = [((a, b), order) for a, b, order in zip(cuts, cuts[1:], orders) if b > a]
        left = [("dp", 2 << b) for b in range(bits - 1, -1, -1)] + [("seq", 2), ("seq", 1)]
        self.left = [list(left) for _ in self.parts]
        self.rows, self.shapes = rows, shapes
        self.stage = 0
        self.keep = [(keep.reshape(-1, LANES), 0)]
        self.recv = [(flip(send, "dp", 1).reshape(-1, LANES), 0)]
        self.done = None

    def task(self):
        stage = self.stage
        ins = self.keep + self.recv
        if stage > self.steps:
            outs = [sds((s[0] // self.dp, s[1] // self.seq), F32) for s in self.shapes]

            def last(ins, outs, sends):
                base = 0
                for out in outs:
                    tall = out.shape[0]
                    for ch in range(out.shape[1] // LANES):
                        total = 0.0
                        for ref, at in ins:
                            total = total + ref[at + base : at + base + tall, :].astype(F32)
                        out[:, ch * LANES : (ch + 1) * LANES] = total
                        base += tall

            return ins, outs, [], last
        count = len(self.keep)
        plans, outs, sends = [], [], []
        for p, (span, order) in enumerate(self.parts):
            tall = span[1] - span[0]
            left = self.left[p]
            src, step, first = (0, self.rows, span[0]) if stage == 0 else (p, tall, 0)
            if stage < self.steps:
                lead = 1 << (len(left) - 1)
                plans.append((src, step, first, tall, len(left), left.index(order[stage]), p))
                outs.append(sds((lead * tall, LANES)))
                sends.append((order[stage], lead * tall))
            else:
                plans.append((src, step, first, tall, len(left), None, span[0]))
        if stage == self.steps:
            outs = [sds((self.rows, LANES))]
            sends = [(key, self.rows) for key in self.last]

        def body(ins, outs, sends):
            for src, step, first, tall, n, pos, slot in plans:
                (keep, at), (recv, at_recv) = ins[src], ins[count + src]
                for m in range(1 << n):
                    row = m * step + first
                    one = keep[at + row : at + row + tall, :].astype(F32)
                    two = recv[at_recv + row : at_recv + row + tall, :].astype(F32)
                    if pos is None:
                        to, base = (outs[0], 0) if m == 0 else sends[m - 1]
                        base += slot
                    else:
                        low = n - 1 - pos
                        index = ((m >> (low + 1)) << low) | (m & ((1 << low) - 1))
                        to, base = sends[slot] if (m >> low) & 1 else (outs[slot], 0)
                        base += index * tall
                    to[base : base + tall, :] = (one + two).astype(BF)

        return ins, outs, sends, body

    def accept(self, outs, recv):
        if self.stage > self.steps:
            self.done = outs
            return
        if self.stage < self.steps:
            for p, (_, order) in enumerate(self.parts):
                self.left[p].remove(order[self.stage])
        self.keep = [(out, 0) for out in outs]
        self.recv = recv
        self.stage += 1


class SmallSum:
    def __init__(self, value, gains, width, heads, buckets, tokens):
        self.value = value
        self.form = (gains, width, heads, buckets, tokens)
        self.keys = [("dp", 1 << b) for b in range(lax.axis_size("dp").bit_length() - 1)]
        self.keys += [("seq", 1 << b) for b in range(lax.axis_size("seq").bit_length() - 1)]
        self.bits = len(self.keys) - 1
        self.stage = 0
        self.recv = [(flip(value, "dp", 1), 0)]
        self.done = None

    def task(self):
        rows = self.value.shape[0]
        whole = self.stage == 0
        final = self.stage == self.bits
        gains, width, heads, buckets, tokens = self.form
        per = width // LANES
        outs = [sds((1, width), F32)] * gains + [sds((heads, buckets), F32)] * 2 + [sds((1, 8), F32)]
        keys = self.keys[self.stage + 1 : self.stage + 2]

        def body(ins, outs, sends):
            total = ins[0][0][...]
            for ref, at in ins[1:]:
                total = total + ref[at : at + rows, :].astype(F32)
                if not whole:
                    total = total + ref[at + rows : at + 2 * rows, :].astype(F32)
            if final:
                for i in range(gains):
                    for k in range(per):
                        row = i * per + k
                        outs[i][:, k * LANES : (k + 1) * LANES] = total[row : row + 1, :]
                base = gains * per
                outs[gains][...] = total[base : base + heads, 0:buckets]
                outs[gains + 1][...] = total[base + heads : base + 2 * heads, 0:buckets]
                outs[gains + 2][...] = jnp.sqrt(total[base : base + 1, LANES // 2 : LANES // 2 + 8] / tokens)
                return
            outs[0][...] = total
            high = total.astype(BF)
            low = (total - high.astype(F32)).astype(BF)
            for ref, at in sends:
                ref[at : at + rows, :] = high
                ref[at + rows : at + 2 * rows, :] = low

        outs = outs if final else [sds(self.value.shape, F32)]
        return [(self.value, 0)] + self.recv, outs, [(key, 2 * rows) for key in keys], body

    def accept(self, outs, recv):
        if self.stage == self.bits:
            self.done = outs
            return
        self.value, self.recv = outs[0], recv
        self.stage += 1


class PairSum:
    def __init__(self, one, two, at):
        self.ins = [(one, 0), (two, at)]
        self.done = None

    def task(self):
        rows, width = self.ins[0][0].shape

        def body(ins, outs, sends):
            (one, _), (two, at) = ins
            ref, base = sends[0]
            for k in range(width // LANES):
                cols = slice(k * LANES, (k + 1) * LANES)
                total = one[:, cols].astype(F32) + two[at : at + rows, cols].astype(F32)
                ref[base + k * rows : base + (k + 1) * rows, :] = total.astype(BF)

        return self.ins, [], [(("seq", 1, "rows"), rows * width // LANES)], body

    def accept(self, outs, recv):
        self.done = recv[0]


class Copy:
    recv = ()

    def __init__(self, value):
        self.value = value
        self.done = None

    def task(self):
        def body(ins, outs, sends):
            outs[0][...] = ins[0][0][...]

        return [(self.value, 0)], [sds(self.value.shape)], [], body

    def accept(self, outs, recv):
        self.done = outs[0]


def advance(name, items, hold):
    items = [item for item in items if item.done is None]
    tasks = [item.task() for item in items]
    arrays, spots = [], []
    for ins, _, _, _ in tasks:
        mine = []
        for array, at in ins:
            known = [k for k, other in enumerate(arrays) if other is array]
            if not known:
                arrays.append(array)
            mine.append((known[0] if known else len(arrays) - 1, at))
        spots.append(mine)
    kept = [out for _, outs, _, _ in tasks for out in outs]
    sizes, slots = {}, []
    for _, _, sends, _ in tasks:
        mine = []
        for key, rows in sends:
            mine.append((key, sizes.get(key, 0)))
            sizes[key] = sizes.get(key, 0) + rows
        slots.append(mine)
    keys = sorted(sizes, key=lambda key: (len(key), key[0] == "seq", key[1]))
    mails = [sds((sizes[key], LANES)) for key in keys]

    def kernel(*refs):
        inputs, outs, mail = refs[: len(arrays)], refs[len(arrays) : len(arrays) + len(kept)], refs[len(arrays) + len(kept) :]
        for (_, task_outs, _, body), mine, to in zip(tasks, spots, slots):
            body(
                [(inputs[k], at) for k, at in mine],
                outs[: len(task_outs)],
                [(mail[keys.index(key)], at) for key, at in to],
            )
            outs = outs[len(task_outs) :]

    total = sum(size_of(a) for a in arrays + kept + mails)
    count = len(kept) + len(mails)
    results = call(kernel, name, arrays, kept + mails, [], [SMALL] * len(arrays), [SMALL] * count, total // 2_000_000 * MICROSECOND, total)
    outs, mail = list(results[: len(kept)]), list(results[len(kept) :])
    hold, mail = lax.optimization_barrier((hold, mail))
    got = {key: flip(array, *key[:2]) for key, array in zip(keys, mail)}
    for item, (_, task_outs, _, _), to in zip(items, tasks, slots):
        item.accept(outs[: len(task_outs)], [(got[key], at) for key, at in to])
        outs = outs[len(task_outs) :]
    return hold


def settle(items, hold):
    waiting = []
    for item in items:
        for array, _ in item.recv:
            if not any(array is other for other in waiting):
                waiting.append(array)
    hold, arrived = lax.optimization_barrier((hold, waiting))
    for item in items:
        item.recv = [
            (next(new for old, new in zip(waiting, arrived) if old is array), at) for array, at in item.recv
        ]
    return hold


def on_device(
    encoder_input,
    decoder_input,
    output_grad,
    segment_lengths,
    bucket_table,
    enc_gain1,
    enc_qkv,
    enc_proj,
    enc_rel,
    enc_gain2,
    enc_wi,
    enc_wo,
    enc_gainf,
    dec_gain1,
    dec_qkv,
    dec_proj,
    dec_rel,
    dec_gain2,
    cross_q,
    cross_kv,
    cross_proj,
    dec_gain3,
    dec_wi,
    dec_wo,
):
    dp, seq = lax.axis_size("dp"), lax.axis_size("seq")
    _, rows, width = encoder_input.shape
    full = rows * seq
    inner = enc_proj.shape[0]
    heads = enc_rel.shape[1]
    hid = enc_wi.shape[1]
    bucket_count = enc_rel.shape[0]
    me, place = lax.axis_index("dp"), lax.axis_index("seq")
    core = me & 1
    quarter = (place & 1) + 2 * core
    first_pos = quarter * rows
    barrier = lax.optimization_barrier

    def row(vec):
        return vec.reshape(1, -1)

    lengths = jnp.where(core == place // 2, segment_lengths, flip(segment_lengths, "dp", 1))[0]
    enc_own, enc_other = swap_rows(encoder_input[0]), swap_rows(encoder_input[0], 1)

    end1 = lengths[0]
    end2 = end1 + lengths[1]
    end3 = end2 + lengths[2]
    end4 = end3 + lengths[3]
    info = jnp.stack([quarter, end1, end2, end3, end4, me, place, me]).astype(jnp.int32)
    span = full + rows
    window = lax.dynamic_slice_in_dim(jnp.pad(bucket_table, (0, 1)), full - first_pos - rows, span)
    onehot = (jnp.arange(bucket_count, dtype=jnp.int32)[:, None] == window[None, :]).astype(F32)

    def offsets_of(rel):
        return lax.dot_general(rel, onehot, (((0,), (0,)), ((), ())), precision=lax.Precision.HIGHEST)

    enc_table, dec_table = offsets_of(enc_rel), offsets_of(dec_rel)
    enc_table, dec_table, dec_from, top_from = barrier((enc_table, dec_table, decoder_input[0], output_grad[0]))
    info, enc_table, joined, dec_from = barrier((info, enc_table, jnp.concatenate([dec_from, top_from]), dec_from))
    enc_own, enc_other, info, enc_table = barrier((enc_own, enc_other, info, enc_table))
    dec_top, dec_other = swap_rows(joined), swap_rows(dec_from, 1)
    enc_blocks = [enc_own, enc_other, flip(enc_own, "dp", 1), flip(enc_other, "dp", 1)]

    exps_shape = (heads, rows, full)
    sems = pltpu.SemaphoreType.DMA
    act2, act1 = (rows, width), (rows, inner)

    attn_scratch = [
        vm((width, 3 * inner)),
        vm((inner, width)),
        vm((full, width)),
        vm(act1),
        vm(act1, F32),
        vm((2, 2 * rows, full), F32),
        vm((2, LANES, full + rows), F32),
        vm((rows, full), F32),
        vm(act1),
        vm(act2, F32),
        vm(act2),
    ]
    attn_outs = [
        sds((full, width)),
        sds((full, 2 * inner)),
        sds(act1),
        sds(exps_shape),
        sds(act1, F32),
        sds(act1),
        sds(act2, F32),
        sds(act2),
    ]
    enc_a, enc_pair, enc_query, enc_exps, enc_inv, enc_mix, enc_h1, enc_b, enc_g, enc_s, enc_h2, encoded, enc_small = call(
        functools.partial(self_fwd_kernel, False, "ffn"),
        "enc_fwd",
        (info, *enc_blocks, row(enc_gain1), enc_qkv, enc_proj, enc_table, row(enc_gain2), enc_wi, enc_wo, row(enc_gainf)),
        attn_outs + [sds((rows, hid)), sds((rows, hid)), sds(act2, F32), sds(act2), sds((32, width), F32)],
        attn_scratch
        + [
            vm((width, hid)),
            vm((hid, width)),
            vm((rows, hid), F32),
            vm((rows, hid)),
            vm((rows, hid)),
            vm(act2, F32),
            sems((19,)),
        ],
        [SCALARS] + [SMALL] * 5 + [ANY, ANY, SMALL, SMALL, ANY, ANY, SMALL],
        [ANY, KEPT, ANY, KEPT] + [ANY] * 7 + [SMALL] * 2,
        0.3 * MICROSECOND,
        20_000_000,
    )
    encoded, dec_top, dec_other = barrier((encoded, dec_top, dec_other))
    dec_blocks = [dec_top, dec_other, flip(dec_top, "dp", 1), flip(dec_other, "dp", 1)]
    encoded_other = flip(encoded, "seq", 1)
    encoded_core = flip(encoded, "dp", 1)

    dec_a, dec_pair, dec_query, dec_exps, dec_inv, dec_mix, dec_h1, dec_c, cross_query, dec_small = call(
        functools.partial(self_fwd_kernel, True, "query"),
        "dec_fwd",
        (info, *dec_blocks, row(dec_gain1), dec_qkv, dec_proj, dec_table, row(dec_gain2), cross_q),
        attn_outs + [sds(act1), sds((16, width), F32)],
        attn_scratch + [vm((width, inner)), sems((19,))],
        [SCALARS] + [SMALL] * 5 + [ANY, ANY, SMALL, SMALL, ANY],
        [ANY, KEPT, ANY, KEPT] + [ANY] * 4 + [SMALL] * 2,
        11.3 * MICROSECOND,
        16_000_000,
    )

    encoded_other, cross_query = barrier((encoded_other, cross_query))
    encoded_blocks = [encoded, encoded_other, encoded_core, flip(encoded_other, "dp", 1)]

    def wide_blocks(*shapes):
        total = sum(block_rows(shape, dp, seq) for shape in shapes)
        return [sds((dp // 2, seq, total, LANES))] * 2

    ffn_shapes = ((hid, width), (width, hid), (inner, width))
    enc_all, cross_pair, cross_exps, cross_inv, cross_mix, dec_out, g_d2, keep, send, cross_small = call(
        functools.partial(cross_kernel, dp=dp, seq=seq),
        "cross_fwd",
        (info, *encoded_blocks, cross_query, dec_h1, dec_top, cross_kv, cross_proj, row(dec_gain3), dec_wi, dec_wo),
        [
            sds((full, width)),
            sds((full, 2 * inner)),
            sds(exps_shape),
            sds(act1, F32),
            sds(act1),
            sds(act2),
            sds(act2, F32),
            *wide_blocks(*ffn_shapes),
            sds((32, width), F32),
        ],
        [
            vm((full, width)),
            vm(act1),
            vm(act1, F32),
            vm((2, 2 * rows, full), F32),
            vm((rows, full), F32),
            vm(act1),
            vm(act2, F32),
            vm(act2),
            vm(act2),
            vm((width, 2 * inner)),
            vm((inner, width)),
            vm((width, hid)),
            vm((hid, width)),
            vm((rows, hid), F32),
            vm((rows, hid)),
            vm((rows, hid)),
            vm((rows, hid)),
            vm(act2, F32),
            vm((8, width), F32),
            vm((hid, width)),
            vm((width, hid)),
            vm((inner, width)),
            sems((16,)),
        ],
        [SCALARS] + [SMALL] * 4 + [ANY] * 5 + [SMALL, ANY, ANY],
        [ANY, KEPT, KEPT, ANY, ANY] + [SMALL] * 2 + [ANY] * 2 + [SMALL],
        17 * MICROSECOND,
        30_000_000,
    )
    tree1 = Tree(keep, send, ffn_shapes)

    def back_scratch(kind):
        out = [
            vm(act1, F32),
            vm(act1),
            vm((inner, width)),
            vm(act1),
        ]
        out += [
            vm((width, 2 * inner)) if kind == "cross" else vm((width, 3 * inner)),
            vm(act1),
            vm((2 * inner, full)),
            vm((2 * rows, full), F32),
            vm((2 * rows, full)),
            vm((2 * rows, LANES), F32),
            vm((full, width), F32),
        ]
        if kind == "self":
            out += [vm((LANES, full + LANES), F32), vm((full, width))]
        return out + [sems((8,))]

    part_outs = [sds(act2, F32), sds(act2), sds((2 * rows, width))]
    pair_outs = [sds(act1), sds((full, 2 * inner))]
    ep0, ep1, ep23, cross_dq, cross_dkv = call(
        functools.partial(attn_back_kernel, kind="cross"),
        "cross_back",
        (info, g_d2, cross_inv, cross_mix, cross_proj, cross_exps, cross_pair, cross_query, cross_kv),
        part_outs + pair_outs,
        back_scratch("cross"),
        [SCALARS, SMALL] + [ANY] * 3 + [KEPT] * 2 + [ANY] * 2,
        [SMALL] * 5,
        10.2 * MICROSECOND,
        15_000_000,
    )
    enc_got = flip(ep23, "dp", 1)
    enc_pass = PairSum(ep1, enc_got, rows)
    cross_dq, cross_dkv = advance("sum_1", [enc_pass], (cross_dq, cross_dkv))

    cross_shapes = ((inner, width), (width, inner), (width, 2 * inner))
    g_d1, keep, send, gain2_small = call(
        functools.partial(cross_weights_kernel, dp=dp, seq=seq),
        "cross_weights",
        (info, cross_dq, cross_dkv, enc_all, dec_c, cross_q, dec_h1, row(dec_gain2), g_d2, dec_mix),
        [sds(act2, F32), *wide_blocks(*cross_shapes), sds((8, width), F32)],
        [
            vm((full, width)),
            vm(act2),
            vm((width, inner)),
            vm(act2, F32),
            vm(act1),
            vm(act2, F32),
            vm((8, width), F32),
            vm((inner, width)),
            vm((width, inner)),
            vm((width, 2 * inner)),
            sems((7,)),
        ],
        [SCALARS, SMALL, SMALL] + [ANY] * 4 + [SMALL, SMALL, ANY],
        [SMALL, ANY, ANY, SMALL],
        7 * MICROSECOND,
        8_000_000,
    )
    tree2 = Tree(keep, send, cross_shapes)
    enc_last, enc_last_at = enc_pass.done
    enc_last, ep0, g_d1, dec_out = advance("sum_2", [tree1], (enc_last, ep0, g_d1, dec_out))
    dec_output = swap_rows(dec_out)

    g_e1, keep, send, enc_gain_small = call(
        functools.partial(enc_ffn_back_kernel, dp=dp, seq=seq, at=enc_last_at),
        "enc_ffn_back",
        (info, ep0, enc_got, enc_last, enc_h2, row(enc_gainf), enc_h1, row(enc_gain2), enc_g, enc_s, enc_b, enc_wi, enc_wo, enc_mix),
        [sds(act2, F32), *wide_blocks(*ffn_shapes), sds((16, width), F32)],
        [
            vm(act2, F32),
            vm(act2, F32),
            vm(act2, F32),
            vm((rows, hid)),
            vm((rows, hid)),
            vm(act2),
            vm((width, hid)),
            vm((hid, width)),
            vm(act1),
            vm(act2, F32),
            vm(act2),
            vm((rows, hid), F32),
            vm((rows, hid)),
            vm(act2, F32),
            vm((8, width), F32),
            vm((hid, width)),
            vm((width, hid)),
            vm((inner, width)),
            sems((9,)),
        ],
        [SCALARS] + [SMALL] * 3 + [ANY, SMALL, ANY, SMALL] + [ANY] * 6,
        [SMALL, ANY, ANY, SMALL],
        9.9 * MICROSECOND,
        14_000_000,
    )
    tree4 = Tree(keep, send, ffn_shapes)
    g_e1 = advance("sum_3", [tree1, tree2], g_e1)

    def self_back(name, grad, inv, mix, proj, exps, pair, query, qkv, source, gain):
        return call(
            functools.partial(attn_back_kernel, kind="self"),
            name,
            (info, grad, inv, mix, proj, exps, pair, query, qkv, source, row(gain)),
            part_outs + pair_outs + [sds((heads, span), F32), sds((8, width), F32)],
            back_scratch("self"),
            [SCALARS, SMALL] + [ANY] * 3 + [KEPT] * 2 + [ANY] * 3 + [SMALL],
            [SMALL] * 7,
            11 * MICROSECOND,
            15_000_000,
        )

    def self_weights(name, dq, dkv, source, cost):
        return call(
            functools.partial(self_weights_kernel, dp=dp, seq=seq),
            name,
            (info, dq, dkv, source),
            wide_blocks((width, 3 * inner)),
            [vm((full, width)), vm((width, inner)), vm((width, 2 * inner)), sems((2,))],
            [SCALARS, SMALL, SMALL, ANY],
            [ANY] * 2,
            cost * MICROSECOND,
            800_000,
        )

    qkv_shapes = ((width, 3 * inner),)
    xp0, xp1, xp23, enc_dq, enc_dkv, enc_spread, enc_first_small = self_back(
        "enc_back", g_e1, enc_inv, enc_mix, enc_proj, enc_exps, enc_pair, enc_query, enc_qkv, enc_a, enc_gain1
    )
    enc_mine = flip(xp23, "dp", 1)
    enc_pass = PairSum(xp1, enc_mine, rows)
    enc_dq, enc_dkv, g_d1, dec_output = advance(
        "sum_4", [tree1, tree2, tree4], (enc_dq, enc_dkv, g_d1, dec_output)
    )
    dp0, dp1, dp23, dec_dq, dec_dkv, dec_spread, dec_first_small = self_back(
        "dec_back", g_d1, dec_inv, dec_mix, dec_proj, dec_exps, dec_pair, dec_query, dec_qkv, dec_a, dec_gain1
    )
    dec_mine = flip(dp23, "dp", 1)
    dec_pass = PairSum(dp1, dec_mine, rows)

    def finish(name, own, got, done, x, gain, g):
        last, at = done
        return call(
            functools.partial(finish_kernel, at=at),
            name,
            (own, got, last, x, row(gain), g),
            [sds(act2)],
            [vm(act2, F32)] * 3 + [vm((8, width), F32)],
            [SMALL] * 6,
            [SMALL],
            1.6 * MICROSECOND,
            2_000_000,
        )[0]

    gain_count = 6
    packed = call(
        lambda e, d, c, g0, g1, g2, g3, s0, s1, oh, out: pack_kernel(
            e, d, c, ((g0, 0), (g1, 1), (g1, 0), (g2, 0), (g3, 0), (c, 3)), (s0, s1), oh, out
        ),
        "pack",
        (enc_small, dec_small, cross_small, enc_first_small, enc_gain_small, dec_first_small, gain2_small, enc_spread, dec_spread, onehot),
        [sds((4 * gain_count + 3 * heads, LANES), F32)],
        [],
        [SMALL] * 10,
        [SMALL],
        1 * MICROSECOND,
        500_000,
    )[0]
    early = [tree1, tree2, tree4]
    small = SmallSum(packed, gain_count, width, heads, bucket_count, float(rows * width * dp * seq))
    out_copy = Copy(dec_output)
    tree5 = Tree(*self_weights("enc_weights", enc_dq, enc_dkv, enc_a, 0.2), qkv_shapes, True)
    dec_dq, xp0 = advance("sum_5", [enc_pass, out_copy] + early, (dec_dq, xp0))
    tree3 = Tree(*self_weights("dec_weights", dec_dq, dec_dkv, dec_a, 5), qkv_shapes, True)
    dp0, xp0 = advance("sum_6", [tree5, tree3, small, dec_pass], (dp0, xp0))
    enc_grad = finish("enc_finish", xp0, enc_mine, enc_pass.done, enc_own, enc_gain1, g_e1)
    dp0, enc_grad = advance("sum_7", [tree5, tree3, small] + early, (dp0, enc_grad))
    encoder_grad = swap_rows(enc_grad)
    dec_grad = finish("dec_finish", dp0, dec_mine, dec_pass.done, dec_top, dec_gain1, g_d1)
    dp0, dec_grad = advance("sum_8", [tree5, tree3, small] + early, (dp0, dec_grad))
    decoder_grad = swap_rows(dec_grad)
    dp0, encoder_grad = advance("sum_9", [tree5, tree3, small], (dp0, encoder_grad))
    enc_copy, dec_copy = Copy(encoder_grad), Copy(decoder_grad)
    step = 10
    while later := [item for item in early + [tree5, tree3, small, enc_copy, dec_copy] if item.done is None]:
        (dp0,) = advance(f"sum_{step}", later, (dp0,))
        step += 1

    gain_sums, (enc_rel_sum, dec_rel_sum, rms) = small.done[:gain_count], small.done[gain_count:]

    def gain_of(i):
        return gain_sums[i].reshape(-1)

    dec_wo_g, dec_wi_g, cross_proj_g = tree1.done
    dec_proj_g, cross_q_g, cross_kv_g = tree2.done
    (dec_qkv_g,) = tree3.done
    (enc_qkv_g,) = tree5.done
    enc_wo_g, enc_wi_g, enc_proj_g = tree4.done
    return (
        out_copy.done[None],
        enc_copy.done[None],
        dec_copy.done[None],
        rms.reshape(-1),
        gain_of(0),
        enc_qkv_g,
        enc_proj_g,
        enc_rel_sum.T,
        gain_of(1),
        enc_wi_g,
        enc_wo_g,
        gain_of(2),
        gain_of(3),
        dec_qkv_g,
        dec_proj_g,
        dec_rel_sum.T,
        gain_of(4),
        cross_q_g,
        cross_kv_g,
        cross_proj_g,
        gain_of(5),
        dec_wi_g,
        dec_wo_g,
    )


def solution(mesh):
    rows = P("dp", "seq", None)
    both = P("dp", "seq")
    return jax.shard_map(
        on_device,
        mesh=mesh,
        in_specs=(rows, rows, rows, P("dp", None)) + (P(),) * 20,
        out_specs=(
            (rows,) * 3
            + (P(),) * 2
            + (both,) * 2
            + (P(),) * 2
            + (both,) * 2
            + (P(),) * 2
            + (both,) * 2
            + (P(),) * 2
            + (both,) * 3
            + (P(),)
            + (both,) * 2
        ),
        check_vma=False,
    )
```
